512 devices in a mesh: dp: 16 (over y_lo, x), tile: 32 (over y_hi, z, core).
Axes of the slice: x: 4, y: 8 (y_hi: 2, y_lo: 4; y = y_hi * 4 + y_lo), z: 8, core: 2. Of those that a mesh axis runs over, the one named last changes fastest.
Arguments:
- features: bfloat16 [16, 32, 8, 16, 1024], P('dp', 'tile'), may hold values from -6 to 6
- cotangent: bfloat16 [16, 32, 8, 16, 1024], P('dp', 'tile'), may hold values from -6 to 6
- in_weight: bfloat16 [3072, 1024], P(('dp', 'tile')), may hold values from -0.1875 to 0.1875
- out_weight: bfloat16 [3072, 1024], P(('dp', 'tile')), may hold values from -0.109375 to 0.109375
- hidden_bias: bfloat16 [3072], P(('dp', 'tile')), may hold values from -3 to 3
- kernel: float32 [49, 1024], P(None, 'dp'), may hold values from -0.875 to 0.875
- conv_bias: float32 [1024], P('dp'), may hold values from -3 to 3
- norm_gain: float32 [1024], P('dp'), may hold values from 0.5 to 1.5
- norm_bias: float32 [1024], P('dp'), may hold values from -3 to 3
- layer_scale: float32 [1024], P('dp'), may hold values from 0.5 to 1.5
- out_bias: float32 [1024], P('dp'), may hold values from -3 to 3
Outputs:
- block_out: bfloat16 [16, 32, 8, 16, 1024], P('dp', 'tile')
- grad_input: bfloat16 [16, 32, 8, 16, 1024], P('dp', 'tile')
- grad_kernel: float32 [49, 1024], P(None, 'dp')
- grad_conv_bias: float32 [1024], P('dp')
- grad_norm_gain: float32 [1024], P('dp')
- grad_norm_bias: float32 [1024], P('dp')
- grad_layer_scale: float32 [1024], P('dp')
The draws below stay inside these ranges and needn't reach their ends.
All inputs are finite; a program needn't handle non-finite values.
Results may differ from the reference program's by a relative error of at most 0.0061.
Values may be sent and summed in bfloat16 or wider, within the bound.
A program may use at most 128 MiB of HBM per device.

```python
import math
import jax
import jax.numpy as jnp
from jax import lax

D = 1024
FF = 3072
KS = 7
GX = 4
TH = 8
TW = 16
KK = 49
IMAGES = 16
TILES = 32
PIXELS = 65536


def raised(entries, rng, source, target, blocks, factor):
    owner, partner = [(jnp.arange(entries.shape[dim]) // (entries.shape[dim] // blocks)).reshape([-1 if axis == dim else 1 for axis in range(entries.ndim)]) for dim in (source, target)]
    chosen = jax.random.permutation(rng, blocks)[partner]
    strong = (owner == chosen) | (owner == (partner + blocks // 2) % blocks)
    return jnp.where(strong, factor * entries, entries)


def block_scale(stream_key, dims, cuts, low, top_value):
    def one(position, parts):
        steps = jax.random.uniform(jax.random.fold_in(jax.random.fold_in(stream_key, 6), position), (parts,), jnp.float32, low / len(cuts), top_value / len(cuts))
        return jnp.repeat(jnp.exp(steps), dims[position] // parts).reshape((-1,) + (1,) * (len(dims) - position - 1))

    loudness = one(*cuts[0])
    for cut in cuts[1:]:
        loudness = loudness * one(*cut)
    return loudness


def noise(stream_key, extent, deviation, limit, pieces=(), kind=jnp.bfloat16):
    entries = deviation * jax.random.normal(stream_key, extent, jnp.float32)
    if pieces:
        entries = entries * block_scale(stream_key, extent, pieces, -0.22, 0.18)
    return jnp.clip(entries, -limit, limit).astype(kind)


def noise_with(key, shape, deviation, bound, cuts, heavy, dtype=jnp.bfloat16):
    entries = deviation * jax.random.normal(key, shape, jnp.float32)
    if cuts:
        entries = entries * block_scale(key, shape, cuts, -0.22, 0.18)
    return jnp.clip(raised(entries, jax.random.fold_in(key, 3), *heavy), -bound, bound).astype(dtype)


def setup_inputs(seed: int = 0) -> dict:
    seeds = jax.random.split(jax.random.key(seed), 12)
    return {
        "features": noise(seeds[0], (IMAGES, TILES, TH, TW, D), 1.0, 6.0, ((0, 16), (1, 32))),
        "cotangent": noise_with(seeds[1], (IMAGES, TILES, TH, TW, D), 1.0, 6.0, ((0, 16), (1, 32)), (1, 4, 32, 2.75)),
        "in_weight": noise(seeds[2], (FF, D), D ** -0.5, 0.1875, ((0, 512),)),
        "out_weight": noise(seeds[3], (FF, D), FF ** -0.5, 0.109375, ((0, 512),)),
        "hidden_bias": noise(seeds[4], (FF,), 0.5, 3.0, ((0, 512),)),
        "kernel": noise(seeds[5], (KK, D), KK ** -0.5, 0.875, ((1, 16),), jnp.float32),
        "conv_bias": noise(seeds[6], (D,), 0.5, 3.0, ((0, 16),), jnp.float32),
        "norm_gain": jnp.clip(0.5 + 1.0 * jax.random.uniform(seeds[7], (D,), jnp.float32) ** block_scale(seeds[7], (D,), ((0, 16),), -0.2, 0.2), 0.5, 1.5),
        "norm_bias": noise(seeds[8], (D,), 0.5, 3.0, ((0, 16),), jnp.float32),
        "layer_scale": jnp.clip(0.5 + 1.0 * jax.random.uniform(seeds[9], (D,), jnp.float32) ** block_scale(seeds[9], (D,), ((0, 16),), -0.2, 0.2), 0.5, 1.5),
        "out_bias": noise(seeds[10], (D,), 0.5, 3.0, ((0, 16),), jnp.float32),
    }


def gelu_exact(values):
    return 0.5 * values * (1.0 + jax.scipy.special.erf(values * 0.7071067811865476))

def gelu_slope(values):
    return 0.5 * (1.0 + jax.scipy.special.erf(values * 0.7071067811865476)) + values * jnp.exp(-0.5 * values * values) * 0.3989422804014327

def reference(features, cotangent, in_weight, out_weight, hidden_bias, kernel, conv_bias, norm_gain, norm_bias, layer_scale, out_bias):
    grid_rows = TILES // GX
    margin = KS // 2
    height = grid_rows * TH
    breadth = GX * TW

    def to_image(tiled):
        shaped = tiled.reshape(IMAGES, grid_rows, GX, TH, TW, D)
        return shaped.transpose(0, 1, 3, 2, 4, 5).reshape(IMAGES, height, breadth, D)

    def to_tiles(whole):
        shaped = whole.reshape(IMAGES, grid_rows, TH, GX, TW, D)
        return shaped.transpose(0, 1, 3, 2, 4, 5).reshape(IMAGES, TILES, TH, TW, D)

    def one_image(pair):
        picture, upper = pair
        source = picture.astype(jnp.float32)
        padded = jnp.pad(source, ((margin, margin), (margin, margin), (0, 0)))
        convolved = jnp.zeros((height, breadth, D), jnp.float32) + conv_bias
        for tap_row in range(KS):
            for tap_col in range(KS):
                convolved = convolved + kernel[tap_row * KS + tap_col] * padded[tap_row:tap_row + height, tap_col:tap_col + breadth]
        average = lax.optimization_barrier(jnp.mean(convolved, axis=-1, keepdims=True))
        centered = convolved - average
        variance = lax.optimization_barrier(jnp.mean(centered * centered, axis=-1, keepdims=True))
        inverse = lax.rsqrt(variance + 1e-06)
        standard = (centered * inverse).reshape(height * breadth, D)
        inverse = inverse.reshape(height * breadth, 1)
        normed = (standard * norm_gain + norm_bias).astype(jnp.bfloat16)
        pre = jnp.dot(normed, in_weight.T, preferred_element_type=jnp.float32) + hidden_bias.astype(jnp.float32)
        hidden = gelu_exact(pre).astype(jnp.bfloat16)
        projected = jnp.dot(hidden, out_weight, preferred_element_type=jnp.float32) + out_bias
        flat_source = source.reshape(height * breadth, D)
        block = (flat_source + layer_scale * projected).astype(jnp.bfloat16)
        upstream = upper.astype(jnp.float32).reshape(height * breadth, D)
        scale_part = lax.optimization_barrier(jnp.sum(upstream * projected, axis=0))
        back_out = (upstream * layer_scale).astype(jnp.bfloat16)
        back_hidden = jnp.dot(back_out, out_weight.T, preferred_element_type=jnp.float32)
        back_pre = (back_hidden * gelu_slope(pre)).astype(jnp.bfloat16)
        back_normed = jnp.dot(back_pre, in_weight, preferred_element_type=jnp.float32)
        gain_part = lax.optimization_barrier(jnp.sum(back_normed * standard, axis=0))
        nbias_part = lax.optimization_barrier(jnp.sum(back_normed, axis=0))
        scaled = back_normed * norm_gain
        back_conv = inverse * (scaled - lax.optimization_barrier(jnp.mean(scaled, axis=-1, keepdims=True)) - standard * lax.optimization_barrier(jnp.mean(scaled * standard, axis=-1, keepdims=True)))
        cbias_part = lax.optimization_barrier(jnp.sum(back_conv, axis=0))
        back_grid = back_conv.reshape(height, breadth, D)
        back_wire = lax.optimization_barrier(back_grid.astype(jnp.bfloat16)).astype(jnp.float32)
        back_padded = jnp.pad(back_wire, ((margin, margin), (margin, margin), (0, 0)))
        grad_grid = upstream.reshape(height, breadth, D)
        kernel_rows = []
        for tap_row in range(KS):
            for tap_col in range(KS):
                tap = kernel[tap_row * KS + tap_col]
                grad_grid = grad_grid + tap * back_padded[2 * margin - tap_row:2 * margin - tap_row + height, 2 * margin - tap_col:2 * margin - tap_col + breadth]
                kernel_rows.append(lax.optimization_barrier(jnp.sum(back_grid * padded[tap_row:tap_row + height, tap_col:tap_col + breadth], axis=(0, 1))))
        vectors = jnp.stack([cbias_part, gain_part, nbias_part, scale_part])
        return (block.reshape(height, breadth, D), grad_grid.astype(jnp.bfloat16), jnp.stack(kernel_rows), vectors)
    blocks, grads, kernel_parts, vector_parts = lax.map(one_image, (to_image(features), to_image(cotangent)))
    factor = 1.0 / math.sqrt(PIXELS)
    kernel_total = lax.optimization_barrier(jnp.sum(kernel_parts, axis=0)) * factor
    vector_total = lax.optimization_barrier(jnp.sum(vector_parts, axis=0)) * factor
    return (to_tiles(blocks), to_tiles(grads), kernel_total, vector_total[0], vector_total[1], vector_total[2], vector_total[3])
```

```python
import functools
import math

import jax
import jax.numpy as jnp
from jax import lax
from jax.experimental import pallas as pl
from jax.experimental.pallas import tpu as pltpu
from jax.sharding import PartitionSpec as P

KS = 7
GX = 4
NX, NY, NZ = 4, 8, 8
MESH = pl.DeviceIdType.MESH
VMEM = pl.BlockSpec(memory_space=pltpu.VMEM)
F32 = jnp.float32
BF16 = jnp.bfloat16
DMA = pltpu.SemaphoreType.DMA


def place():
    dp = lax.axis_index("dp")
    tile = lax.axis_index("tile")
    x = lax.rem(dp, 4)
    y = lax.div(tile, 16) * 4 + lax.div(dp, 4)
    z = lax.rem(lax.div(tile, 2), 8)
    core = lax.rem(tile, 2)
    return x, y, z, core


def device(x, y, z, core):
    return (lax.rem(y, 4) * 4 + x, lax.div(y, 4) * 16 + z * 2 + core)


def turned(index, by, size):
    return lax.rem(index + (by % size), size)


def greet(barrier, peer):
    pl.semaphore_signal(barrier, inc=1, device_id=peer, device_id_type=MESH)


def remote(src, dst, ssem, rsem, peer):
    return pltpu.make_async_remote_copy(
        src_ref=src, dst_ref=dst, send_sem=ssem, recv_sem=rsem, device_id=peer, device_id_type=MESH
    )


STEPS = [(-1, 0), (1, 0), (0, -1), (0, 1), (-1, -1), (-1, 1), (1, -1), (1, 1)]


def halo_sides():
    dp = lax.axis_index("dp")
    tile = lax.axis_index("tile")
    ty = lax.div(tile, GX)
    tx = lax.rem(tile, GX)
    sides = []
    for dr, dc in STEPS:
        there = None
        for ok in ([ty >= 1] if dr < 0 else [ty <= 6] if dr > 0 else []) + (
            [tx >= 1] if dc < 0 else [tx <= 2] if dc > 0 else []
        ):
            there = ok if there is None else there & ok
        sides.append((there, (dp, tile + dr * GX + dc)))
    return sides


def halo_greet(barrier):
    for there, peer in halo_sides():
        @pl.when(there)
        def _():
            greet(barrier, peer)


def halo_count():
    count = 0
    for there, _ in halo_sides():
        count = count + there.astype(jnp.int32)
    return count


def halo_copies(field, edges, rows, cols, cors, ssem, rsem):
    src = [field.at[0:3], field.at[5:8], edges.at[0:24], edges.at[24:48]]
    src += [edges.at[48 + 16 * k : 64 + 16 * k] for k in range(4)]
    dst = [rows.at[1], rows.at[0], cols.at[1], cols.at[0], cors.at[3], cors.at[2], cors.at[1], cors.at[0]]
    back = [1, 0, 3, 2, 7, 6, 5, 4]
    out = []
    for k, (there, peer) in enumerate(halo_sides()):
        out.append((there, remote(src[k], dst[k], ssem.at[k], rsem.at[back[k]], peer)))
    return out, dst, back


def halo_start(copies):
    for there, copy in copies[0]:
        @pl.when(there)
        def _():
            copy.start()


def halo_finish(copies, rsem):
    moves, dst, back = copies
    for k, (there, copy) in enumerate(moves):
        landed = dst[back[k]]
        @pl.when(there)
        def _():
            pltpu.make_async_copy(landed, landed, rsem.at[k]).wait()
            copy.wait_send()

        @pl.when(jnp.logical_not(there))
        def _():
            landed[...] = jnp.zeros(landed.shape, landed.dtype)


def head_body(field, edges, par, bia, rows, cols, cors, pars, bias, row, zbias, hs, hr, ps, pr, zs, zr, bs, br):
    x, y, z, core = place()
    dp = lax.axis_index("dp")
    tile = lax.axis_index("tile")
    barrier = pltpu.get_barrier_semaphore()
    halo_greet(barrier)
    dps = [(turned(dp, k, 16), tile) for k in range(1, 16)]
    zps = [device(x, y, turned(z, k, NZ), core) for k in range(1, NZ)]
    xys = []
    for k in range(1, 32):
        ky, kx = k // 4, k % 4
        xys.append(device(turned(x, kx, NX), turned(y, ky, NY), z, core))
    for peer in dps + zps + xys:
        greet(barrier, peer)
    pl.semaphore_wait(barrier, 15 + 7 + 31 + halo_count())
    zcp = [remote(bia, zbias.at[z], zs.at[k], zr.at[k], peer) for k, peer in enumerate(zps)]
    for copy in zcp:
        copy.start()
    copies = halo_copies(field, edges, rows, cols, cors, hs, hr)
    halo_start(copies)
    pcp = [remote(par, pars.at[dp], ps.at[k], pr.at[k], peer) for k, peer in enumerate(dps)]
    for copy in pcp:
        copy.start()
    zbias[z] = bia[...]
    pars[dp] = par[...]
    for copy in zcp:
        copy.wait()
    total = zbias[0]
    for k in range(1, NZ):
        total = total + pltpu.roll(zbias[k], 6 * k, 1)
    row[...] = total
    me = x * 8 + y
    bias[me] = total
    bcp = [remote(row, bias.at[me], bs.at[k], br.at[k], peer) for k, peer in enumerate(xys)]
    for copy in bcp:
        copy.start()
    halo_finish(copies, hr)
    for copy in pcp:
        copy.wait()
    for copy in bcp:
        copy.wait()


def head(field, edges, par, bia):
    width = field.shape[-1]
    return pl.pallas_call(
        head_body,
        out_shape=(
            jax.ShapeDtypeStruct((2, 3, 16, width), BF16),
            jax.ShapeDtypeStruct((2, 24, width), BF16),
            jax.ShapeDtypeStruct((4, 16, width), BF16),
            jax.ShapeDtypeStruct((16, 28, 128), F32),
            jax.ShapeDtypeStruct((32, 1, 128), F32),
        ),
        in_specs=[VMEM] * 4,
        out_specs=[VMEM] * 5,
        scratch_shapes=[
            pltpu.VMEM((1, 128), F32),
            pltpu.VMEM((8, 1, 128), F32),
            DMA((8,)), DMA((8,)), DMA((15,)), DMA((15,)), DMA((7,)), DMA((7,)), DMA((31,)), DMA((31,)),
        ],
        compiler_params=pltpu.CompilerParams(collective_id=0, has_side_effects=True),
        name="head",
    )(field, edges, par, bia)


def halo_body(field, edges, rows, cols, cors, hs, hr):
    barrier = pltpu.get_barrier_semaphore()
    halo_greet(barrier)
    pl.semaphore_wait(barrier, halo_count())
    copies = halo_copies(field, edges, rows, cols, cors, hs, hr)
    halo_start(copies)
    halo_finish(copies, hr)


def halo(field, edges):
    width = field.shape[-1]
    return pl.pallas_call(
        halo_body,
        out_shape=(
            jax.ShapeDtypeStruct((2, 3, 16, width), BF16),
            jax.ShapeDtypeStruct((2, 24, width), BF16),
            jax.ShapeDtypeStruct((4, 16, width), BF16),
        ),
        in_specs=[VMEM] * 2,
        out_specs=[VMEM] * 3,
        scratch_shapes=[DMA((8,)), DMA((8,))],
        compiler_params=pltpu.CompilerParams(collective_id=1, has_side_effects=True),
        name="halo",
    )(field, edges)


def edges_of(field):
    width = field.shape[-1]

    def corner(rows, cols):
        return jnp.pad(field[rows, cols].reshape(9, width), ((0, 7), (0, 0)))

    low, high, left, right = slice(0, 3), slice(5, 8), slice(0, 3), slice(13, 16)
    return jnp.concatenate(
        [
            field[:, left].reshape(24, width),
            field[:, right].reshape(24, width),
            corner(low, left),
            corner(low, right),
            corner(high, left),
            corner(high, right),
        ]
    )


def padded_of(field, rows, cols, cors):
    width = field.shape[-1]
    cor = cors[:, :9].reshape(4, 3, 3, width)
    side = cols.reshape(2, 8, 3, width)
    return jnp.concatenate(
        [
            jnp.concatenate([cor[0], rows[0], cor[1]], axis=1),
            jnp.concatenate([side[0], field, side[1]], axis=1),
            jnp.concatenate([cor[2], rows[1], cor[3]], axis=1),
        ]
    )


OFF4 = [0, -1, 1, 2]
OFF8 = [0, -1, 1, -2, 2, -3, 3, 4]


def ring_slots(n, count):
    half = n // 2
    right = [(s, j) for s in range(1, half) for j in range(count)] + [(half, j) for j in range(count // 2)]
    left = [(s, j) for s in range(1, half) for j in range(count)] + [(half, j) for j in range(count // 2, count)]
    return right, left


class Ring:
    def __init__(self, n, count, offs, sub, peers, ssem, rsem, wire):
        self.n, self.count, self.offs, self.sub, self.peers = n, count, offs, sub, peers
        self.ssem, self.rsem, self.wire = ssem, rsem, wire
        self.slots = ring_slots(n, count)

    def copy(self, way, s, j):
        i = self.slots[way].index((s, j))
        ref = self.sub(-(s - 1) if way == 0 else (s - 1), j)
        return remote(ref, ref, self.ssem.at[way, i], self.rsem.at[way, i], self.peers[way])

    def landed(self, way, s, j):
        i = self.slots[way].index((s, j))
        ref = self.sub(-s if way == 0 else s, j)
        return pltpu.make_async_copy(ref, ref, self.rsem.at[way, i])


def plan(outer, inner):
    events = []
    latency = 1.7
    for c, (o, i) in enumerate(zip(outer, inner)):
        ready = {0: 0.0}
        for way in (0, 1):
            t, got = 0.0, {}
            for s, j in i.slots[way]:
                t = max(t, 0.0 if s == 1 else got[s - 1, j]) + i.wire
                got[s, j] = t + latency
                events.append((got[s, j], c, 0, way, s, j))
        for way in (0, 1):
            for s, j in i.slots[way]:
                pass
        half = i.n // 2
        seen = {(e[3], e[4], e[5]): e[0] for e in events if e[1] == c and e[2] == 0}
        for k, off in enumerate(o.offs):
            if off == 0:
                continue
            if abs(off) == half:
                ready[k] = max(v for (w, s, j), v in seen.items() if s == half)
            else:
                ready[k] = max(v for (w, s, j), v in seen.items() if s == abs(off) and w == (0 if off < 0 else 1))
        for way in (0, 1):
            t, got = 0.0, {}
            for s, j in o.slots[way]:
                t = max(t, ready[j] if s == 1 else got[s - 1, j]) + o.wire
                got[s, j] = t + latency
                events.append((got[s, j], c, 1, way, s, j))
    return sorted(events)


def mlp_body(normed, bout, wt, bias, mlp_out, bn_out, rz, ry, scr, g0, g1, g2, act, acc, part,
             as_, ar, s0s, s0r, p1s, p1r, q0s, q0r, q1s, q1r, q2s, q2r, r0s, r0r, r1s, r1r, r2s, r2r, es, er):
    x, y, z, core = place()
    barrier = pltpu.get_barrier_semaphore()
    sibling = device(x, y, z, 1 - core)
    xps = [device(turned(x, k, NX), y, z, core) for k in range(1, NX)]
    yps = [device(x, turned(y, k, NY), z, core) for k in range(1, NY)]
    zps = [device(x, y, turned(z, k, NZ), core) for k in range(1, NZ)]
    for peer in [sibling] + xps + yps + zps:
        greet(barrier, peer)
    pl.semaphore_wait(barrier, 1 + 3 + 7 + 7)

    copies = []
    for k in range(1, NZ):
        copies.append(remote(wt.at[turned(z, k, NZ)], rz.at[z], s0s.at[0, k - 1], s0r.at[0, k - 1], zps[k - 1]))
    for k in range(1, NY):
        copies.append(remote(wt.at[turned(y, k, NY)], ry.at[y], s0s.at[1, k - 1], s0r.at[1, k - 1], yps[k - 1]))
    for copy in copies:
        copy.start()
    ship = []
    for a, src in enumerate((normed, bout)):
        ship.append(remote(src, act.at[a, core], as_.at[a], ar.at[a], sibling))
        ship[-1].start()
    rz[z] = wt[z]
    ry[y] = wt[y]
    act[0, core] = normed[...]
    act[1, core] = bout[...]
    for copy in copies:
        copy.wait()
    home = (g0.at[y, x, z], g1.at[x, z, y], g2.at[z, y, x])
    for k in range(3):
        src = (rz, ry, ry)[k]
        for d in range(8):
            val = src[d].astype(F32)
            scr[k, 0, 2 * d : 2 * d + 2, :] = val[2 * k : 2 * k + 2]
            scr[k, 1, 2 * d : 2 * d + 2, :] = val[6 + 2 * k : 8 + 2 * k]
        home[k][...] = scr[k].astype(BF16)
    first = []
    for k, peers in enumerate((zps, yps, xps)):
        row = [remote(home[k], home[k], p1s.at[k, i], p1r.at[k, i], peer) for i, peer in enumerate(peers)]
        for copy in row:
            copy.start()
        first.append(row)

    xr, xl = xps[0], xps[-1]
    yr, yl = yps[0], yps[-1]
    zr, zl = zps[0], zps[-1]
    inner = [
        Ring(4, 2, None, lambda b, j: g0.at[y, turned(x, b, 4), pl.ds(4 * j, 4)], (xr, xl), q0s, q0r, 0.7),
        Ring(8, 2, None, lambda b, j: g1.at[x, turned(z, b, 8), pl.ds(4 * j, 4)], (zr, zl), q1s, q1r, 0.7),
        Ring(8, 2, None, lambda b, j: g2.at[z, turned(y, b, 8), pl.ds(2 * j, 2)], (yr, yl), q2s, q2r, 0.35),
    ]
    outer = [
        Ring(8, 4, OFF4, lambda b, j: g0.at[turned(y, b, 8), turned(x, OFF4[j], 4)], (yr, yl), r0s, r0r, 1.4),
        Ring(4, 8, OFF8, lambda b, j: g1.at[turned(x, b, 4), turned(z, OFF8[j], 8)], (xr, xl), r1s, r1r, 1.4),
        Ring(8, 8, OFF8, lambda b, j: g2.at[turned(z, b, 8), turned(y, OFF8[j], 8)], (zr, zl), r2s, r2r, 0.7),
    ]
    started = []

    def go(copy):
        copy.start()
        started.append(copy)

    for k in range(3):
        for copy in first[k]:
            copy.wait()
        for way in (0, 1):
            go(outer[k].copy(way, 1, 0)) if (1, 0) in outer[k].slots[way] else None
            for j in range(2):
                go(inner[k].copy(way, 1, j))
    for _, k, level, way, s, j in plan(outer, inner):
        ring = (inner, outer)[level][k]
        ring.landed(way, s, j).wait()
        if (s + 1, j) in ring.slots[way]:
            go(ring.copy(way, s + 1, j))
        if level == 0 and j == (1 if s < ring.n // 2 else way):
            half = ring.n // 2
            if s == half:
                if way == 0:
                    continue
                index = outer[k].offs.index(half)
            else:
                index = outer[k].offs.index(-s if way == 0 else s)
            for w in (0, 1):
                if (1, index) in outer[k].slots[w]:
                    go(outer[k].copy(w, 1, index))
    for copy in ship:
        copy.wait()

    acc[...] = jnp.zeros_like(acc)
    a_in = act[0].reshape(256, 1024)
    a_out = act[1].reshape(256, 1024)
    nt = (((1,), (1,)), ((), ()))

    def chunk(read, number):
        w_in = jnp.concatenate([read(cb, 0).reshape(256, 128) for cb in range(8)], axis=1)
        w_out = jnp.concatenate([read(cb, 1).reshape(256, 128) for cb in range(8)], axis=1)
        pre = lax.dot_general(a_in, w_in, nt, preferred_element_type=F32) + bias[number]
        back = lax.dot_general(a_out, w_out, nt, preferred_element_type=F32)
        cdf = 0.5 * (1.0 + lax.erf(pre * 0.7071067811865476))
        hidden = (pre * cdf).astype(BF16)
        slope = cdf + pre * jnp.exp(-0.5 * pre * pre) * 0.3989422804014327
        back_pre = (back * slope).astype(BF16)
        acc[0] += jnp.dot(hidden, w_out, preferred_element_type=F32).reshape(2, 128, 1024)
        acc[1] += jnp.dot(back_pre, w_in, preferred_element_type=F32).reshape(2, 128, 1024)

    for k in range(3):
        def step(i, carry):
            if k == 0:
                chunk(lambda cb, m: g0[pl.ds(4 * i, 4), :, cb, m], i)
            elif k == 1:
                chunk(lambda cb, m: g1[pl.ds(2 * i, 2), :, cb, m], 2 + i)
            else:
                chunk(lambda cb, m: g2[pl.ds(4 * i, 4), cb, :, m], 4 + i)
            return carry

        lax.fori_loop(0, 2, step, 0)
    swap = []
    for a in range(2):
        swap.append(remote(acc.at[a, 1 - core], part.at[a], es.at[a], er.at[a], sibling))
        swap[-1].start()
    for a, out in enumerate((mlp_out, bn_out)):
        swap[a].wait_recv()
        out[...] = acc[a, core] + part[a]
    for copy in started + swap:
        copy.wait_send()


def mlp(normed, bout, wt, bias):
    tile = (2, 16, 128)
    return pl.pallas_call(
        mlp_body,
        out_shape=(jax.ShapeDtypeStruct((128, 1024), F32), jax.ShapeDtypeStruct((128, 1024), F32)),
        in_specs=[VMEM] * 4,
        out_specs=[VMEM] * 2,
        scratch_shapes=[
            pltpu.VMEM((8, 16, 128), BF16),
            pltpu.VMEM((8, 16, 128), BF16),
            pltpu.VMEM((3, 2, 16, 128), F32),
            pltpu.VMEM((8, 4, 8) + tile, BF16),
            pltpu.VMEM((4, 8, 8) + tile, BF16),
            pltpu.VMEM((8, 8, 4) + tile, BF16),
            pltpu.VMEM((2, 2, 128, 1024), BF16),
            pltpu.VMEM((2, 2, 128, 1024), F32),
            pltpu.VMEM((2, 128, 1024), F32),
            DMA((2,)), DMA((2,)), DMA((2, 7)), DMA((2, 7)), DMA((3, 7)), DMA((3, 7)),
            DMA((2, 3)), DMA((2, 3)), DMA((2, 7)), DMA((2, 7)), DMA((2, 7)), DMA((2, 7)),
            DMA((2, 14)), DMA((2, 14)), DMA((2, 12)), DMA((2, 12)), DMA((2, 28)), DMA((2, 28)),
            DMA((2,)), DMA((2,)),
        ],
        compiler_params=pltpu.CompilerParams(
            collective_id=2, has_side_effects=True, vmem_limit_bytes=48 * 1024 * 1024
        ),
        name="mlp",
    )(normed, bout, wt, bias)


def reduce_body(sums, out, r1, r2, r3, mid, low, fin, s1, t1, s2, t2, s3, t3, s4, t4):
    x, y, z, core = place()
    yl, yh = lax.rem(y, 4), lax.div(y, 4)
    xl, xh = lax.rem(x, 2), lax.div(x, 2)
    mine = yl * 2 + xh
    barrier = pltpu.get_barrier_semaphore()
    firsts, blocks = [], []
    for k in range(1, 8):
        other = turned(mine, k, 8)
        blocks.append(other)
        firsts.append(device(lax.rem(other, 2) * 2 + xl, yh * 4 + lax.div(other, 2), z, core))
    zps = [device(x, y, turned(z, k, NZ), core) for k in range(1, NZ)]
    member = yh * 4 + xl * 2 + core
    thirds = []
    for k in range(1, 8):
        o = turned(member, k, 8)
        thirds.append(device(xh * 2 + lax.rem(lax.div(o, 2), 2), lax.div(o, 4) * 4 + yl, z, lax.rem(o, 2)))
    for peer in firsts + zps + thirds:
        greet(barrier, peer)
    pl.semaphore_wait(barrier, 21)

    def lanes(block):
        return sums.at[:, pl.ds(pl.multiple_of(block * 128, 128), 128)]

    c1 = [remote(lanes(blocks[k]), r1.at[mine], s1.at[k], t1.at[k], firsts[k]) for k in range(7)]
    for copy in c1:
        copy.start()
    r1[mine] = lanes(mine)[...]
    for copy in c1:
        copy.wait()
    mid[...] = jnp.sum(r1[...], axis=0).reshape(8, 8, 128)
    c2 = [remote(mid.at[turned(z, k + 1, 8)], r2.at[z], s2.at[k], t2.at[k], zps[k]) for k in range(7)]
    for copy in c2:
        copy.start()
    r2[z] = mid[z]
    for copy in c2:
        copy.wait()
    low[...] = jnp.sum(r2[...], axis=0)
    c3 = [remote(low, r3.at[member], s3.at[k], t3.at[k], thirds[k]) for k in range(7)]
    for copy in c3:
        copy.start()
    r3[member] = low[...]
    for copy in c3:
        copy.wait()
    fin[...] = jnp.sum(r3[...], axis=0)
    c4 = [remote(fin, out.at[z], s4.at[k], t4.at[k], zps[k]) for k in range(7)]
    for copy in c4:
        copy.start()
    out[z] = fin[...]
    for copy in c4:
        copy.wait()


def reduced(sums):
    return pl.pallas_call(
        reduce_body,
        out_shape=jax.ShapeDtypeStruct((8, 8, 128), F32),
        in_specs=[VMEM],
        out_specs=VMEM,
        scratch_shapes=[
            pltpu.VMEM((8, 64, 128), F32),
            pltpu.VMEM((8, 8, 128), F32),
            pltpu.VMEM((8, 8, 128), F32),
            pltpu.VMEM((8, 8, 128), F32),
            pltpu.VMEM((8, 128), F32),
            pltpu.VMEM((8, 128), F32),
        ]
        + [DMA((7,))] * 8,
        compiler_params=pltpu.CompilerParams(collective_id=3, has_side_effects=True),
        name="reduced",
    )(sums)


def per_device(
    features,
    cotangent,
    in_weight,
    out_weight,
    hidden_bias,
    kernel,
    conv_bias,
    norm_gain,
    norm_bias,
    layer_scale,
    out_bias,
):
    _, _, rows, cols, width = features.shape
    margin = KS // 2
    pixel_rows = rows * cols
    field = features.reshape(rows, cols, width)
    slab = jnp.concatenate(
        [kernel] + [v[None] for v in (conv_bias, norm_gain, norm_bias, layer_scale, out_bias)] + [jnp.zeros((2, 64), F32)]
    )
    par = jnp.concatenate([slab[:28], slab[28:]], axis=1)
    bia = jnp.pad(hidden_bias.astype(F32)[None], ((0, 0), (0, 122)))
    hrows, hcols, hcors, pars, bias = head(field, edges_of(field), par, bia)
    pars = pars.reshape(16, 28, 2, 64).transpose(2, 1, 0, 3).reshape(56, width)
    kernel_all = pars[:49]
    cbias, gain, nbias, lscale, obias = (pars[49 + i] for i in range(5))
    b = bias.reshape(4, 8, 128)[:, :, :48].reshape(4, 8, 8, 6)
    bias_rows = jnp.concatenate(
        [
            b[..., 0:2].transpose(1, 0, 2, 3).reshape(2, 1, 256),
            b[..., 2:4].transpose(0, 2, 1, 3).reshape(2, 1, 256),
            b[..., 4:6].transpose(2, 0, 1, 3).reshape(2, 1, 256),
        ]
    )
    both = jnp.concatenate([in_weight, out_weight, jnp.zeros((4, width), BF16)])
    wt = both.reshape(16, 8, 128).transpose(1, 0, 2)

    padded = padded_of(field, hrows, hcols, hcors)
    convolved = jnp.zeros((rows, cols, width), F32) + cbias
    for tap_row in range(KS):
        for tap_col in range(KS):
            window = padded[tap_row : tap_row + rows, tap_col : tap_col + cols, :].astype(F32)
            convolved = convolved + kernel_all[tap_row * KS + tap_col] * window
    average = jnp.mean(convolved, axis=-1, keepdims=True)
    centered = convolved - average
    variance = jnp.mean(centered * centered, axis=-1, keepdims=True)
    inverse = lax.rsqrt(variance + 1e-06)
    standard = (centered * inverse).reshape(pixel_rows, width)
    inverse = inverse.reshape(pixel_rows, 1)
    normed = (standard * gain + nbias).astype(BF16)
    upstream = cotangent.reshape(pixel_rows, width).astype(F32)
    back_out = (upstream * lscale).astype(BF16)

    mlp_sum, back_normed = mlp(normed, back_out, wt, bias_rows)

    projected = mlp_sum + obias
    source = field.reshape(pixel_rows, width).astype(F32)
    block_out = (source + lscale * projected).astype(BF16).reshape(features.shape)
    scale_part = jnp.sum(upstream * projected, axis=0)
    gain_part = jnp.sum(back_normed * standard, axis=0)
    nbias_part = jnp.sum(back_normed, axis=0)
    scaled = back_normed * gain
    back_conv = inverse * (
        scaled
        - jnp.mean(scaled, axis=-1, keepdims=True)
        - standard * jnp.mean(scaled * standard, axis=-1, keepdims=True)
    )
    cbias_part = jnp.sum(back_conv, axis=0)
    back_grid = back_conv.reshape(rows, cols, width)
    wire = back_grid.astype(BF16)
    wrows, wcols, wcors = halo(wire, edges_of(wire))
    back_padded = padded_of(wire, wrows, wcols, wcors)
    grad_grid = upstream.reshape(rows, cols, width)
    kernel_rows = []
    for tap_row in range(KS):
        for tap_col in range(KS):
            tap_weight = kernel_all[tap_row * KS + tap_col]
            flipped = back_padded[
                2 * margin - tap_row : 2 * margin - tap_row + rows,
                2 * margin - tap_col : 2 * margin - tap_col + cols,
                :,
            ].astype(F32)
            grad_grid = grad_grid + tap_weight * flipped
            window = padded[tap_row : tap_row + rows, tap_col : tap_col + cols, :].astype(F32)
            kernel_rows.append(jnp.sum(back_grid * window, axis=(0, 1)))
    grad_input = grad_grid.astype(BF16).reshape(features.shape)
    sums = jnp.stack(kernel_rows + [cbias_part, gain_part, nbias_part, scale_part] + [jnp.zeros(width, F32)] * 11)
    total = reduced(sums).reshape(64, 2, 64)
    half = lax.rem(lax.axis_index("dp"), 2)
    factor = 1.0 / math.sqrt(65536)
    total = jnp.where(half == 0, total[:, 0], total[:, 1]) * factor
    return (block_out, grad_input, total[:49], total[49], total[50], total[51], total[52])


def solution(mesh):
    placed = (
        P("dp", "tile", None, None, None),
        P("dp", "tile", None, None, None),
        P(("dp", "tile"), None),
        P(("dp", "tile"), None),
        P(("dp", "tile")),
        P(None, "dp"),
        P("dp"),
        P("dp"),
        P("dp"),
        P("dp"),
        P("dp"),
    )
    return jax.shard_map(
        per_device,
        mesh=mesh,
        in_specs=placed,
        out_specs=(
            P("dp", "tile", None, None, None),
            P("dp", "tile", None, None, None),
            P(None, "dp"),
            P("dp"),
            P("dp"),
            P("dp"),
            P("dp"),
        ),
        check_vma=False,
    )
```

```python
import functools

import jax
import jax.numpy as jnp
from jax import lax
from jax.experimental import pallas as pl
from jax.experimental.pallas import tpu as pltpu
from jax.sharding import PartitionSpec as P

KS = 7
GX = 4
NX, NY, NZ = 4, 8, 8
MESH = pl.DeviceIdType.MESH
VMEM = pl.BlockSpec(memory_space=pltpu.VMEM)
F32 = jnp.float32
BF16 = jnp.bfloat16
DMA = pltpu.SemaphoreType.DMA


def place():
    dp = lax.axis_index("dp")
    tile = lax.axis_index("tile")
    x = lax.rem(dp, 4)
    y = lax.div(tile, 16) * 4 + lax.div(dp, 4)
    z = lax.rem(lax.div(tile, 2), 8)
    core = lax.rem(tile, 2)
    return x, y, z, core


def device(x, y, z, core):
    return (lax.rem(y, 4) * 4 + x, lax.div(y, 4) * 16 + z * 2 + core)


def turned(index, by, size):
    return lax.rem(index + (by % size), size)


def greet(barrier, peer):
    pl.semaphore_signal(barrier, inc=1, device_id=peer, device_id_type=MESH)


def remote(src, dst, ssem, rsem, peer):
    return pltpu.make_async_remote_copy(
        src_ref=src, dst_ref=dst, send_sem=ssem, recv_sem=rsem, device_id=peer, device_id_type=MESH
    )


STEPS = [(-1, 0), (1, 0), (0, -1), (0, 1), (-1, -1), (-1, 1), (1, -1), (1, 1)]


def halo_sides():
    dp = lax.axis_index("dp")
    tile = lax.axis_index("tile")
    ty = lax.div(tile, GX)
    tx = lax.rem(tile, GX)
    sides = []
    for dr, dc in STEPS:
        there = None
        for ok in ([ty >= 1] if dr < 0 else [ty <= 6] if dr > 0 else []) + (
            [tx >= 1] if dc < 0 else [tx <= 2] if dc > 0 else []
        ):
            there = ok if there is None else there & ok
        sides.append((there, (dp, tile + dr * GX + dc)))
    return sides


OFF4 = [0, -1, 1, 2]
OFF8 = [0, -1, 1, -2, 2, -3, 3, 4]


def ring_slots(n, count):
    half = n // 2
    right = [(s, j) for s in range(1, half) for j in range(count)] + [(half, j) for j in range(count // 2)]
    left = [(s, j) for s in range(1, half) for j in range(count)] + [(half, j) for j in range(count // 2, count)]
    return right, left


class Ring:
    def __init__(self, n, count, offs, sub, peers, ssem, rsem, wire):
        self.n, self.count, self.offs, self.sub, self.peers = n, count, offs, sub, peers
        self.ssem, self.rsem, self.wire = ssem, rsem, wire
        self.slots = ring_slots(n, count)

    def copy(self, way, s, j):
        i = self.slots[way].index((s, j))
        ref = self.sub(-(s - 1) if way == 0 else (s - 1), j)
        return remote(ref, ref, self.ssem.at[way, i], self.rsem.at[way, i], self.peers[way])

    def landed(self, way, s, j):
        i = self.slots[way].index((s, j))
        ref = self.sub(-s if way == 0 else s, j)
        return pltpu.make_async_copy(ref, ref, self.rsem.at[way, i])


def plan(outer, inner):
    events = []
    latency = 1.7
    for c, (o, i) in enumerate(zip(outer, inner)):
        ready = {0: 0.0}
        for way in (0, 1):
            t, got = 0.0, {}
            for s, j in i.slots[way]:
                t = max(t, 0.0 if s == 1 else got[s - 1, j]) + i.wire
                got[s, j] = t + latency
                events.append((got[s, j], c, 0, way, s, j))
        for way in (0, 1):
            for s, j in i.slots[way]:
                pass
        half = i.n // 2
        seen = {(e[3], e[4], e[5]): e[0] for e in events if e[1] == c and e[2] == 0}
        for k, off in enumerate(o.offs):
            if off == 0:
                continue
            if abs(off) == half:
                ready[k] = max(v for (w, s, j), v in seen.items() if s == half)
            else:
                ready[k] = max(v for (w, s, j), v in seen.items() if s == abs(off) and w == (0 if off < 0 else 1))
        for way in (0, 1):
            t, got = 0.0, {}
            for s, j in o.slots[way]:
                t = max(t, ready[j] if s == 1 else got[s - 1, j]) + o.wire
                got[s, j] = t + latency
                events.append((got[s, j], c, 1, way, s, j))
    return sorted(events)


def halo_count():
    count = 0
    for there, _ in halo_sides():
        count = count + there.astype(jnp.int32)
    return count


BACK = [1, 0, 3, 2, 7, 6, 5, 4]


class Halo:
    def __init__(self, grid, ecol, ecor, rows, cols, cors, ssem, rsem):
        self.grid, self.ecol, self.ecor = grid, ecol, ecor
        self.rows, self.cols, self.cors = rows, cols, cors
        src = [grid.at[:, 0:3], grid.at[:, 5:8], ecol.at[0], ecol.at[1]] + [ecor.at[k] for k in range(4)]
        self.dst = [rows.at[1], rows.at[0], cols.at[1], cols.at[0], cors.at[3], cors.at[2], cors.at[1], cors.at[0]]
        self.rsem = rsem
        self.moves = []
        for k, (there, peer) in enumerate(halo_sides()):
            self.moves.append((there, remote(src[k], self.dst[k], ssem.at[k], rsem.at[BACK[k]], peer)))

    def start(self):
        for there, copy in self.moves:
            @pl.when(there)
            def _():
                copy.start()

    def finish(self):
        for k, (there, copy) in enumerate(self.moves):
            landed = self.dst[BACK[k]]
            @pl.when(there)
            def _():
                pltpu.make_async_copy(landed, landed, self.rsem.at[k]).wait()
                copy.wait_send()

            @pl.when(jnp.logical_not(there))
            def _():
                landed[...] = jnp.zeros(landed.shape, landed.dtype)

    def cut(self, cb, value, stage):
        for i in range(8):
            stage[3 * i : 3 * i + 3, :] = value[i, 0:3, :]
            stage[24 + 3 * i : 27 + 3 * i, :] = value[i, 13:16, :]
        for k, (r, c) in enumerate(((0, 0), (0, 13), (5, 0), (5, 13))):
            for i in range(3):
                at = 48 + 16 * k + 3 * i
                stage[at : at + 3, :] = value[r + i, c : c + 3, :]
        self.ecol[0, cb] = stage[0:24, :].astype(BF16)
        self.ecol[1, cb] = stage[24:48, :].astype(BF16)
        for k in range(4):
            self.ecor[k, cb] = stage[48 + 16 * k : 64 + 16 * k, :].astype(BF16)

    def fill(self, cb, pad):
        pad[cb, 3:11, 8:24, :] = self.grid[cb].astype(F32)
        pad[cb, 0:3, 8:24, :] = self.rows[0, cb].astype(F32)
        pad[cb, 11:14, 8:24, :] = self.rows[1, cb].astype(F32)
        for side, col in ((0, 5), (1, 24)):
            value = self.cols[side, cb].astype(F32)
            for i in range(8):
                pad[cb, 3 + i, col : col + 3, :] = value[3 * i : 3 * i + 3, :]
        for k, (row, col) in enumerate(((0, 5), (0, 24), (11, 5), (11, 24))):
            value = self.cors[k, cb].astype(F32)
            for i in range(3):
                pad[cb, row + i, col : col + 3, :] = value[3 * i : 3 * i + 3, :]


def each(count, body):
    def step(i, carry):
        body(i)
        return carry

    lax.fori_loop(0, count, step, 0)


def block_conv(start, pad, taps, cb, flip):
    total = start
    for b in range(KS):
        window = pad[cb, :, 5 + b : 21 + b, :]
        for a in range(KS):
            tap = (6 - a) * KS + (6 - b) if flip else a * KS + b
            total = total + taps[cb, tap : tap + 1, :][None] * window[a : a + 8]
    return total


LAST = 5
CHUNKS = [
    [(0, 0), (2, 0), (1, 0)],
    [(0, -1), (0, 1), (2, -1), (2, 1)],
    [(1, -1), (1, 1)],
    [(0, -2), (0, 2), (2, -2), (2, 2)],
    [(0, -3), (0, 3), (2, -3), (2, 3)],
    [(0, 4), (2, 4), (1, 2)],
]


def whole_body(
    field, cot, wt, par, bia,
    block_out, grad_in, out_kernel, out_vec,
    fb, cb_, ecol, ecor, stage, hrows, hcols, hcors, wrows, wcols, wcors, pad, bpad, pars, taps, row, zbias, bias, table,
    rz, ry, scr, g0, g1, g2, act, hid, acc, part, mypart, conv, inv, bc, wire, ob, sums,
    r1, r2, r3, mid, low, fin, tot,
    ls, hs, hr, h2s, h2r, ps, pr, zs, zr, bs, br, as_, ar, s0s, s0r, p1s, p1r,
    q0s, q0r, q1s, q1r, q2s, q2r, r0s, r0r, r1s, r1r, r2s, r2r, es, er,
    s1, t1, s2, t2, s3, t3, s4, t4, os_,
):
    x, y, z, core = place()
    dp = lax.axis_index("dp")
    tile = lax.axis_index("tile")
    yl, yh = lax.rem(y, 4), lax.div(y, 4)
    xl, xh = lax.rem(x, 2), lax.div(x, 2)
    lane = lax.broadcasted_iota(jnp.int32, (1, 128), 1)
    barrier = pltpu.get_barrier_semaphore()
    sibling = device(x, y, z, 1 - core)
    xps = [device(turned(x, k, NX), y, z, core) for k in range(1, NX)]
    yps = [device(x, turned(y, k, NY), z, core) for k in range(1, NY)]
    zps = [device(x, y, turned(z, k, NZ), core) for k in range(1, NZ)]
    dps = [(turned(dp, k, 16), tile) for k in range(1, 16)]
    xys = [device(turned(x, k % 4, NX), turned(y, k // 4, NY), z, core) for k in range(1, 32)]
    mine = yl * 2 + xh
    member = yh * 4 + xl * 2 + core
    thirds = []
    for k in range(1, 8):
        o = turned(member, k, 8)
        thirds.append(device(xh * 2 + lax.rem(lax.div(o, 2), 2), lax.div(o, 4) * 4 + yl, z, lax.rem(o, 2)))
    for peer in xys + zps + thirds[0::2]:
        greet(barrier, peer)
    for there, peer in halo_sides():
        @pl.when(there)
        def _():
            greet(barrier, peer)

    loads = []
    for cb in range(8):
        lanes = pl.ds(128 * cb, 128)
        loads.append(pltpu.make_async_copy(field.at[:, :, lanes], fb.at[cb], ls.at[0, cb]))
        loads.append(pltpu.make_async_copy(cot.at[:, lanes], cb_.at[cb], ls.at[1, cb]))
    for copy in loads:
        copy.start()
    halo1 = Halo(fb, ecol, ecor, hrows, hcols, hcors, hs, hr)
    for copy in loads:
        copy.wait()
    pl.semaphore_wait(barrier, 31 + 7 + 4 + halo_count())

    zero = []
    for k in range(1, NZ):
        zero.append(remote(wt.at[turned(z, k, NZ)], rz.at[z], s0s.at[0, k - 1], s0r.at[0, k - 1], zps[k - 1]))
    for k in range(1, NY):
        zero.append(remote(wt.at[turned(y, k, NY)], ry.at[y], s0s.at[1, k - 1], s0r.at[1, k - 1], yps[k - 1]))
    for copy in zero:
        copy.start()
    zcp = [remote(bia, zbias.at[z], zs.at[k], zr.at[k], peer) for k, peer in enumerate(zps)]
    for copy in zcp:
        copy.start()
    pcp = [remote(par, pars.at[dp], ps.at[k], pr.at[k], peer) for k, peer in enumerate(dps)]
    for copy in pcp:
        copy.start()
    rz[z] = wt[z]
    ry[y] = wt[y]
    zbias[z] = bia[...]
    pars[dp] = par[...]
    stage[...] = jnp.zeros_like(stage)
    each(8, lambda cb: halo1.cut(cb, fb[cb].astype(F32), stage))
    halo1.start()

    for copy in zero:
        copy.wait()
    home = (g0.at[y, x, z], g1.at[x, z, y], g2.at[z, y, x])
    for k in range(3):
        src = (rz, ry, ry)[k]
        for d in range(8):
            val = src[d].astype(F32)
            scr[k, 0, 2 * d : 2 * d + 2, :] = val[2 * k : 2 * k + 2]
            scr[k, 1, 2 * d : 2 * d + 2, :] = val[6 + 2 * k : 8 + 2 * k]
        home[k][...] = scr[k].astype(BF16)
    first = []
    for k, peers in enumerate((zps, yps, xps)):
        line = [remote(home[k], home[k], p1s.at[k, i], p1r.at[k, i], peer) for i, peer in enumerate(peers)]
        for copy in line:
            copy.start()
        first.append(line)

    for copy in zcp:
        copy.wait()
    total = zbias[0]
    for k in range(1, NZ):
        total = total + pltpu.roll(zbias[k], 6 * k, 1)
    row[...] = total
    me = x * 8 + y
    bias[me] = total
    bcp = [remote(row, bias.at[me], bs.at[k], br.at[k], peer) for k, peer in enumerate(xys)]
    for copy in bcp:
        copy.start()

    xr, xb = xps[0], xps[-1]
    yr, yb = yps[0], yps[-1]
    zr_, zb = zps[0], zps[-1]
    inner = [
        Ring(4, 2, OFF4, lambda b, j: g0.at[y, turned(x, b, 4), pl.ds(4 * j, 4)], (xr, xb), q0s, q0r, 0.7),
        Ring(8, 2, OFF8, lambda b, j: g1.at[x, turned(z, b, 8), pl.ds(4 * j, 4)], (zr_, zb), q1s, q1r, 0.7),
        Ring(8, 2, OFF8, lambda b, j: g2.at[z, turned(y, b, 8), pl.ds(2 * j, 2)], (yr, yb), q2s, q2r, 0.35),
    ]
    outer = [
        Ring(8, 4, OFF4, lambda b, j: g0.at[turned(y, b, 8), turned(x, OFF4[j], 4)], (yr, yb), r0s, r0r, 1.4),
        Ring(4, 8, OFF8, lambda b, j: g1.at[turned(x, b, 4), turned(z, OFF8[j], 8)], (xr, xb), r1s, r1r, 1.4),
        Ring(8, 8, OFF8, lambda b, j: g2.at[turned(z, b, 8), turned(y, OFF8[j], 8)], (zr_, zb), r2s, r2r, 0.7),
    ]
    started = []

    def go(copy):
        copy.start()
        started.append(copy)

    def arrive(k, level, way, s, j):
        ring = (inner, outer)[level][k]
        ring.landed(way, s, j).wait()
        if (s + 1, j) in ring.slots[way]:
            go(ring.copy(way, s + 1, j))
        half = ring.n // 2
        if level == 0 and j == (1 if s < half else way) and not (s == half and way == 0):
            index = ring.offs.index(half if s == half else -s if way == 0 else s)
            for w in (0, 1):
                if (1, index) in outer[k].slots[w]:
                    go(outer[k].copy(w, 1, index))

    ship = [remote(act.at[a, core], act.at[a, core], as_.at[a], ar.at[a], sibling) for a in range(2)]

    def params():
        for copy in pcp:
            copy.wait()

        def unpack(cb):
            one, two = pars[2 * cb], pars[2 * cb + 1]
            taps[cb, 0:28, :] = jnp.where(lane < 64, one, pltpu.roll(two, 64, 1))
            taps[cb, 28:56, :] = jnp.where(lane < 64, pltpu.roll(one, 64, 1), two)

        each(8, unpack)
        for cb in range(8):
            scaled = cb_[cb].astype(F32) * taps[cb, 52:53, :]
            act[1, core, :, 128 * cb : 128 * cb + 128] = scaled.astype(BF16)

    def borders():
        ship[1].start()
        halo1.finish()
        each(8, lambda cb: halo1.fill(cb, pad))

    def conv_piece(part_number):
        def one(i):
            cb = i + 2 * part_number
            start = jnp.broadcast_to(taps[cb, 49:50, :][None], (8, 16, 128))
            conv[cb] = block_conv(start, pad, taps, cb, False).reshape(128, 128)

        each(2, one)

    def norm():
        mean = jnp.sum(sum(conv[cb] for cb in range(8)), axis=-1, keepdims=True) * (1.0 / 1024)
        square = jnp.zeros((128, 128), F32)
        for cb in range(8):
            centered = conv[cb] - mean
            square = square + centered * centered
        inverse = lax.rsqrt(jnp.sum(square, axis=-1, keepdims=True) * (1.0 / 1024) + 1e-06)
        inv[...] = jnp.broadcast_to(inverse, (128, 128))
        for cb in range(8):
            standard = (conv[cb] - mean) * inverse
            conv[cb] = standard
            normed = standard * taps[cb, 50:51, :] + taps[cb, 51:52, :]
            act[0, core, :, 128 * cb : 128 * cb + 128] = normed.astype(BF16)

    def biases():
        ship[0].start()
        for copy in bcp:
            copy.wait()
        values = bias[...].reshape(32, 128).astype(BF16)
        j = lax.broadcasted_iota(jnp.int32, (128, 128), 0)
        l = lax.broadcasted_iota(jnp.int32, (128, 128), 1)
        bx = lax.broadcasted_iota(jnp.int32, (4, 8, 128), 0)
        by = lax.broadcasted_iota(jnp.int32, (4, 8, 128), 1)
        bl = lax.broadcasted_iota(jnp.int32, (4, 8, 128), 2)
        l64 = bl & 63

        def pick(where):
            chosen = jnp.where(where, 1.0, 0.0).astype(BF16)
            return jnp.dot(values, chosen, preferred_element_type=F32).reshape(4, 8, 128)

        t0 = pick(j == 6 * ((l >> 1) & 7) + (l & 1))
        table[0] = jnp.sum(jnp.where(bx == (l64 >> 4), t0, 0.0), axis=0)
        t1_ = pick(j == 6 * (l >> 4) + 2 + (l & 1))
        table[1, 0:4, :] = jnp.sum(jnp.where(by == ((bl >> 1) & 7), t1_, 0.0), axis=1)
        for zz in range(8):
            t2_ = pick(j == 6 * zz + 4 + (l & 1))
            kept = jnp.where((bx == (l64 >> 4)) & (by == ((bl >> 1) & 7)), t2_, 0.0)
            table[2, zz : zz + 1, :] = jnp.sum(jnp.sum(kept, axis=0), axis=0, keepdims=True)
        for copy in ship:
            copy.wait()

    at = (lambda off: turned(y, off, 8), lambda off: turned(x, off, 4), lambda off: turned(z, off, 8))
    nt = (((1,), (1,)), ((), ()))

    def weights(blocks, m):
        columns = []
        for cb in range(8):
            pieces = []
            for k, off in blocks:
                if k == 0:
                    pieces.append(g0[at[0](off), :, cb, m].reshape(64, 128))
                elif k == 1:
                    pieces.append(g1[at[1](off), :, cb, m].reshape(128, 128))
                else:
                    pieces.append(g2[at[2](off), cb, :, m].reshape(64, 128))
            columns.append(jnp.concatenate(pieces, axis=0))
        return jnp.concatenate(columns, axis=1)

    def bias_row(blocks):
        out, pend = [], None
        for k, off in blocks:
            value = table[k, pl.ds(at[k](off), 1), :]
            if k == 1:
                out.append(value)
            elif pend is None:
                pend = value
            else:
                out.append(jnp.where(lane < 64, pend, value))
                pend = None
        return jnp.concatenate(out, axis=1)

    def front(blocks, a_in, a_out):
        pre = lax.dot_general(a_in, weights(blocks, 0), nt, preferred_element_type=F32) + bias_row(blocks)
        back = lax.dot_general(a_out, weights(blocks, 1), nt, preferred_element_type=F32)
        cdf = 0.5 * (1.0 + lax.erf(pre * 0.7071067811865476))
        slope = cdf + pre * jnp.exp(-0.5 * pre * pre) * 0.3989422804014327
        return (pre * cdf).astype(BF16), (back * slope).astype(BF16)

    def chunk_front(n):
        hidden, back_pre = front(CHUNKS[n], act[0].reshape(256, 1024), act[1].reshape(256, 1024))
        hid[0], hid[1] = hidden, back_pre

    def chunk_back(n):
        for m in range(2):
            value = jnp.dot(hid[m], weights(CHUNKS[n], 1 - m), preferred_element_type=F32).reshape(2, 128, 1024)
            for cb in range(8):
                piece = value[:, :, 128 * cb : 128 * cb + 128]
                acc[m, :, cb] = piece if n == 0 else acc[m, :, cb] + piece

    tasks = [(0.7, None, functools.partial(conv_piece, i)) for i in range(4)]
    tasks += [(1.0, None, norm), (0.8, None, biases)]
    for n in range(LAST):
        tasks.append((1.2, CHUNKS[n], functools.partial(chunk_front, n)))
        tasks.append((1.0, CHUNKS[n], functools.partial(chunk_back, n)))
    params()
    borders()
    for k in range(3):
        for copy in first[k]:
            copy.wait()
        for way in (0, 1):
            go(outer[k].copy(way, 1, 0))
            for j in range(2):
                go(inner[k].copy(way, 1, j))
    events = plan(outer, inner)

    def needs(event, blocks):
        _, k, level, way, s, j = event
        if blocks is None:
            return False
        for kk, off in blocks:
            if kk != k:
                continue
            if off == 0 and level == 0:
                return True
            if off != 0 and level == 1 and (abs(off) == s) and (s == outer[k].n // 2 or (off < 0) == (way == 0)):
                return True
        return False

    clock = 0.0
    while events or tasks:
        ready = bool(tasks) and not any(needs(e, tasks[0][1]) for e in events)
        if events and (events[0][0] <= clock or not ready):
            event = events.pop(0)
            clock = max(clock, event[0])
            arrive(*event[1:])
        else:
            length, _, piece = tasks.pop(0)
            piece()
            clock += length

    blocks = CHUNKS[LAST]
    swap = [remote(mypart.at[a], part.at[a], es.at[a], er.at[a], sibling) for a in range(2)]
    for turn, who in enumerate((1 - core, core)):
        for m, h in enumerate(front(blocks, act[0, who], act[1, who])):
            hid[m, 0:128, :] = h
        for m in range(2):
            value = jnp.dot(hid[m, 0:128, :], weights(blocks, 1 - m), preferred_element_type=F32)
            for cb in range(8):
                piece = acc[m, who, cb] + value[:, 128 * cb : 128 * cb + 128]
                if turn == 0:
                    mypart[m, cb] = piece.astype(BF16)
                else:
                    acc[m, core, cb] = piece
            if turn == 0:
                swap[m].start()
    for copy in swap:
        copy.wait_recv()

    sums[:, 48:64, :] = jnp.zeros((8, 16, 128), F32)

    def down(value):
        return jnp.sum(value, axis=0, keepdims=True)

    def ending(cb, carry):
        one, two = carry
        standard = conv[cb]
        upstream = cb_[cb].astype(F32)
        projected = acc[0, core, cb] + part[0, cb].astype(F32) + taps[cb, 53:54, :]
        normed = acc[1, core, cb] + part[1, cb].astype(F32)
        source = fb[cb].astype(F32).reshape(128, 128)
        ob[0, cb] = (source + taps[cb, 52:53, :] * projected).astype(BF16)
        sums[cb, 50:51, :] = down(normed * standard)
        sums[cb, 51:52, :] = down(normed)
        sums[cb, 52:53, :] = down(upstream * projected)
        scaled = normed * taps[cb, 50:51, :]
        bc[cb] = scaled
        return one + scaled, two + scaled * standard

    none = jnp.zeros((128, 128), F32)
    one, two = lax.fori_loop(0, 8, ending, (none, none))
    mean_one = jnp.sum(one, axis=-1, keepdims=True) * (1.0 / 1024)
    mean_two = jnp.sum(two, axis=-1, keepdims=True) * (1.0 / 1024)
    halo2 = Halo(wire, ecol, ecor, wrows, wcols, wcors, h2s, h2r)
    inverse = inv[...]

    def rear(cb):
        back = inverse * (bc[cb] - mean_one - conv[cb] * mean_two)
        bc[cb] = back
        sums[cb, 49:50, :] = down(back)
        back = back.reshape(8, 16, 128)
        wire[cb] = back.astype(BF16)
        halo2.cut(cb, back, stage)

    each(8, rear)
    halo2.start()
    puts = []
    for cb in range(8):
        puts.append(pltpu.make_async_copy(ob.at[0, cb], block_out.at[:, pl.ds(128 * cb, 128)], os_.at[0, cb]))
        puts[-1].start()

    def block_grad(cb):
        back = bc[cb].reshape(8, 16, 128)
        for b in range(KS):
            window = pad[cb, :, 5 + b : 21 + b, :]
            for a in range(KS):
                product = jnp.sum(back * window[a : a + 8], axis=0)
                sums[cb, a * KS + b : a * KS + b + 1, :] = down(product)

    def firsts(k):
        other = lax.rem(mine + k, 8)
        peer = device(lax.rem(other, 2) * 2 + xl, yh * 4 + lax.div(other, 2), z, core)
        return other, remote(sums.at[other], r1.at[mine], s1.at[k - 1], t1.at[k - 1], peer)

    def grad_step(i):
        other, copy = firsts(i + 1)
        block_grad(other)
        copy.start()

    each(7, grad_step)
    block_grad(mine)
    r1[mine] = sums[mine]
    halo2.finish()

    def conv_back(low_, count):
        def one(i):
            cb = i + low_
            halo2.fill(cb, bpad)
            start = cb_[cb].astype(F32).reshape(8, 16, 128)
            ob[1, cb] = block_conv(start, bpad, taps, cb, True).reshape(128, 128).astype(BF16)

        each(count, one)
        for cb in range(low_, low_ + count):
            puts.append(pltpu.make_async_copy(ob.at[1, cb], grad_in.at[:, pl.ds(128 * cb, 128)], os_.at[1, cb]))
            puts[-1].start()

    conv_back(0, 2)
    for k in range(1, 8):
        firsts(k)[1].wait()
    mid[...] = jnp.sum(r1[...], axis=0).reshape(8, 8, 128)
    c2 = [remote(mid.at[turned(z, k + 1, 8)], r2.at[z], s2.at[k], t2.at[k], zps[k]) for k in range(7)]
    for copy in c2:
        copy.start()
    r2[z] = mid[z]
    conv_back(2, 3)
    for copy in c2:
        copy.wait()
    low[...] = jnp.sum(r2[...], axis=0)
    c3 = [remote(low, r3.at[member], s3.at[k], t3.at[k], thirds[k]) for k in range(7)]
    for copy in c3:
        copy.start()
    r3[member] = low[...]
    conv_back(5, 3)
    for copy in c3:
        copy.wait()
    fin[...] = jnp.sum(r3[...], axis=0)
    c4 = [remote(fin, tot.at[z], s4.at[k], t4.at[k], zps[k]) for k in range(7)]
    for copy in c4:
        copy.start()
    tot[z] = fin[...]
    for copy in started + swap:
        copy.wait_send()
    for copy in puts:
        copy.wait()
    for copy in c4:
        copy.wait()
    final = tot[...].reshape(64, 128) * (1.0 / 256.0)
    final = jnp.where(xl == 0, final, pltpu.roll(final, 64, 1))
    out_kernel[...] = final[0:49, 0:64]
    out_vec[...] = final[48:56, 0:64]


def whole(field, cot, wt, par, bia):
    cell = (2, 16, 128)
    any_ = pl.BlockSpec(memory_space=pl.ANY)
    scratch = [
        ((8, 8, 16, 128), BF16), ((8, 128, 128), BF16), ((2, 8, 24, 128), BF16), ((4, 8, 16, 128), BF16), ((112, 128), F32),
        ((2, 8, 3, 16, 128), BF16), ((2, 8, 24, 128), BF16), ((4, 8, 16, 128), BF16),
        ((2, 8, 3, 16, 128), BF16), ((2, 8, 24, 128), BF16), ((4, 8, 16, 128), BF16),
        ((8, 14, 32, 128), F32), ((8, 14, 32, 128), F32), ((16, 28, 128), F32), ((8, 56, 128), F32),
        ((1, 128), F32), ((8, 1, 128), F32), ((32, 1, 128), F32), ((3, 8, 128), F32),
        ((8, 16, 128), BF16), ((8, 16, 128), BF16), ((3, 2, 16, 128), F32),
        ((8, 4, 8) + cell, BF16), ((4, 8, 8) + cell, BF16), ((8, 8, 4) + cell, BF16),
        ((2, 2, 128, 1024), BF16), ((2, 256, 256), BF16), ((2, 2, 8, 128, 128), F32),
        ((2, 8, 128, 128), BF16), ((2, 8, 128, 128), BF16), ((8, 128, 128), F32), ((128, 128), F32),
        ((8, 128, 128), F32), ((8, 8, 16, 128), BF16), ((2, 8, 128, 128), BF16), ((8, 64, 128), F32),
        ((8, 64, 128), F32), ((8, 8, 128), F32), ((8, 8, 128), F32), ((8, 8, 128), F32), ((8, 128), F32), ((8, 128), F32),
        ((8, 8, 128), F32),
    ]
    sems = [(2, 8), (8,), (8,), (8,), (8,), (15,), (15,), (7,), (7,), (31,), (31,), (2,), (2,), (2, 7), (2, 7), (3, 7), (3, 7)]
    sems += [(2, 3), (2, 3), (2, 7), (2, 7), (2, 7), (2, 7), (2, 14), (2, 14), (2, 12), (2, 12), (2, 28), (2, 28), (2,), (2,)]
    sems += [(7,)] * 8 + [(2, 8)]
    return pl.pallas_call(
        whole_body,
        out_shape=(
            jax.ShapeDtypeStruct((128, 1024), BF16),
            jax.ShapeDtypeStruct((128, 1024), BF16),
            jax.ShapeDtypeStruct((49, 64), F32),
            jax.ShapeDtypeStruct((8, 64), F32),
        ),
        in_specs=[any_, any_, VMEM, VMEM, VMEM],
        out_specs=[any_, any_, VMEM, VMEM],
        scratch_shapes=[pltpu.VMEM(*s) for s in scratch] + [DMA(s) for s in sems],
        compiler_params=pltpu.CompilerParams(
            collective_id=0, has_side_effects=True, vmem_limit_bytes=56 * 1024 * 1024
        ),
        name="whole",
    )(field, cot, wt, par, bia)


def per_device(
    features,
    cotangent,
    in_weight,
    out_weight,
    hidden_bias,
    kernel,
    conv_bias,
    norm_gain,
    norm_bias,
    layer_scale,
    out_bias,
):
    _, _, rows, cols, width = features.shape
    field = features.reshape(rows, cols, width)
    cot = cotangent.reshape(rows * cols, width)
    slab = jnp.concatenate(
        [kernel] + [v[None] for v in (conv_bias, norm_gain, norm_bias, layer_scale, out_bias)] + [jnp.zeros((2, 64), F32)]
    )
    par = jnp.concatenate([slab[:28], slab[28:]], axis=1)
    bia = jnp.pad(hidden_bias.astype(F32)[None], ((0, 0), (0, 122)))
    both = jnp.concatenate([in_weight, out_weight, jnp.zeros((4, width), BF16)])
    wt = both.reshape(16, 8, 128).transpose(1, 0, 2)
    block_out, grad_in, out_kernel, out_vec = whole(field, cot, wt, par, bia)
    return (
        block_out.reshape(features.shape),
        grad_in.reshape(features.shape),
        out_kernel,
        out_vec[1],
        out_vec[2],
        out_vec[3],
        out_vec[4],
    )


def solution(mesh):
    placed = (
        P("dp", "tile", None, None, None),
        P("dp", "tile", None, None, None),
        P(("dp", "tile"), None),
        P(("dp", "tile"), None),
        P(("dp", "tile")),
        P(None, "dp"),
        P("dp"),
        P("dp"),
        P("dp"),
        P("dp"),
        P("dp"),
    )
    return jax.shard_map(
        per_device,
        mesh=mesh,
        in_specs=placed,
        out_specs=(
            P("dp", "tile", None, None, None),
            P("dp", "tile", None, None, None),
            P(None, "dp"),
            P("dp"),
            P("dp"),
            P("dp"),
            P("dp"),
        ),
        check_vma=False,
    )
```

```python
import functools

import jax
import jax.numpy as jnp
from jax import lax
from jax.experimental import pallas as pl
from jax.experimental.pallas import tpu as pltpu
from jax.sharding import PartitionSpec as P

KS = 7
GX = 4
NX, NY, NZ = 4, 8, 8
MESH = pl.DeviceIdType.MESH
VMEM = pl.BlockSpec(memory_space=pltpu.VMEM)
F32 = jnp.float32
BF16 = jnp.bfloat16
DMA = pltpu.SemaphoreType.DMA


def place():
    dp = lax.axis_index("dp")
    tile = lax.axis_index("tile")
    x = lax.rem(dp, 4)
    y = lax.div(tile, 16) * 4 + lax.div(dp, 4)
    z = lax.rem(lax.div(tile, 2), 8)
    core = lax.rem(tile, 2)
    return x, y, z, core


def device(x, y, z, core):
    return (lax.rem(y, 4) * 4 + x, lax.div(y, 4) * 16 + z * 2 + core)


def turned(index, by, size):
    return lax.rem(index + (by % size), size)


def greet(barrier, peer):
    pl.semaphore_signal(barrier, inc=1, device_id=peer, device_id_type=MESH)


def remote(src, dst, ssem, rsem, peer):
    return pltpu.make_async_remote_copy(
        src_ref=src, dst_ref=dst, send_sem=ssem, recv_sem=rsem, device_id=peer, device_id_type=MESH
    )


STEPS = [(-1, 0), (1, 0), (0, -1), (0, 1), (-1, -1), (-1, 1), (1, -1), (1, 1)]


def halo_sides():
    dp = lax.axis_index("dp")
    tile = lax.axis_index("tile")
    ty = lax.div(tile, GX)
    tx = lax.rem(tile, GX)
    sides = []
    for dr, dc in STEPS:
        there = None
        for ok in ([ty >= 1] if dr < 0 else [ty <= 6] if dr > 0 else []) + (
            [tx >= 1] if dc < 0 else [tx <= 2] if dc > 0 else []
        ):
            there = ok if there is None else there & ok
        sides.append((there, (dp, tile + dr * GX + dc)))
    return sides


OFF4 = [0, -1, 1, 2]
OFF8 = [0, -1, 1, -2, 2, -3, 3, 4]


def ring_slots(n, count):
    half = n // 2
    right = [(s, j) for s in range(1, half) for j in range(count)] + [(half, j) for j in range(count // 2)]
    left = [(s, j) for s in range(1, half) for j in range(count)] + [(half, j) for j in range(count // 2, count)]
    return right, left


class Ring:
    def __init__(self, n, count, offs, sub, peers, ssem, rsem, wire):
        self.n, self.count, self.offs, self.sub, self.peers = n, count, offs, sub, peers
        self.ssem, self.rsem, self.wire = ssem, rsem, wire
        self.slots = ring_slots(n, count)

    def copy(self, way, s, j):
        i = self.slots[way].index((s, j))
        ref = self.sub(-(s - 1) if way == 0 else (s - 1), j)
        return remote(ref, ref, self.ssem, self.rsem.at[way, i], self.peers[way])

    def landed(self, way, s, j):
        i = self.slots[way].index((s, j))
        ref = self.sub(-s if way == 0 else s, j)
        return pltpu.make_async_copy(ref, ref, self.rsem.at[way, i])


def plan(outer, inner):
    events = []
    latency = 1.7
    for c, (o, i) in enumerate(zip(outer, inner)):
        ready = {0: 0.0}
        for way in (0, 1):
            t, got = 0.0, {}
            for s, j in i.slots[way]:
                t = max(t, 0.0 if s == 1 else got[s - 1, j]) + i.wire
                got[s, j] = t + latency
                events.append((got[s, j], c, 0, way, s, j))
        for way in (0, 1):
            for s, j in i.slots[way]:
                pass
        half = i.n // 2
        seen = {(e[3], e[4], e[5]): e[0] for e in events if e[1] == c and e[2] == 0}
        for k, off in enumerate(o.offs):
            if off == 0:
                continue
            if abs(off) == half:
                ready[k] = max(v for (w, s, j), v in seen.items() if s == half)
            else:
                ready[k] = max(v for (w, s, j), v in seen.items() if s == abs(off) and w == (0 if off < 0 else 1))
        for way in (0, 1):
            t, got = 0.0, {}
            for s, j in o.slots[way]:
                t = max(t, ready[j] if s == 1 else got[s - 1, j]) + o.wire
                got[s, j] = t + latency
                events.append((got[s, j], c, 1, way, s, j))
    return sorted(events)


def halo_count():
    count = 0
    for there, _ in halo_sides():
        count = count + there.astype(jnp.int32)
    return count


BACK = [1, 0, 3, 2, 7, 6, 5, 4]


class Halo:
    def __init__(self, grid, ecol, ecor, rows, cols, cors, ssem, rsem):
        self.grid, self.ecol, self.ecor = grid, ecol, ecor
        self.rows, self.cols, self.cors = rows, cols, cors
        src = [grid.at[:, 0:3], grid.at[:, 5:8], ecol.at[0], ecol.at[1]] + [ecor.at[k] for k in range(4)]
        self.dst = [rows.at[1], rows.at[0], cols.at[1], cols.at[0], cors.at[3], cors.at[2], cors.at[1], cors.at[0]]
        self.rsem = rsem
        self.moves = []
        for k, (there, peer) in enumerate(halo_sides()):
            self.moves.append((there, remote(src[k], self.dst[k], ssem.at[k], rsem.at[BACK[k]], peer)))

    def start(self):
        for there, copy in self.moves:
            @pl.when(there)
            def _():
                copy.start()

    def finish(self):
        for k, (there, copy) in enumerate(self.moves):
            landed = self.dst[BACK[k]]
            @pl.when(there)
            def _():
                pltpu.make_async_copy(landed, landed, self.rsem.at[k]).wait()
                copy.wait_send()

            @pl.when(jnp.logical_not(there))
            def _():
                landed[...] = jnp.zeros(landed.shape, landed.dtype)

    def cut(self, cb, value, stage):
        for i in range(8):
            stage[3 * i : 3 * i + 3, :] = value[i, 0:3, :]
            stage[24 + 3 * i : 27 + 3 * i, :] = value[i, 13:16, :]
        for k, (r, c) in enumerate(((0, 0), (0, 13), (5, 0), (5, 13))):
            for i in range(3):
                at = 48 + 16 * k + 3 * i
                stage[at : at + 3, :] = value[r + i, c : c + 3, :]
        self.ecol[0, cb] = stage[0:24, :].astype(BF16)
        self.ecol[1, cb] = stage[24:48, :].astype(BF16)
        for k in range(4):
            self.ecor[k, cb] = stage[48 + 16 * k : 64 + 16 * k, :].astype(BF16)

    def fill(self, cb, pad):
        pad[cb, 3:11, 8:24, :] = self.grid[cb].astype(F32)
        pad[cb, 0:3, 8:24, :] = self.rows[0, cb].astype(F32)
        pad[cb, 11:14, 8:24, :] = self.rows[1, cb].astype(F32)
        for side, col in ((0, 5), (1, 24)):
            value = self.cols[side, cb].astype(F32)
            for i in range(8):
                pad[cb, 3 + i, col : col + 3, :] = value[3 * i : 3 * i + 3, :]
        for k, (row, col) in enumerate(((0, 5), (0, 24), (11, 5), (11, 24))):
            value = self.cors[k, cb].astype(F32)
            for i in range(3):
                pad[cb, row + i, col : col + 3, :] = value[3 * i : 3 * i + 3, :]


def each(count, body):
    def step(i, carry):
        body(i)
        return carry

    lax.fori_loop(0, count, step, 0)


def block_conv(start, pad, taps, cb, flip):
    total = start
    for b in range(KS):
        window = pad[cb, :, 5 + b : 21 + b, :]
        for a in range(KS):
            tap = (6 - a) * KS + (6 - b) if flip else a * KS + b
            total = total + taps[cb, tap : tap + 1, :][None] * window[a : a + 8]
    return total


LAST = 5
CHUNKS = [
    [(0, 0), (2, 0), (1, 0)],
    [(0, -1), (0, 1), (2, -1), (2, 1)],
    [(1, -1), (1, 1)],
    [(0, -2), (0, 2), (2, -2), (2, 2)],
    [(0, -3), (0, 3), (2, -3), (2, 3)],
    [(0, 4), (2, 4), (1, 2)],
]


def whole_body(
    field, cot, w_in, w_out, hbias, taps_in, v0, v1, v2, v3, v4,
    block_out, grad_in, out_sums,
    fb, cb_, raw, rawz, rawy, slab, par, bia, ecol, ecor, stage, hrows, hcols, hcors, wrows, wcols, wcors, pad, bpad, pars, taps, row, zbias, bias, table,
    rz, ry, g0, g1, g2, act, hid, acc, part, mypart, conv, inv, bc, wire, ob, sums,
    r1, r2, r3, mid, low, fin, tot,
    ls, hs, hr, h2r, ps, zs, bs, as_, ar, fs, q0r, q1r, q2r, r0r, r1r, r2r, rs, es, er, ts, os_,
):
    x, y, z, core = place()
    dp = lax.axis_index("dp")
    tile = lax.axis_index("tile")
    yl, yh = lax.rem(y, 4), lax.div(y, 4)
    xl, xh = lax.rem(x, 2), lax.div(x, 2)
    lane = lax.broadcasted_iota(jnp.int32, (1, 128), 1)
    barrier = pltpu.get_barrier_semaphore()
    sibling = device(x, y, z, 1 - core)
    xps = [device(turned(x, k, NX), y, z, core) for k in range(1, NX)]
    yps = [device(x, turned(y, k, NY), z, core) for k in range(1, NY)]
    zps = [device(x, y, turned(z, k, NZ), core) for k in range(1, NZ)]
    dps = [(turned(dp, k, 16), tile) for k in range(1, 16)]
    xys = [device(turned(x, k % 4, NX), turned(y, k // 4, NY), z, core) for k in range(1, 32)]
    mine = yl * 2 + xh
    member = yh * 4 + xl * 2 + core
    thirds = []
    for k in range(1, 8):
        o = turned(member, k, 8)
        thirds.append(device(xh * 2 + lax.rem(lax.div(o, 2), 2), lax.div(o, 4) * 4 + yl, z, lax.rem(o, 2)))
    for peer in xys + zps + thirds[0::2]:
        greet(barrier, peer)
    for there, peer in halo_sides():
        @pl.when(there)
        def _():
            greet(barrier, peer)

    for cb in range(8):
        lanes = pl.ds(128 * cb, 128)
        pltpu.make_async_copy(field.at[:, :, lanes], fb.at[cb], ls.at[0]).start()
        pltpu.make_async_copy(cot.at[:, lanes], cb_.at[cb], ls.at[1]).start()

    def settle(ref, sem):
        pltpu.make_async_copy(ref, ref, sem).wait()

    rows_in, rows_out = w_in[...].astype(F32), w_out[...].astype(F32)
    raw[0, 0:4, :], raw[0, 4:8, :] = rows_in[0:4], rows_out[0:4]
    raw[1, 0:2, :], raw[1, 2:4, :] = rows_in[4:6], rows_out[4:6]
    raw[1, 4:8, :] = jnp.zeros((4, 1024), F32)
    rawz[...] = raw[0].astype(BF16)
    rawy[...] = raw[1].astype(BF16)
    bia[...] = jnp.zeros((1, 128), F32)
    bia[:, 0:6] = hbias[...].astype(F32)
    slab[...] = jnp.zeros_like(slab)
    slab[0:49, 0:64] = taps_in[...]
    for k, v in enumerate((v0, v1, v2, v3, v4)):
        slab[49 + k : 50 + k, 0:64] = v[...]
    par[...] = jnp.where(lane < 64, slab[0:28, :], pltpu.roll(slab[28:56, :], 64, 1))
    stage[...] = jnp.zeros_like(stage)
    halo1 = Halo(fb, ecol, ecor, hrows, hcols, hcors, hs, hr)
    pl.semaphore_wait(barrier, 31 + 7 + 4 + halo_count())

    for peer in zps:
        remote(rawz, rz.at[z], fs.at[0], fs.at[1], peer).start()
    for peer in yps:
        remote(rawy, ry.at[y], fs.at[2], fs.at[3], peer).start()
    for peer in zps:
        remote(bia, zbias.at[z], zs.at[0], zs.at[1], peer).start()
    settle(fb, ls.at[0])
    settle(cb_, ls.at[1])
    each(8, lambda cb: halo1.cut(cb, fb[cb].astype(F32), stage))
    halo1.start()
    for peer in dps:
        remote(par, pars.at[dp], ps.at[0], ps.at[1], peer).start()
    rz[z] = rawz[...]
    ry[y] = rawy[...]
    zbias[z] = bia[...]
    pars[dp] = par[...]

    to = lax.broadcasted_iota(jnp.int32, (32, 64), 0)
    fro = lax.broadcasted_iota(jnp.int32, (32, 64), 1)

    def tiles(got, first_row, step):
        chosen = fro == ((to >> 1) & 7) * 8 + (to >> 4) * step + first_row + (to & 1)
        rows = jnp.concatenate([got[d].astype(F32) for d in range(8)], axis=0).astype(BF16)
        made = jnp.dot(jnp.where(chosen, 1.0, 0.0).astype(BF16), rows, preferred_element_type=F32)
        return made.astype(BF16)

    def put(home, made):
        for cb in range(8):
            for m in range(2):
                home[cb, m] = made[16 * m : 16 * m + 16, 128 * cb : 128 * cb + 128]

    xr, xb = xps[0], xps[-1]
    yr, yb = yps[0], yps[-1]
    zr_, zb = zps[0], zps[-1]
    inner = [
        Ring(4, 2, OFF4, lambda b, j: g0.at[y, turned(x, b, 4), pl.ds(4 * j, 4)], (xr, xb), rs.at[0], q0r, 0.7),
        Ring(8, 2, OFF8, lambda b, j: g1.at[x, turned(y, b, 8), pl.ds(4 * j, 4)], (yr, yb), rs.at[1], q1r, 0.7),
        Ring(4, 2, OFF4, lambda b, j: g2.at[z, turned(x, b, 4), pl.ds(4 * j, 4)], (xr, xb), rs.at[2], q2r, 0.7),
    ]
    outer = [
        Ring(8, 4, OFF4, lambda b, j: g0.at[turned(y, b, 8), turned(x, OFF4[j], 4)], (yr, yb), rs.at[3], r0r, 1.4),
        Ring(4, 8, OFF8, lambda b, j: g1.at[turned(x, b, 4), turned(y, OFF8[j], 8)], (xr, xb), rs.at[4], r1r, 1.4),
        Ring(8, 4, OFF4, lambda b, j: g2.at[turned(z, b, 8), turned(x, OFF4[j], 4)], (zr_, zb), rs.at[5], r2r, 1.4),
    ]
    def go(copy):
        copy.start()

    def arrive(k, level, way, s, j):
        ring = (inner, outer)[level][k]
        ring.landed(way, s, j).wait()
        if (s + 1, j) in ring.slots[way]:
            go(ring.copy(way, s + 1, j))
        half = ring.n // 2
        if level == 0 and j == (1 if s < half else way) and not (s == half and way == 0):
            index = ring.offs.index(half if s == half else -s if way == 0 else s)
            for w in (0, 1):
                if (1, index) in outer[k].slots[w]:
                    go(outer[k].copy(w, 1, index))

    ship = [remote(act.at[a, core], act.at[a, core], as_.at[a], ar.at[a], sibling) for a in range(2)]

    def bias_push():
        settle(zbias.at[0:7], zs.at[0])
        settle(zbias.at[0:7], zs.at[1])
        total = zbias[0]
        for k in range(1, NZ):
            total = total + pltpu.roll(zbias[k], 6 * k, 1)
        row[...] = total
        me = x * 8 + y
        bias[me] = total
        for peer in xys:
            remote(row, bias.at[me], bs.at[0], bs.at[1], peer).start()

    def params():
        settle(pars.at[0:15], ps.at[0])
        settle(pars.at[0:15], ps.at[1])

        def unpack(cb):
            one, two = pars[2 * cb], pars[2 * cb + 1]
            taps[cb, 0:28, :] = jnp.where(lane < 64, one, pltpu.roll(two, 64, 1))
            taps[cb, 28:56, :] = jnp.where(lane < 64, pltpu.roll(one, 64, 1), two)

        each(8, unpack)
        for cb in range(8):
            scaled = cb_[cb].astype(F32) * taps[cb, 52:53, :]
            act[1, core, :, 128 * cb : 128 * cb + 128] = scaled.astype(BF16)

    def borders():
        ship[1].start()
        halo1.finish()
        each(8, lambda cb: halo1.fill(cb, pad))

    def conv_piece(part_number):
        def one(i):
            cb = i + 2 * part_number
            start = jnp.broadcast_to(taps[cb, 49:50, :][None], (8, 16, 128))
            conv[cb] = block_conv(start, pad, taps, cb, False).reshape(128, 128)

        each(2, one)

    def norm():
        mean = jnp.sum(sum(conv[cb] for cb in range(8)), axis=-1, keepdims=True) * (1.0 / 1024)
        square = jnp.zeros((128, 128), F32)
        for cb in range(8):
            centered = conv[cb] - mean
            square = square + centered * centered
        inverse = lax.rsqrt(jnp.sum(square, axis=-1, keepdims=True) * (1.0 / 1024) + 1e-06)
        inv[...] = jnp.broadcast_to(inverse, (128, 128))
        for cb in range(8):
            standard = (conv[cb] - mean) * inverse
            conv[cb] = standard
            normed = standard * taps[cb, 50:51, :] + taps[cb, 51:52, :]
            act[0, core, :, 128 * cb : 128 * cb + 128] = normed.astype(BF16)

    def biases():
        ship[0].start()
        settle(bias.at[0:31], bs.at[0])
        settle(bias.at[0:31], bs.at[1])
        values = bias[...].reshape(32, 128).astype(BF16)
        j = lax.broadcasted_iota(jnp.int32, (128, 128), 0)
        l = lax.broadcasted_iota(jnp.int32, (128, 128), 1)
        bx = lax.broadcasted_iota(jnp.int32, (4, 8, 128), 0)
        by = lax.broadcasted_iota(jnp.int32, (4, 8, 128), 1)
        bl = lax.broadcasted_iota(jnp.int32, (4, 8, 128), 2)
        l64 = bl & 63

        def pick(where):
            chosen = jnp.where(where, 1.0, 0.0).astype(BF16)
            return jnp.dot(values, chosen, preferred_element_type=F32).reshape(4, 8, 128)

        t0 = pick(j == 6 * ((l >> 1) & 7) + (l & 1))
        table[0] = jnp.sum(jnp.where(bx == (l64 >> 4), t0, 0.0), axis=0)
        t1_ = pick(j == 6 * ((l >> 1) & 7) + 2 + (l & 1))
        table[1, 0:4, :] = jnp.sum(jnp.where(by == (bl >> 4), t1_, 0.0), axis=1)
        for zz in range(8):
            t2_ = pick(j == 6 * zz + 4 + (l & 1))
            kept = jnp.where((bx == (l64 >> 4)) & (by == ((bl >> 1) & 7)), t2_, 0.0)
            table[2, zz : zz + 1, :] = jnp.sum(jnp.sum(kept, axis=0), axis=0, keepdims=True)
        for copy in ship:
            copy.wait()

    at = (lambda off: turned(y, off, 8), lambda off: turned(x, off, 4), lambda off: turned(z, off, 8))
    nt = (((1,), (1,)), ((), ()))

    def weights(blocks, m):
        columns = []
        for cb in range(8):
            pieces = []
            for k, off in blocks:
                if k == 0:
                    pieces.append(g0[at[0](off), :, cb, m].reshape(64, 128))
                elif k == 1:
                    pieces.append(g1[at[1](off), :, cb, m].reshape(128, 128))
                else:
                    pieces.append(g2[at[2](off), :, cb, m].reshape(64, 128))
            columns.append(jnp.concatenate(pieces, axis=0))
        return jnp.concatenate(columns, axis=1)

    def bias_row(blocks):
        out, pend = [], None
        for k, off in blocks:
            value = table[k, pl.ds(at[k](off), 1), :]
            if k == 1:
                out.append(value)
            elif pend is None:
                pend = value
            else:
                out.append(jnp.where(lane < 64, pend, value))
                pend = None
        return jnp.concatenate(out, axis=1)

    def front(blocks, a_in, a_out):
        pre = lax.dot_general(a_in, weights(blocks, 0), nt, preferred_element_type=F32) + bias_row(blocks)
        back = lax.dot_general(a_out, weights(blocks, 1), nt, preferred_element_type=F32)
        cdf = 0.5 * (1.0 + lax.erf(pre * 0.7071067811865476))
        slope = cdf + pre * jnp.exp(-0.5 * pre * pre) * 0.3989422804014327
        return (pre * cdf).astype(BF16), (back * slope).astype(BF16)

    def chunk_front(n):
        hidden, back_pre = front(CHUNKS[n], act[0].reshape(256, 1024), act[1].reshape(256, 1024))
        hid[0], hid[1] = hidden, back_pre

    def chunk_back(n):
        for m in range(2):
            value = jnp.dot(hid[m], weights(CHUNKS[n], 1 - m), preferred_element_type=F32).reshape(2, 128, 1024)
            for cb in range(8):
                piece = value[:, :, 128 * cb : 128 * cb + 128]
                acc[m, :, cb] = piece if n == 0 else acc[m, :, cb] + piece

    tasks = [(0.3, 0.5, None, bias_push), (0.6, 1.5, None, params), (1.2, 2.5, None, borders)]
    tasks += [(0.6, 0.0, None, functools.partial(conv_piece, i)) for i in range(4)]
    tasks += [(0.8, 0.0, None, norm), (0.6, 0.0, None, biases)]
    for n in range(LAST):
        tasks.append((1.0, 0.0, CHUNKS[n], functools.partial(chunk_front, n)))
        tasks.append((0.8, 0.0, CHUNKS[n], functools.partial(chunk_back, n)))
    home = (g0.at[y, x], g1.at[x, y], g2.at[z, x])
    for k, (got, first_row, step) in enumerate(((rz, 0, 4), (rz, 2, 4), (ry, 0, 2))):
        if k != 1:
            settle((rz, ry)[k // 2].at[0:7], fs.at[k])
            settle((rz, ry)[k // 2].at[0:7], fs.at[k + 1])
        put(home[k], tiles(got, first_row, step))
        for way in (0, 1):
            go(outer[k].copy(way, 1, 0))
            for j in range(2):
                go(inner[k].copy(way, 1, j))
    events = plan(outer, inner)

    def needs(event, blocks):
        _, k, level, way, s, j = event
        if blocks is None:
            return False
        for kk, off in blocks:
            if kk != k:
                continue
            if off == 0 and level == 0:
                return True
            if off != 0 and level == 1 and (abs(off) == s) and (s == outer[k].n // 2 or (off < 0) == (way == 0)):
                return True
        return False

    clock = 0.0
    while events or tasks:
        ready = bool(tasks) and not any(needs(e, tasks[0][2]) for e in events)
        if events and (events[0][0] <= clock or not ready or clock < tasks[0][1]):
            event = events.pop(0)
            clock = max(clock, event[0])
            arrive(*event[1:])
        else:
            length, _, _, piece = tasks.pop(0)
            piece()
            clock += length

    blocks = CHUNKS[LAST]
    swap = [remote(mypart.at[a], part.at[a], es.at[a], er.at[a], sibling) for a in range(2)]
    for turn, who in enumerate((1 - core, core)):
        for m, h in enumerate(front(blocks, act[0, who], act[1, who])):
            hid[m, 0:128, :] = h
        for m in range(2):
            value = jnp.dot(hid[m, 0:128, :], weights(blocks, 1 - m), preferred_element_type=F32)
            for cb in range(8):
                piece = acc[m, who, cb] + value[:, 128 * cb : 128 * cb + 128]
                if turn == 0:
                    mypart[m, cb] = piece.astype(BF16)
                else:
                    acc[m, core, cb] = piece
            if turn == 0:
                swap[m].start()
    for copy in swap:
        copy.wait_recv()

    sums[:, 48:64, :] = jnp.zeros((8, 16, 128), F32)

    def down(value):
        return jnp.sum(value, axis=0, keepdims=True)

    def ending(cb, carry):
        one, two = carry
        standard = conv[cb]
        upstream = cb_[cb].astype(F32)
        projected = acc[0, core, cb] + part[0, cb].astype(F32) + taps[cb, 53:54, :]
        normed = acc[1, core, cb] + part[1, cb].astype(F32)
        source = fb[cb].astype(F32).reshape(128, 128)
        ob[0, cb] = (source + taps[cb, 52:53, :] * projected).astype(BF16)
        sums[cb, 50:51, :] = down(normed * standard)
        sums[cb, 51:52, :] = down(normed)
        sums[cb, 52:53, :] = down(upstream * projected)
        scaled = normed * taps[cb, 50:51, :]
        bc[cb] = scaled
        return one + scaled, two + scaled * standard

    none = jnp.zeros((128, 128), F32)
    one, two = lax.fori_loop(0, 8, ending, (none, none))
    mean_one = jnp.sum(one, axis=-1, keepdims=True) * (1.0 / 1024)
    mean_two = jnp.sum(two, axis=-1, keepdims=True) * (1.0 / 1024)
    halo2 = Halo(wire, ecol, ecor, wrows, wcols, wcors, hs, h2r)
    inverse = inv[...]

    def rear(cb):
        back = inverse * (bc[cb] - mean_one - conv[cb] * mean_two)
        bc[cb] = back
        sums[cb, 49:50, :] = down(back)
        back = back.reshape(8, 16, 128)
        wire[cb] = back.astype(BF16)
        halo2.cut(cb, back, stage)

    each(8, rear)
    halo2.start()
    for cb in range(8):
        pltpu.make_async_copy(ob.at[0, cb], block_out.at[:, pl.ds(128 * cb, 128)], os_.at[0]).start()

    def block_grad(cb):
        back = bc[cb].reshape(8, 16, 128)
        for b in range(KS):
            window = pad[cb, :, 5 + b : 21 + b, :]
            for a in range(KS):
                product = jnp.sum(back * window[a : a + 8], axis=0)
                sums[cb, a * KS + b : a * KS + b + 1, :] = down(product)

    def firsts(k):
        other = lax.rem(mine + k, 8)
        peer = device(lax.rem(other, 2) * 2 + xl, yh * 4 + lax.div(other, 2), z, core)
        return other, remote(sums.at[other], r1.at[mine], ts.at[0], ts.at[1], peer)

    def grad_step(i):
        other, copy = firsts(i + 1)
        block_grad(other)
        copy.start()

    each(7, grad_step)
    block_grad(mine)
    r1[mine] = sums[mine]
    halo2.finish()

    def conv_back(low_, count):
        def one(i):
            cb = i + low_
            halo2.fill(cb, bpad)
            start = cb_[cb].astype(F32).reshape(8, 16, 128)
            ob[1, cb] = block_conv(start, bpad, taps, cb, True).reshape(128, 128).astype(BF16)

        each(count, one)
        for cb in range(low_, low_ + count):
            pltpu.make_async_copy(ob.at[1, cb], grad_in.at[:, pl.ds(128 * cb, 128)], os_.at[1]).start()

    conv_back(0, 2)
    settle(r1.at[0:7], ts.at[0])
    settle(r1.at[0:7], ts.at[1])
    mid[...] = jnp.sum(r1[...], axis=0).reshape(8, 8, 128)
    for k in range(7):
        remote(mid.at[turned(z, k + 1, 8)], r2.at[z], ts.at[2], ts.at[3], zps[k]).start()
    r2[z] = mid[z]
    conv_back(2, 3)
    settle(r2.at[0:7], ts.at[3])
    low[...] = jnp.sum(r2[...], axis=0)
    for k in range(7):
        remote(low, r3.at[member], ts.at[4], ts.at[5], thirds[k]).start()
    r3[member] = low[...]
    conv_back(5, 3)
    settle(r3.at[0:7], ts.at[5])
    fin[...] = jnp.sum(r3[...], axis=0)
    for k in range(7):
        remote(fin, tot.at[z], ts.at[6], ts.at[7], zps[k]).start()
    tot[z] = fin[...]
    for k, ref in enumerate((g0.at[0, 0:3], g1.at[0, 0:7], g2.at[0, 0:3], g0.at[0:7], g1.at[0:3], g2.at[0:7])):
        settle(ref, rs.at[k])
    for copy in swap:
        copy.wait_send()
    settle(r2.at[0:7], ts.at[2])
    settle(r3.at[0:7], ts.at[4])
    settle(ob.at[0], os_.at[0])
    settle(ob.at[1], os_.at[1])
    settle(tot.at[0:7], ts.at[6])
    settle(tot.at[0:7], ts.at[7])
    final = tot[...].reshape(64, 128) * (1.0 / 256.0)
    final = jnp.where(xl == 0, final, pltpu.roll(final, 64, 1))
    out_sums[...] = final[0:56, 0:64]


def whole(*args):
    cell = (2, 16, 128)
    any_ = pl.BlockSpec(memory_space=pl.ANY)
    scratch = [
        ((8, 8, 16, 128), BF16), ((8, 128, 128), BF16), ((2, 8, 1024), F32), ((8, 1024), BF16), ((8, 1024), BF16),
        ((56, 128), F32), ((28, 128), F32), ((1, 128), F32), ((2, 8, 24, 128), BF16), ((4, 8, 16, 128), BF16), ((112, 128), F32),
        ((2, 8, 3, 16, 128), BF16), ((2, 8, 24, 128), BF16), ((4, 8, 16, 128), BF16),
        ((2, 8, 3, 16, 128), BF16), ((2, 8, 24, 128), BF16), ((4, 8, 16, 128), BF16),
        ((8, 14, 32, 128), F32), ((8, 14, 32, 128), F32), ((16, 28, 128), F32), ((8, 56, 128), F32),
        ((1, 128), F32), ((8, 1, 128), F32), ((32, 1, 128), F32), ((3, 8, 128), F32),
        ((8, 8, 1024), BF16), ((8, 8, 1024), BF16),
        ((8, 4, 8) + cell, BF16), ((4, 8, 8) + cell, BF16), ((8, 4, 8) + cell, BF16),
        ((2, 2, 128, 1024), BF16), ((2, 256, 256), BF16), ((2, 2, 8, 128, 128), F32),
        ((2, 8, 128, 128), BF16), ((2, 8, 128, 128), BF16), ((8, 128, 128), F32), ((128, 128), F32),
        ((8, 128, 128), F32), ((8, 8, 16, 128), BF16), ((2, 8, 128, 128), BF16), ((8, 64, 128), F32),
        ((8, 64, 128), F32), ((8, 8, 128), F32), ((8, 8, 128), F32), ((8, 8, 128), F32), ((8, 128), F32), ((8, 128), F32),
        ((8, 8, 128), F32),
    ]
    sems = [(2,), (8,), (8,), (8,), (2,), (2,), (2,), (2,), (2,), (4,), (2, 3), (2, 7), (2, 3), (2, 14), (2, 12), (2, 14)]
    sems += [(6,), (2,), (2,), (8,), (2,)]
    return pl.pallas_call(
        whole_body,
        out_shape=(
            jax.ShapeDtypeStruct((128, 1024), BF16),
            jax.ShapeDtypeStruct((128, 1024), BF16),
            jax.ShapeDtypeStruct((56, 64), F32),
        ),
        in_specs=[any_, any_] + [VMEM] * 9,
        out_specs=[any_, any_, VMEM],
        scratch_shapes=[pltpu.VMEM(*s) for s in scratch] + [DMA(s) for s in sems],
        compiler_params=pltpu.CompilerParams(
            collective_id=0, has_side_effects=True, vmem_limit_bytes=56 * 1024 * 1024
        ),
        name="whole",
    )(*args)


def per_device(
    features,
    cotangent,
    in_weight,
    out_weight,
    hidden_bias,
    kernel,
    conv_bias,
    norm_gain,
    norm_bias,
    layer_scale,
    out_bias,
):
    _, _, rows, cols, width = features.shape
    field = features.reshape(rows, cols, width)
    cot = cotangent.reshape(rows * cols, width)
    vectors = [v.reshape(1, -1) for v in (conv_bias, norm_gain, norm_bias, layer_scale, out_bias)]
    block_out, grad_in, sums = whole(field, cot, in_weight, out_weight, hidden_bias.reshape(1, -1), kernel, *vectors)
    return (
        block_out.reshape(features.shape),
        grad_in.reshape(features.shape),
        sums[0:49],
        sums[49],
        sums[50],
        sums[51],
        sums[52],
    )


def solution(mesh):
    placed = (
        P("dp", "tile", None, None, None),
        P("dp", "tile", None, None, None),
        P(("dp", "tile"), None),
        P(("dp", "tile"), None),
        P(("dp", "tile")),
        P(None, "dp"),
        P("dp"),
        P("dp"),
        P("dp"),
        P("dp"),
        P("dp"),
    )
    return jax.shard_map(
        per_device,
        mesh=mesh,
        in_specs=placed,
        out_specs=(
            P("dp", "tile", None, None, None),
            P("dp", "tile", None, None, None),
            P(None, "dp"),
            P("dp"),
            P("dp"),
            P("dp"),
            P("dp"),
        ),
        check_vma=False,
    )
```

```python
import functools
import heapq

import jax
import jax.numpy as jnp
from jax import lax
from jax.experimental import pallas as pl
from jax.experimental.pallas import tpu as pltpu
from jax.sharding import PartitionSpec as P

KS = 7
GX = 4
NX, NY, NZ = 4, 8, 8
MESH = pl.DeviceIdType.MESH
VMEM = pl.BlockSpec(memory_space=pltpu.VMEM)
F32 = jnp.float32
BF16 = jnp.bfloat16
DMA = pltpu.SemaphoreType.DMA


def place():
    dp = lax.axis_index("dp")
    tile = lax.axis_index("tile")
    x = lax.rem(dp, 4)
    y = lax.div(tile, 16) * 4 + lax.div(dp, 4)
    z = lax.rem(lax.div(tile, 2), 8)
    core = lax.rem(tile, 2)
    return x, y, z, core


def device(x, y, z, core):
    return (lax.rem(y, 4) * 4 + x, lax.div(y, 4) * 16 + z * 2 + core)


def turned(index, by, size):
    return lax.rem(index + (by % size), size)


def greet(barrier, peer):
    pl.semaphore_signal(barrier, inc=1, device_id=peer, device_id_type=MESH)


def remote(src, dst, ssem, rsem, peer):
    return pltpu.make_async_remote_copy(
        src_ref=src, dst_ref=dst, send_sem=ssem, recv_sem=rsem, device_id=peer, device_id_type=MESH
    )


STEPS = [(-1, 0), (1, 0), (0, -1), (0, 1), (-1, -1), (-1, 1), (1, -1), (1, 1)]


def halo_sides():
    dp = lax.axis_index("dp")
    tile = lax.axis_index("tile")
    ty = lax.div(tile, GX)
    tx = lax.rem(tile, GX)
    sides = []
    for dr, dc in STEPS:
        there = None
        for ok in ([ty >= 1] if dr < 0 else [ty <= 6] if dr > 0 else []) + (
            [tx >= 1] if dc < 0 else [tx <= 2] if dc > 0 else []
        ):
            there = ok if there is None else there & ok
        sides.append((there, (dp, tile + dr * GX + dc)))
    return sides


OFF4 = [0, -1, 1, 2]
OFF8 = [0, -1, 1, -2, 2, -3, 3, 4]


def ring_slots(n, count):
    half = n // 2
    right = [(s, j) for s in range(1, half) for j in range(count)] + [(half, j) for j in range(count // 2)]
    left = [(s, j) for s in range(1, half) for j in range(count)] + [(half, j) for j in range(count // 2, count)]
    return right, left


class Ring:
    def __init__(self, axis, n, count, offs, sub, peers, ssem, rsem, wire):
        self.axis, self.n, self.count, self.offs, self.sub, self.peers = axis, n, count, offs, sub, peers
        self.ssem, self.rsem, self.wire = ssem, rsem, wire
        self.slots = ring_slots(n, count)

    def copy(self, way, s, j):
        i = self.slots[way].index((s, j))
        ref = self.sub(-(s - 1) if way == 0 else (s - 1), j)
        return remote(ref, ref, self.ssem, self.rsem.at[way, i], self.peers[way])

    def landed(self, way, s, j):
        i = self.slots[way].index((s, j))
        ref = self.sub(-s if way == 0 else s, j)
        return pltpu.make_async_copy(ref, ref, self.rsem.at[way, i])

    def completes(self, way, s, seen):
        half = self.n // 2
        parts = [(w, s, j) for w in (0, 1) for j in range(self.count) if (s, j) in self.slots[w] and (s == half or w == way)]
        if not all(part in seen for part in parts):
            return None
        return self.offs.index(half if s == half else -s if way == 0 else s)


def plan(outer, inner, begin):
    rings = (inner, outer)
    free = {(axis, way): late for axis, late in zip("xyz", (0.0, 1.0, 2.0)) for way in (0, 1)}
    heap, events, seen = [], [], {}
    count = 0

    def push(at, what):
        nonlocal count
        count += 1
        heapq.heappush(heap, (at, count, what))

    for k in range(3):
        for way in (0, 1):
            for j in range(2):
                push(begin[k], (False, k, 0, way, 1, j))
        for way in (0, 1):
            push(begin[k], (False, k, 1, way, 1, 0))
    while heap:
        at, _, (arrived, k, level, way, s, j) = heapq.heappop(heap)
        ring = rings[level][k]
        if not arrived:
            end = max(at, free[ring.axis, way]) + ring.wire
            free[ring.axis, way] = end
            push(end + 1.7, (True, k, level, way, s, j))
            continue
        events.append((at, k, level, way, s, j))
        if (s + 1, j) in ring.slots[way]:
            push(at, (False, k, level, way, s + 1, j))
        if level == 0:
            seen.setdefault(k, set()).add((way, s, j))
            index = ring.completes(way, s, seen[k])
            for w in (0, 1):
                if index is not None and (1, index) in outer[k].slots[w]:
                    push(at, (False, k, 1, w, 1, index))
    return events


def halo_count():
    count = 0
    for there, _ in halo_sides():
        count = count + there.astype(jnp.int32)
    return count


BACK = [1, 0, 3, 2, 7, 6, 5, 4]


class Halo:
    def __init__(self, grid, ecol, ecor, rows, cols, cors, ssem, rsem):
        self.grid, self.ecol, self.ecor = grid, ecol, ecor
        self.rows, self.cols, self.cors = rows, cols, cors
        src = [grid.at[:, 0:3], grid.at[:, 5:8], ecol.at[0], ecol.at[1]] + [ecor.at[k] for k in range(4)]
        self.dst = [rows.at[1], rows.at[0], cols.at[1], cols.at[0], cors.at[3], cors.at[2], cors.at[1], cors.at[0]]
        self.rsem = rsem
        self.moves = []
        for k, (there, peer) in enumerate(halo_sides()):
            self.moves.append((there, remote(src[k], self.dst[k], ssem.at[k], rsem.at[BACK[k]], peer)))

    def start(self):
        for there, copy in self.moves:
            @pl.when(there)
            def _():
                copy.start()

    def finish(self):
        for k, (there, copy) in enumerate(self.moves):
            landed = self.dst[BACK[k]]
            @pl.when(there)
            def _():
                pltpu.make_async_copy(landed, landed, self.rsem.at[k]).wait()
                copy.wait_send()

            @pl.when(jnp.logical_not(there))
            def _():
                landed[...] = jnp.zeros(landed.shape, landed.dtype)

    def cut(self, cb, value, stage):
        for i in range(8):
            stage[3 * i : 3 * i + 3, :] = value[i, 0:3, :]
            stage[24 + 3 * i : 27 + 3 * i, :] = value[i, 13:16, :]
        for k, (r, c) in enumerate(((0, 0), (0, 13), (5, 0), (5, 13))):
            for i in range(3):
                at = 48 + 16 * k + 3 * i
                stage[at : at + 3, :] = value[r + i, c : c + 3, :]
        self.ecol[0, cb] = stage[0:24, :].astype(BF16)
        self.ecol[1, cb] = stage[24:48, :].astype(BF16)
        for k in range(4):
            self.ecor[k, cb] = stage[48 + 16 * k : 64 + 16 * k, :].astype(BF16)

    def fill(self, cb, pad):
        pad[cb, 3:11, 8:24, :] = self.grid[cb].astype(F32)
        pad[cb, 0:3, 8:24, :] = self.rows[0, cb].astype(F32)
        pad[cb, 11:14, 8:24, :] = self.rows[1, cb].astype(F32)
        for side, col in ((0, 5), (1, 24)):
            value = self.cols[side, cb].astype(F32)
            for i in range(8):
                pad[cb, 3 + i, col : col + 3, :] = value[3 * i : 3 * i + 3, :]
        for k, (row, col) in enumerate(((0, 5), (0, 24), (11, 5), (11, 24))):
            value = self.cors[k, cb].astype(F32)
            for i in range(3):
                pad[cb, row + i, col : col + 3, :] = value[3 * i : 3 * i + 3, :]


def each(count, body):
    def step(i, carry):
        body(i)
        return carry

    lax.fori_loop(0, count, step, 0)


def block_conv(start, pad, taps, cb, flip):
    total = start
    for b in range(KS):
        window = pad[cb, :, 5 + b : 21 + b, :]
        for a in range(KS):
            tap = (6 - a) * KS + (6 - b) if flip else a * KS + b
            total = total + taps[cb, tap : tap + 1, :][None] * window[a : a + 8]
    return total


LAST = 5
CHUNKS = [
    [(0, 0), (2, 0), (1, 0)],
    [(0, -1), (0, 1), (2, -1), (2, 1)],
    [(1, -1), (1, 1)],
    [(0, -2), (0, 2), (2, -2), (2, 2)],
    [(0, -3), (0, 3), (2, -3), (2, 3)],
    [(0, 4), (2, 4), (1, 2)],
]


def whole_body(
    field, cot, w_in, w_out, hbias, taps_in, v0, v1, v2, v3, v4,
    block_out, grad_in, out_sums,
    fb, cb_, raw, rawz, rawy, slab, par, bia, ecol, ecor, stage, hrows, hcols, hcors, wrows, wcols, wcors, pad, bpad, pars, taps, row, zbias, bias, table,
    rz, ry, g0, g1, g2, act, hid, acc, part, mypart, conv, inv, bc, wire, ob, sums,
    r1, r2, r3, mid, low, fin, tot,
    ls, hs, hr, h2r, ps, zs, bs, as_, ar, fs, q0r, q1r, q2r, r0r, r1r, r2r, rs, es, er, ts, os_,
):
    x, y, z, core = place()
    dp = lax.axis_index("dp")
    tile = lax.axis_index("tile")
    yl, yh = lax.rem(y, 4), lax.div(y, 4)
    xl, xh = lax.rem(x, 2), lax.div(x, 2)
    lane = lax.broadcasted_iota(jnp.int32, (1, 128), 1)
    barrier = pltpu.get_barrier_semaphore()
    sibling = device(x, y, z, 1 - core)
    xps = [device(turned(x, k, NX), y, z, core) for k in range(1, NX)]
    yps = [device(x, turned(y, k, NY), z, core) for k in range(1, NY)]
    zps = [device(x, y, turned(z, k, NZ), core) for k in range(1, NZ)]
    dps = [(turned(dp, k, 16), tile) for k in range(1, 16)]
    xys = [device(turned(x, k % 4, NX), turned(y, k // 4, NY), z, core) for k in range(1, 32)]
    mine = yl * 2 + xh
    member = yh * 4 + xl * 2 + core
    thirds = []
    for k in range(1, 8):
        o = turned(member, k, 8)
        thirds.append(device(xh * 2 + lax.rem(lax.div(o, 2), 2), lax.div(o, 4) * 4 + yl, z, lax.rem(o, 2)))
    for peer in xys + zps + thirds[0::2]:
        greet(barrier, peer)
    for there, peer in halo_sides():
        @pl.when(there)
        def _():
            greet(barrier, peer)

    for cb in range(8):
        lanes = pl.ds(128 * cb, 128)
        pltpu.make_async_copy(field.at[:, :, lanes], fb.at[cb], ls.at[0]).start()
        pltpu.make_async_copy(cot.at[:, lanes], cb_.at[cb], ls.at[1]).start()

    def settle(ref, sem):
        pltpu.make_async_copy(ref, ref, sem).wait()

    rows_in, rows_out = w_in[...].astype(F32), w_out[...].astype(F32)
    raw[0, 0:4, :], raw[0, 4:8, :] = rows_in[0:4], rows_out[0:4]
    raw[1, 0:2, :], raw[1, 2:4, :] = rows_in[4:6], rows_out[4:6]
    raw[1, 4:8, :] = jnp.zeros((4, 1024), F32)
    rawz[...] = raw[0].astype(BF16)
    rawy[...] = raw[1].astype(BF16)
    bia[...] = jnp.zeros((1, 128), F32)
    bia[:, 0:6] = hbias[...].astype(F32)
    slab[...] = jnp.zeros_like(slab)
    slab[0:49, 0:64] = taps_in[...]
    for k, v in enumerate((v0, v1, v2, v3, v4)):
        slab[49 + k : 50 + k, 0:64] = v[...]
    par[...] = jnp.where(lane < 64, slab[0:28, :], pltpu.roll(slab[28:56, :], 64, 1))
    stage[...] = jnp.zeros_like(stage)
    halo1 = Halo(fb, ecol, ecor, hrows, hcols, hcors, hs, hr)
    pl.semaphore_wait(barrier, 31 + 7 + 4 + halo_count())

    for peer in zps:
        remote(rawz, rz.at[z], fs.at[0], fs.at[1], peer).start()
    for peer in yps:
        remote(rawy, ry.at[y], fs.at[2], fs.at[3], peer).start()
    for peer in zps:
        remote(bia, zbias.at[z], zs.at[0], zs.at[1], peer).start()
    settle(fb, ls.at[0])
    settle(cb_, ls.at[1])
    each(8, lambda cb: halo1.cut(cb, fb[cb].astype(F32), stage))
    halo1.start()
    for peer in dps:
        remote(par, pars.at[dp], ps.at[0], ps.at[1], peer).start()
    rz[z] = rawz[...]
    ry[y] = rawy[...]
    zbias[z] = bia[...]
    pars[dp] = par[...]

    to = lax.broadcasted_iota(jnp.int32, (32, 64), 0)
    fro = lax.broadcasted_iota(jnp.int32, (32, 64), 1)

    def tiles(got, first_row, step):
        chosen = fro == ((to >> 1) & 7) * 8 + (to >> 4) * step + first_row + (to & 1)
        rows = jnp.concatenate([got[d].astype(F32) for d in range(8)], axis=0).astype(BF16)
        made = jnp.dot(jnp.where(chosen, 1.0, 0.0).astype(BF16), rows, preferred_element_type=F32)
        return made.astype(BF16)

    def put(home, made):
        for cb in range(8):
            for m in range(2):
                home[cb, m] = made[16 * m : 16 * m + 16, 128 * cb : 128 * cb + 128]

    xr, xb = xps[0], xps[-1]
    yr, yb = yps[0], yps[-1]
    zr_, zb = zps[0], zps[-1]
    inner = [
        Ring("x", 4, 2, OFF4, lambda b, j: g0.at[y, turned(x, b, 4), pl.ds(4 * j, 4)], (xr, xb), rs.at[0], q0r, 0.7),
        Ring("y", 8, 2, OFF8, lambda b, j: g1.at[x, turned(y, b, 8), pl.ds(4 * j, 4)], (yr, yb), rs.at[1], q1r, 0.7),
        Ring("x", 4, 2, OFF4, lambda b, j: g2.at[z, turned(x, b, 4), pl.ds(4 * j, 4)], (xr, xb), rs.at[2], q2r, 0.7),
    ]
    outer = [
        Ring("y", 8, 4, OFF4, lambda b, j: g0.at[turned(y, b, 8), turned(x, OFF4[j], 4)], (yr, yb), rs.at[3], r0r, 1.4),
        Ring("x", 4, 8, OFF8, lambda b, j: g1.at[turned(x, b, 4), turned(y, OFF8[j], 8)], (xr, xb), rs.at[4], r1r, 1.4),
        Ring("z", 8, 4, OFF4, lambda b, j: g2.at[turned(z, b, 8), turned(x, OFF4[j], 4)], (zr_, zb), rs.at[5], r2r, 1.4),
    ]
    def go(copy):
        copy.start()

    seen = [set(), set(), set()]

    def arrive(k, level, way, s, j):
        ring = (inner, outer)[level][k]
        ring.landed(way, s, j).wait()
        if (s + 1, j) in ring.slots[way]:
            go(ring.copy(way, s + 1, j))
        if level == 0:
            seen[k].add((way, s, j))
            index = ring.completes(way, s, seen[k])
            for w in (0, 1):
                if index is not None and (1, index) in outer[k].slots[w]:
                    go(outer[k].copy(w, 1, index))

    ship = [remote(act.at[a, core], act.at[a, core], as_.at[a], ar.at[a], sibling) for a in range(2)]

    def bias_push():
        settle(zbias.at[0:7], zs.at[0])
        settle(zbias.at[0:7], zs.at[1])
        total = zbias[0]
        for k in range(1, NZ):
            total = total + pltpu.roll(zbias[k], 6 * k, 1)
        row[...] = total
        me = x * 8 + y
        bias[me] = total
        for peer in xys:
            remote(row, bias.at[me], bs.at[0], bs.at[1], peer).start()

    def params():
        settle(pars.at[0:15], ps.at[0])
        settle(pars.at[0:15], ps.at[1])

        def unpack(cb):
            one, two = pars[2 * cb], pars[2 * cb + 1]
            taps[cb, 0:28, :] = jnp.where(lane < 64, one, pltpu.roll(two, 64, 1))
            taps[cb, 28:56, :] = jnp.where(lane < 64, pltpu.roll(one, 64, 1), two)

        each(8, unpack)
        for cb in range(8):
            scaled = cb_[cb].astype(F32) * taps[cb, 52:53, :]
            act[1, core, :, 128 * cb : 128 * cb + 128] = scaled.astype(BF16)

    def borders():
        ship[1].start()
        halo1.finish()
        each(8, lambda cb: halo1.fill(cb, pad))

    def conv_piece(part_number):
        def one(i):
            cb = i + 2 * part_number
            start = jnp.broadcast_to(taps[cb, 49:50, :][None], (8, 16, 128))
            conv[cb] = block_conv(start, pad, taps, cb, False).reshape(128, 128)

        each(2, one)

    def norm():
        mean = jnp.sum(sum(conv[cb] for cb in range(8)), axis=-1, keepdims=True) * (1.0 / 1024)
        square = jnp.zeros((128, 128), F32)
        for cb in range(8):
            centered = conv[cb] - mean
            square = square + centered * centered
        inverse = lax.rsqrt(jnp.sum(square, axis=-1, keepdims=True) * (1.0 / 1024) + 1e-06)
        inv[...] = jnp.broadcast_to(inverse, (128, 128))
        for cb in range(8):
            standard = (conv[cb] - mean) * inverse
            conv[cb] = standard
            normed = standard * taps[cb, 50:51, :] + taps[cb, 51:52, :]
            act[0, core, :, 128 * cb : 128 * cb + 128] = normed.astype(BF16)

    def biases():
        ship[0].start()
        settle(bias.at[0:31], bs.at[0])
        settle(bias.at[0:31], bs.at[1])
        values = bias[...].reshape(32, 128).astype(BF16)
        j = lax.broadcasted_iota(jnp.int32, (128, 128), 0)
        l = lax.broadcasted_iota(jnp.int32, (128, 128), 1)
        bx = lax.broadcasted_iota(jnp.int32, (4, 8, 128), 0)
        by = lax.broadcasted_iota(jnp.int32, (4, 8, 128), 1)
        bl = lax.broadcasted_iota(jnp.int32, (4, 8, 128), 2)
        l64 = bl & 63

        def pick(where):
            chosen = jnp.where(where, 1.0, 0.0).astype(BF16)
            return jnp.dot(values, chosen, preferred_element_type=F32).reshape(4, 8, 128)

        t0 = pick(j == 6 * ((l >> 1) & 7) + (l & 1))
        table[0] = jnp.sum(jnp.where(bx == (l64 >> 4), t0, 0.0), axis=0)
        t1_ = pick(j == 6 * ((l >> 1) & 7) + 2 + (l & 1))
        table[1, 0:4, :] = jnp.sum(jnp.where(by == (bl >> 4), t1_, 0.0), axis=1)
        for zz in range(8):
            t2_ = pick(j == 6 * zz + 4 + (l & 1))
            kept = jnp.where((bx == (l64 >> 4)) & (by == ((bl >> 1) & 7)), t2_, 0.0)
            table[2, zz : zz + 1, :] = jnp.sum(jnp.sum(kept, axis=0), axis=0, keepdims=True)
        for copy in ship:
            copy.wait()

    at = (lambda off: turned(y, off, 8), lambda off: turned(x, off, 4), lambda off: turned(z, off, 8))
    nt = (((1,), (1,)), ((), ()))

    def weights(blocks, m):
        columns = []
        for cb in range(8):
            pieces = []
            for k, off in blocks:
                if k == 0:
                    pieces.append(g0[at[0](off), :, cb, m].reshape(64, 128))
                elif k == 1:
                    pieces.append(g1[at[1](off), :, cb, m].reshape(128, 128))
                else:
                    pieces.append(g2[at[2](off), :, cb, m].reshape(64, 128))
            columns.append(jnp.concatenate(pieces, axis=0))
        return jnp.concatenate(columns, axis=1)

    def bias_row(blocks):
        out, pend = [], None
        for k, off in blocks:
            value = table[k, pl.ds(at[k](off), 1), :]
            if k == 1:
                out.append(value)
            elif pend is None:
                pend = value
            else:
                out.append(jnp.where(lane < 64, pend, value))
                pend = None
        return jnp.concatenate(out, axis=1)

    def front(blocks, a_in, a_out):
        pre = lax.dot_general(a_in, weights(blocks, 0), nt, preferred_element_type=F32) + bias_row(blocks)
        back = lax.dot_general(a_out, weights(blocks, 1), nt, preferred_element_type=F32)
        cdf = 0.5 * (1.0 + lax.erf(pre * 0.7071067811865476))
        slope = cdf + pre * jnp.exp(-0.5 * pre * pre) * 0.3989422804014327
        return (pre * cdf).astype(BF16), (back * slope).astype(BF16)

    def chunk_front(n):
        hidden, back_pre = front(CHUNKS[n], act[0].reshape(256, 1024), act[1].reshape(256, 1024))
        hid[0], hid[1] = hidden, back_pre

    def chunk_back(n):
        for m in range(2):
            value = jnp.dot(hid[m], weights(CHUNKS[n], 1 - m), preferred_element_type=F32).reshape(2, 128, 1024)
            for cb in range(8):
                piece = value[:, :, 128 * cb : 128 * cb + 128]
                acc[m, :, cb] = piece if n == 0 else acc[m, :, cb] + piece

    tasks = [(0.3, 0.5, None, bias_push), (0.6, 1.5, None, params), (1.2, 2.5, None, borders)]
    tasks += [(0.6, 0.0, None, functools.partial(conv_piece, i)) for i in range(4)]
    tasks += [(0.8, 0.0, None, norm), (0.6, 0.0, None, biases)]
    for n in range(LAST):
        tasks.append((1.0, 0.0, CHUNKS[n], functools.partial(chunk_front, n)))
        tasks.append((0.8, 0.0, CHUNKS[n], functools.partial(chunk_back, n)))
    home = (g0.at[y, x], g1.at[x, y], g2.at[z, x])
    for k, (got, first_row, step) in enumerate(((rz, 0, 4), (rz, 2, 4), (ry, 0, 2))):
        if k != 1:
            settle((rz, ry)[k // 2].at[0:7], fs.at[k])
            settle((rz, ry)[k // 2].at[0:7], fs.at[k + 1])
        put(home[k], tiles(got, first_row, step))
        for way in (0, 1):
            for j in range(2):
                go(inner[k].copy(way, 1, j))
        for way in (0, 1):
            go(outer[k].copy(way, 1, 0))
    events = plan(outer, inner, (0.0, 0.3, 0.6))

    def needs(event, blocks):
        _, k, level, way, s, j = event
        if blocks is None:
            return False
        for kk, off in blocks:
            if kk != k:
                continue
            if off == 0 and level == 0:
                return True
            if off != 0 and level == 1 and (abs(off) == s) and (s == outer[k].n // 2 or (off < 0) == (way == 0)):
                return True
        return False

    clock = 0.0
    while events or tasks:
        ready = bool(tasks) and not any(needs(e, tasks[0][2]) for e in events)
        if events and (events[0][0] <= clock or not ready or clock < tasks[0][1]):
            event = events.pop(0)
            clock = max(clock, event[0])
            arrive(*event[1:])
        else:
            length, _, _, piece = tasks.pop(0)
            piece()
            clock += length

    blocks = CHUNKS[LAST]
    swap = [remote(mypart.at[a], part.at[a], es.at[a], er.at[a], sibling) for a in range(2)]
    for turn, who in enumerate((1 - core, core)):
        for m, h in enumerate(front(blocks, act[0, who], act[1, who])):
            hid[m, 0:128, :] = h
        for m in range(2):
            value = jnp.dot(hid[m, 0:128, :], weights(blocks, 1 - m), preferred_element_type=F32)
            for cb in range(8):
                piece = acc[m, who, cb] + value[:, 128 * cb : 128 * cb + 128]
                if turn == 0:
                    mypart[m, cb] = piece.astype(BF16)
                else:
                    acc[m, core, cb] = piece
            if turn == 0:
                swap[m].start()
    for copy in swap:
        copy.wait_recv()

    sums[:, 48:64, :] = jnp.zeros((8, 16, 128), F32)

    def down(value):
        return jnp.sum(value, axis=0, keepdims=True)

    def ending(cb, carry):
        one, two = carry
        standard = conv[cb]
        upstream = cb_[cb].astype(F32)
        projected = acc[0, core, cb] + part[0, cb].astype(F32) + taps[cb, 53:54, :]
        normed = acc[1, core, cb] + part[1, cb].astype(F32)
        source = fb[cb].astype(F32).reshape(128, 128)
        ob[0, cb] = (source + taps[cb, 52:53, :] * projected).astype(BF16)
        sums[cb, 50:51, :] = down(normed * standard)
        sums[cb, 51:52, :] = down(normed)
        sums[cb, 52:53, :] = down(upstream * projected)
        scaled = normed * taps[cb, 50:51, :]
        bc[cb] = scaled
        return one + scaled, two + scaled * standard

    none = jnp.zeros((128, 128), F32)
    one, two = lax.fori_loop(0, 8, ending, (none, none))
    mean_one = jnp.sum(one, axis=-1, keepdims=True) * (1.0 / 1024)
    mean_two = jnp.sum(two, axis=-1, keepdims=True) * (1.0 / 1024)
    halo2 = Halo(wire, ecol, ecor, wrows, wcols, wcors, hs, h2r)
    inverse = inv[...]

    def rear(cb):
        back = inverse * (bc[cb] - mean_one - conv[cb] * mean_two)
        bc[cb] = back
        sums[cb, 49:50, :] = down(back)
        wire[cb] = back.reshape(8, 16, 128).astype(BF16)

    def block_grad(cb):
        back = bc[cb].reshape(8, 16, 128)
        for b in range(KS):
            window = pad[cb, :, 5 + b : 21 + b, :]
            for a in range(KS):
                product = jnp.sum(back * window[a : a + 8], axis=0)
                sums[cb, a * KS + b : a * KS + b + 1, :] = down(product)

    def firsts(k):
        other = lax.rem(mine + k, 8)
        peer = device(lax.rem(other, 2) * 2 + xl, yh * 4 + lax.div(other, 2), z, core)
        return other, remote(sums.at[other], r1.at[mine], ts.at[0], ts.at[1], peer)

    def grad_step(i):
        other, copy = firsts(i + 1)
        rear(other)
        block_grad(other)
        copy.start()

    each(7, grad_step)
    rear(mine)
    block_grad(mine)
    r1[mine] = sums[mine]
    each(8, lambda cb: halo2.cut(cb, bc[cb].reshape(8, 16, 128), stage))
    halo2.start()
    for cb in range(8):
        pltpu.make_async_copy(ob.at[0, cb], block_out.at[:, pl.ds(128 * cb, 128)], os_.at[0]).start()

    def conv_back(low_, count):
        def one(i):
            cb = i + low_
            halo2.fill(cb, bpad)
            start = cb_[cb].astype(F32).reshape(8, 16, 128)
            ob[1, cb] = block_conv(start, bpad, taps, cb, True).reshape(128, 128).astype(BF16)

        each(count, one)
        for cb in range(low_, low_ + count):
            pltpu.make_async_copy(ob.at[1, cb], grad_in.at[:, pl.ds(128 * cb, 128)], os_.at[1]).start()

    settle(r1.at[0:7], ts.at[1])
    mid[...] = jnp.sum(r1[...], axis=0).reshape(8, 8, 128)
    for k in range(7):
        remote(mid.at[turned(z, k + 1, 8)], r2.at[z], ts.at[2], ts.at[3], zps[k]).start()
    r2[z] = mid[z]
    halo2.finish()
    conv_back(0, 3)
    settle(r2.at[0:7], ts.at[3])
    low[...] = jnp.sum(r2[...], axis=0)
    for k in range(7):
        remote(low, r3.at[member], ts.at[4], ts.at[5], thirds[k]).start()
    r3[member] = low[...]
    conv_back(3, 3)
    settle(r3.at[0:7], ts.at[5])
    fin[...] = jnp.sum(r3[...], axis=0)
    for k in range(7):
        remote(fin, tot.at[z], ts.at[6], ts.at[7], zps[k]).start()
    tot[z] = fin[...]
    conv_back(6, 2)
    settle(r1.at[0:7], ts.at[0])
    for k, ref in enumerate((g0.at[0, 0:3], g1.at[0, 0:7], g2.at[0, 0:3], g0.at[0:7], g1.at[0:3], g2.at[0:7])):
        settle(ref, rs.at[k])
    for copy in swap:
        copy.wait_send()
    settle(r2.at[0:7], ts.at[2])
    settle(r3.at[0:7], ts.at[4])
    settle(ob.at[0], os_.at[0])
    settle(ob.at[1], os_.at[1])
    settle(tot.at[0:7], ts.at[6])
    settle(tot.at[0:7], ts.at[7])
    final = tot[...].reshape(64, 128) * (1.0 / 256.0)
    final = jnp.where(xl == 0, final, pltpu.roll(final, 64, 1))
    out_sums[...] = final[0:56, 0:64]


def whole(*args):
    cell = (2, 16, 128)
    any_ = pl.BlockSpec(memory_space=pl.ANY)
    scratch = [
        ((8, 8, 16, 128), BF16), ((8, 128, 128), BF16), ((2, 8, 1024), F32), ((8, 1024), BF16), ((8, 1024), BF16),
        ((56, 128), F32), ((28, 128), F32), ((1, 128), F32), ((2, 8, 24, 128), BF16), ((4, 8, 16, 128), BF16), ((112, 128), F32),
        ((2, 8, 3, 16, 128), BF16), ((2, 8, 24, 128), BF16), ((4, 8, 16, 128), BF16),
        ((2, 8, 3, 16, 128), BF16), ((2, 8, 24, 128), BF16), ((4, 8, 16, 128), BF16),
        ((8, 14, 32, 128), F32), ((8, 14, 32, 128), F32), ((16, 28, 128), F32), ((8, 56, 128), F32),
        ((1, 128), F32), ((8, 1, 128), F32), ((32, 1, 128), F32), ((3, 8, 128), F32),
        ((8, 8, 1024), BF16), ((8, 8, 1024), BF16),
        ((8, 4, 8) + cell, BF16), ((4, 8, 8) + cell, BF16), ((8, 4, 8) + cell, BF16),
        ((2, 2, 128, 1024), BF16), ((2, 256, 256), BF16), ((2, 2, 8, 128, 128), F32),
        ((2, 8, 128, 128), BF16), ((2, 8, 128, 128), BF16), ((8, 128, 128), F32), ((128, 128), F32),
        ((8, 128, 128), F32), ((8, 8, 16, 128), BF16), ((2, 8, 128, 128), BF16), ((8, 64, 128), F32),
        ((8, 64, 128), F32), ((8, 8, 128), F32), ((8, 8, 128), F32), ((8, 8, 128), F32), ((8, 128), F32), ((8, 128), F32),
        ((8, 8, 128), F32),
    ]
    sems = [(2,), (8,), (8,), (8,), (2,), (2,), (2,), (2,), (2,), (4,), (2, 3), (2, 7), (2, 3), (2, 14), (2, 12), (2, 14)]
    sems += [(6,), (2,), (2,), (8,), (2,)]
    return pl.pallas_call(
        whole_body,
        out_shape=(
            jax.ShapeDtypeStruct((128, 1024), BF16),
            jax.ShapeDtypeStruct((128, 1024), BF16),
            jax.ShapeDtypeStruct((56, 64), F32),
        ),
        in_specs=[any_, any_] + [VMEM] * 9,
        out_specs=[any_, any_, VMEM],
        scratch_shapes=[pltpu.VMEM(*s) for s in scratch] + [DMA(s) for s in sems],
        compiler_params=pltpu.CompilerParams(
            collective_id=0, has_side_effects=True, vmem_limit_bytes=56 * 1024 * 1024
        ),
        name="whole",
    )(*args)


def hand_out(block_in, grad_in, sums, block_out, grad_out, kernel_out, *rest):
    block_out[...] = block_in[...]
    grad_out[...] = grad_in[...]
    kernel_out[...] = sums[0:49, :]
    for k, out in enumerate(rest):
        out[...] = sums[49 + k : 50 + k, :]


def per_device(
    features,
    cotangent,
    in_weight,
    out_weight,
    hidden_bias,
    kernel,
    conv_bias,
    norm_gain,
    norm_bias,
    layer_scale,
    out_bias,
):
    _, _, rows, cols, width = features.shape
    field = features.reshape(rows, cols, width)
    cot = cotangent.reshape(rows * cols, width)
    pixels = rows * cols
    vectors = [v.reshape(1, -1) for v in (conv_bias, norm_gain, norm_bias, layer_scale, out_bias)]
    made = whole(field, cot, in_weight, out_weight, hidden_bias.reshape(1, -1), kernel, *vectors)
    block_out, grad_in, out_kernel, *rest = pl.pallas_call(
        hand_out,
        out_shape=[jax.ShapeDtypeStruct((pixels, width), BF16)] * 2
        + [jax.ShapeDtypeStruct((49, 64), F32)]
        + [jax.ShapeDtypeStruct((1, 64), F32)] * 4,
        in_specs=[VMEM] * 3,
        out_specs=[VMEM] * 7,
        name="hand_out",
    )(*made)
    return (block_out.reshape(features.shape), grad_in.reshape(features.shape), out_kernel, *[v.reshape(-1) for v in rest])


def solution(mesh):
    placed = (
        P("dp", "tile", None, None, None),
        P("dp", "tile", None, None, None),
        P(("dp", "tile"), None),
        P(("dp", "tile"), None),
        P(("dp", "tile")),
        P(None, "dp"),
        P("dp"),
        P("dp"),
        P("dp"),
        P("dp"),
        P("dp"),
    )
    return jax.shard_map(
        per_device,
        mesh=mesh,
        in_specs=placed,
        out_specs=(
            P("dp", "tile", None, None, None),
            P("dp", "tile", None, None, None),
            P(None, "dp"),
            P("dp"),
            P("dp"),
            P("dp"),
            P("dp"),
        ),
        check_vma=False,
    )
```

```python
import functools
import heapq

import jax
import jax.numpy as jnp
from jax import lax
from jax.experimental import pallas as pl
from jax.experimental.pallas import tpu as pltpu
from jax.sharding import PartitionSpec as P

KS = 7
GX = 4
NX, NY, NZ = 4, 8, 8
MESH = pl.DeviceIdType.MESH
VMEM = pl.BlockSpec(memory_space=pltpu.VMEM)
F32 = jnp.float32
BF16 = jnp.bfloat16
DMA = pltpu.SemaphoreType.DMA


def place():
    dp = lax.axis_index("dp")
    tile = lax.axis_index("tile")
    x = lax.rem(dp, 4)
    y = lax.div(tile, 16) * 4 + lax.div(dp, 4)
    z = lax.rem(lax.div(tile, 2), 8)
    core = lax.rem(tile, 2)
    return x, y, z, core


def device(x, y, z, core):
    return (lax.rem(y, 4) * 4 + x, lax.div(y, 4) * 16 + z * 2 + core)


def turned(index, by, size):
    return lax.rem(index + (by % size), size)


def greet(barrier, peer):
    pl.semaphore_signal(barrier, inc=1, device_id=peer, device_id_type=MESH)


def remote(src, dst, ssem, rsem, peer):
    return pltpu.make_async_remote_copy(
        src_ref=src, dst_ref=dst, send_sem=ssem, recv_sem=rsem, device_id=peer, device_id_type=MESH
    )


STEPS = [(-1, 0), (1, 0), (0, -1), (0, 1), (-1, -1), (-1, 1), (1, -1), (1, 1)]


def halo_sides():
    dp = lax.axis_index("dp")
    tile = lax.axis_index("tile")
    ty = lax.div(tile, GX)
    tx = lax.rem(tile, GX)
    sides = []
    for dr, dc in STEPS:
        there = None
        for ok in ([ty >= 1] if dr < 0 else [ty <= 6] if dr > 0 else []) + (
            [tx >= 1] if dc < 0 else [tx <= 2] if dc > 0 else []
        ):
            there = ok if there is None else there & ok
        sides.append((there, (dp, tile + dr * GX + dc)))
    return sides


OFF4 = [0, -1, 1, 2]
OFF8 = [0, -1, 1, -2, 2, -3, 3, 4]


def ring_slots(n, count):
    half = n // 2
    right = [(s, j) for s in range(1, half) for j in range(count)] + [(half, j) for j in range(count // 2)]
    left = [(s, j) for s in range(1, half) for j in range(count)] + [(half, j) for j in range(count // 2, count)]
    return right, left


class Ring:
    def __init__(self, axis, n, count, offs, sub, peers, ssem, rsem, wire):
        self.axis, self.n, self.count, self.offs, self.sub, self.peers = axis, n, count, offs, sub, peers
        self.ssem, self.rsem, self.wire = ssem, rsem, wire
        self.slots = ring_slots(n, count)

    def copy(self, way, s, j):
        i = self.slots[way].index((s, j))
        ref = self.sub(-(s - 1) if way == 0 else (s - 1), j)
        return remote(ref, ref, self.ssem, self.rsem.at[way, i], self.peers[way])

    def landed(self, way, s, j):
        i = self.slots[way].index((s, j))
        ref = self.sub(-s if way == 0 else s, j)
        return pltpu.make_async_copy(ref, ref, self.rsem.at[way, i])

    def completes(self, way, s, seen):
        half = self.n // 2
        parts = [(w, s, j) for w in (0, 1) for j in range(self.count) if (s, j) in self.slots[w] and (s == half or w == way)]
        if not all(part in seen for part in parts):
            return None
        return self.offs.index(half if s == half else -s if way == 0 else s)


LEAD = 1.5


def plan(outer, inner, begin):
    rings = (inner, outer)
    free = {(axis, way): late for axis, late in zip("xyz", (0.0, 1.0, 2.0)) for way in (0, 1)}
    queues = {link: [] for link in free}
    heap, steps, seen = [], [], {}
    count = 0

    def push(at, kind, what):
        nonlocal count
        count += 1
        heapq.heappush(heap, (at, count, kind, what))

    def dispatch(at, link):
        if queues[link] and free[link] <= at:
            _, _, ready, given, (k, level, way, s, j) = heapq.heappop(queues[link])
            free[link] = at + rings[level][k].wire
            push(free[link], "free", link)
            push(free[link] + 1.7, "landed", (k, level, way, s, j))
            if not given:
                steps.append((max(ready, at - LEAD), 1, (k, level, way, s, j)))

    for link, late in free.items():
        push(late, "free", link)
    for k in range(3):
        for way in (0, 1):
            for j in range(2):
                push(begin[k], "given", (k, 0, way, 1, j))
        for way in (0, 1):
            push(begin[k], "given", (k, 1, way, 1, 0))
    while heap:
        at, number, kind, what = heapq.heappop(heap)
        if kind == "free":
            dispatch(at, what)
            continue
        k, level, way, s, j = what
        ring = rings[level][k]
        if kind in ("ready", "given"):
            link = (ring.axis, way)
            heapq.heappush(queues[link], (0 if kind == "given" else level, number, at, kind == "given", what))
            dispatch(at, link)
            continue
        steps.append((at, 0, what))
        if (s + 1, j) in ring.slots[way]:
            push(at, "ready", (k, level, way, s + 1, j))
        if level == 0:
            seen.setdefault(k, set()).add((way, s, j))
            index = ring.completes(way, s, seen[k])
            for w in (0, 1):
                if index is not None and (1, index) in outer[k].slots[w]:
                    push(at, "ready", (k, 1, w, 1, index))
    return sorted(steps)


def halo_count():
    count = 0
    for there, _ in halo_sides():
        count = count + there.astype(jnp.int32)
    return count


BACK = [1, 0, 3, 2, 7, 6, 5, 4]


class Halo:
    def __init__(self, grid, ecol, ecor, rows, cols, cors, ssem, rsem):
        self.grid, self.ecol, self.ecor = grid, ecol, ecor
        self.rows, self.cols, self.cors = rows, cols, cors
        src = [grid.at[:, 0:3], grid.at[:, 5:8], ecol.at[0], ecol.at[1]] + [ecor.at[k] for k in range(4)]
        self.dst = [rows.at[1], rows.at[0], cols.at[1], cols.at[0], cors.at[3], cors.at[2], cors.at[1], cors.at[0]]
        self.rsem = rsem
        self.moves = []
        for k, (there, peer) in enumerate(halo_sides()):
            self.moves.append((there, remote(src[k], self.dst[k], ssem.at[k], rsem.at[BACK[k]], peer)))

    def start(self):
        for there, copy in self.moves:
            @pl.when(there)
            def _():
                copy.start()

    def finish(self):
        for k, (there, copy) in enumerate(self.moves):
            landed = self.dst[BACK[k]]
            @pl.when(there)
            def _():
                pltpu.make_async_copy(landed, landed, self.rsem.at[k]).wait()
                copy.wait_send()

            @pl.when(jnp.logical_not(there))
            def _():
                landed[...] = jnp.zeros(landed.shape, landed.dtype)

    def cut(self, cb, value, stage):
        for i in range(8):
            stage[3 * i : 3 * i + 3, :] = value[i, 0:3, :]
            stage[24 + 3 * i : 27 + 3 * i, :] = value[i, 13:16, :]
        for k, (r, c) in enumerate(((0, 0), (0, 13), (5, 0), (5, 13))):
            for i in range(3):
                at = 48 + 16 * k + 3 * i
                stage[at : at + 3, :] = value[r + i, c : c + 3, :]
        self.ecol[0, cb] = stage[0:24, :].astype(BF16)
        self.ecol[1, cb] = stage[24:48, :].astype(BF16)
        for k in range(4):
            self.ecor[k, cb] = stage[48 + 16 * k : 64 + 16 * k, :].astype(BF16)

    def fill(self, cb, pad):
        pad[cb, 3:11, 8:24, :] = self.grid[cb].astype(F32)
        pad[cb, 0:3, 8:24, :] = self.rows[0, cb].astype(F32)
        pad[cb, 11:14, 8:24, :] = self.rows[1, cb].astype(F32)
        for side, col in ((0, 5), (1, 24)):
            value = self.cols[side, cb].astype(F32)
            for i in range(8):
                pad[cb, 3 + i, col : col + 3, :] = value[3 * i : 3 * i + 3, :]
        for k, (row, col) in enumerate(((0, 5), (0, 24), (11, 5), (11, 24))):
            value = self.cors[k, cb].astype(F32)
            for i in range(3):
                pad[cb, row + i, col : col + 3, :] = value[3 * i : 3 * i + 3, :]


def each(count, body):
    def step(i, carry):
        body(i)
        return carry

    lax.fori_loop(0, count, step, 0)


def block_conv(start, pad, taps, cb, flip):
    total = start
    for b in range(KS):
        window = pad[cb, :, 5 + b : 21 + b, :]
        for a in range(KS):
            tap = (6 - a) * KS + (6 - b) if flip else a * KS + b
            total = total + taps[cb, tap : tap + 1, :][None] * window[a : a + 8]
    return total


LAST = 5
CHUNKS = [
    [(0, 0), (2, 0), (1, 0)],
    [(0, -1), (0, 1), (2, -1), (2, 1)],
    [(1, -1), (1, 1)],
    [(0, -2), (0, 2), (2, -2), (2, 2)],
    [(0, -3), (0, 3), (2, -3), (2, 3)],
    [(0, 4), (2, 4), (1, 2)],
]


def whole_body(
    field, cot, w_in, w_out, hbias, taps_in, v0, v1, v2, v3, v4,
    block_out, grad_in, out_sums,
    fb, cb_, raw, rawz, rawy, slab, par, bia, ecol, ecor, stage, hrows, hcols, hcors, wrows, wcols, wcors, pad, bpad, pars, taps, row, zbias, bias, table,
    rz, ry, g0, g1, g2, act, hid, acc, part, mypart, conv, inv, bc, wire, ob, sums,
    r1, r2, r3, mid, low, fin, tot,
    ls, hs, hr, h2r, ps, zs, bs, as_, ar, fs, q0r, q1r, q2r, r0r, r1r, r2r, rs, es, er, ts, os_,
):
    x, y, z, core = place()
    dp = lax.axis_index("dp")
    tile = lax.axis_index("tile")
    yl, yh = lax.rem(y, 4), lax.div(y, 4)
    xl, xh = lax.rem(x, 2), lax.div(x, 2)
    lane = lax.broadcasted_iota(jnp.int32, (1, 128), 1)
    barrier = pltpu.get_barrier_semaphore()
    sibling = device(x, y, z, 1 - core)
    xps = [device(turned(x, k, NX), y, z, core) for k in range(1, NX)]
    yps = [device(x, turned(y, k, NY), z, core) for k in range(1, NY)]
    zps = [device(x, y, turned(z, k, NZ), core) for k in range(1, NZ)]
    dps = [(turned(dp, k, 16), tile) for k in range(1, 16)]
    xys = [device(turned(x, k % 4, NX), turned(y, k // 4, NY), z, core) for k in range(1, 32)]
    mine = yl * 2 + xh
    member = yh * 4 + xl * 2 + core
    thirds = []
    for k in range(1, 8):
        o = turned(member, k, 8)
        thirds.append(device(xh * 2 + lax.rem(lax.div(o, 2), 2), lax.div(o, 4) * 4 + yl, z, lax.rem(o, 2)))
    for peer in xys + zps + thirds[0::2]:
        greet(barrier, peer)
    for there, peer in halo_sides():
        @pl.when(there)
        def _():
            greet(barrier, peer)

    for cb in range(8):
        lanes = pl.ds(128 * cb, 128)
        pltpu.make_async_copy(field.at[:, :, lanes], fb.at[cb], ls.at[0]).start()
        pltpu.make_async_copy(cot.at[:, lanes], cb_.at[cb], ls.at[1]).start()

    def settle(ref, sem):
        pltpu.make_async_copy(ref, ref, sem).wait()

    rows_in, rows_out = w_in[...].astype(F32), w_out[...].astype(F32)
    raw[0, 0:4, :], raw[0, 4:8, :] = rows_in[0:4], rows_out[0:4]
    raw[1, 0:2, :], raw[1, 2:4, :] = rows_in[4:6], rows_out[4:6]
    raw[1, 4:8, :] = jnp.zeros((4, 1024), F32)
    rawz[...] = raw[0].astype(BF16)
    rawy[...] = raw[1].astype(BF16)
    bia[...] = jnp.zeros((1, 128), F32)
    bia[:, 0:6] = hbias[...].astype(F32)
    slab[...] = jnp.zeros_like(slab)
    slab[0:49, 0:64] = taps_in[...]
    for k, v in enumerate((v0, v1, v2, v3, v4)):
        slab[49 + k : 50 + k, 0:64] = v[...]
    par[...] = jnp.where(lane < 64, slab[0:28, :], pltpu.roll(slab[28:56, :], 64, 1))
    stage[...] = jnp.zeros_like(stage)
    halo1 = Halo(fb, ecol, ecor, hrows, hcols, hcors, hs, hr)
    pl.semaphore_wait(barrier, 31 + 7 + 4 + halo_count())

    for peer in zps:
        remote(rawz, rz.at[z], fs.at[0], fs.at[1], peer).start()
    for peer in yps:
        remote(rawy, ry.at[y], fs.at[2], fs.at[3], peer).start()
    for peer in zps:
        remote(bia, zbias.at[z], zs.at[0], zs.at[1], peer).start()
    settle(fb, ls.at[0])
    settle(cb_, ls.at[1])
    each(8, lambda cb: halo1.cut(cb, fb[cb].astype(F32), stage))
    rz[z] = rawz[...]
    ry[y] = rawy[...]
    zbias[z] = bia[...]
    pars[dp] = par[...]

    to = lax.broadcasted_iota(jnp.int32, (32, 64), 0)
    fro = lax.broadcasted_iota(jnp.int32, (32, 64), 1)

    def tiles(got, first_row, step):
        chosen = fro == ((to >> 1) & 7) * 8 + (to >> 4) * step + first_row + (to & 1)
        rows = jnp.concatenate([got[d].astype(F32) for d in range(8)], axis=0).astype(BF16)
        made = jnp.dot(jnp.where(chosen, 1.0, 0.0).astype(BF16), rows, preferred_element_type=F32)
        return made.astype(BF16)

    def put(home, made):
        for cb in range(8):
            for m in range(2):
                home[cb, m] = made[16 * m : 16 * m + 16, 128 * cb : 128 * cb + 128]

    xr, xb = xps[0], xps[-1]
    yr, yb = yps[0], yps[-1]
    zr_, zb = zps[0], zps[-1]
    inner = [
        Ring("x", 4, 2, OFF4, lambda b, j: g0.at[y, turned(x, b, 4), pl.ds(4 * j, 4)], (xr, xb), rs.at[0], q0r, 0.7),
        Ring("y", 8, 2, OFF8, lambda b, j: g1.at[x, turned(y, b, 8), pl.ds(4 * j, 4)], (yr, yb), rs.at[1], q1r, 0.7),
        Ring("x", 4, 2, OFF4, lambda b, j: g2.at[z, turned(x, b, 4), pl.ds(4 * j, 4)], (xr, xb), rs.at[2], q2r, 0.7),
    ]
    outer = [
        Ring("y", 8, 4, OFF4, lambda b, j: g0.at[turned(y, b, 8), turned(x, OFF4[j], 4)], (yr, yb), rs.at[3], r0r, 1.4),
        Ring("x", 4, 8, OFF8, lambda b, j: g1.at[turned(x, b, 4), turned(y, OFF8[j], 8)], (xr, xb), rs.at[4], r1r, 1.4),
        Ring("z", 8, 4, OFF4, lambda b, j: g2.at[turned(z, b, 8), turned(x, OFF4[j], 4)], (zr_, zb), rs.at[5], r2r, 1.4),
    ]
    def go(copy):
        copy.start()

    def perform(kind, what):
        k, level, way, s, j = what
        ring = (inner, outer)[level][k]
        if kind == 0:
            ring.landed(way, s, j).wait()
        else:
            go(ring.copy(way, s, j))

    ship = [remote(act.at[a, core], act.at[a, core], as_.at[a], ar.at[a], sibling) for a in range(2)]

    def bias_push():
        settle(zbias.at[0:7], zs.at[0])
        settle(zbias.at[0:7], zs.at[1])
        total = zbias[0]
        for k in range(1, NZ):
            total = total + pltpu.roll(zbias[k], 6 * k, 1)
        row[...] = total
        me = x * 8 + y
        bias[me] = total
        for peer in xys:
            remote(row, bias.at[me], bs.at[0], bs.at[1], peer).start()

    def params():
        settle(pars.at[0:15], ps.at[0])
        settle(pars.at[0:15], ps.at[1])

        def unpack(cb):
            one, two = pars[2 * cb], pars[2 * cb + 1]
            taps[cb, 0:28, :] = jnp.where(lane < 64, one, pltpu.roll(two, 64, 1))
            taps[cb, 28:56, :] = jnp.where(lane < 64, pltpu.roll(one, 64, 1), two)

        each(8, unpack)
        for cb in range(8):
            scaled = cb_[cb].astype(F32) * taps[cb, 52:53, :]
            act[1, core, :, 128 * cb : 128 * cb + 128] = scaled.astype(BF16)

    def borders():
        ship[1].start()
        halo1.finish()
        each(8, lambda cb: halo1.fill(cb, pad))

    def conv_piece(part_number):
        def one(i):
            cb = i + 2 * part_number
            start = jnp.broadcast_to(taps[cb, 49:50, :][None], (8, 16, 128))
            conv[cb] = block_conv(start, pad, taps, cb, False).reshape(128, 128)

        each(2, one)

    def norm():
        mean = jnp.sum(sum(conv[cb] for cb in range(8)), axis=-1, keepdims=True) * (1.0 / 1024)
        square = jnp.zeros((128, 128), F32)
        for cb in range(8):
            centered = conv[cb] - mean
            square = square + centered * centered
        inverse = lax.rsqrt(jnp.sum(square, axis=-1, keepdims=True) * (1.0 / 1024) + 1e-06)
        inv[...] = jnp.broadcast_to(inverse, (128, 128))
        for cb in range(8):
            standard = (conv[cb] - mean) * inverse
            conv[cb] = standard
            normed = standard * taps[cb, 50:51, :] + taps[cb, 51:52, :]
            act[0, core, :, 128 * cb : 128 * cb + 128] = normed.astype(BF16)

    def biases():
        ship[0].start()
        settle(bias.at[0:31], bs.at[0])
        settle(bias.at[0:31], bs.at[1])
        values = bias[...].reshape(32, 128).astype(BF16)
        j = lax.broadcasted_iota(jnp.int32, (128, 128), 0)
        l = lax.broadcasted_iota(jnp.int32, (128, 128), 1)
        bx = lax.broadcasted_iota(jnp.int32, (4, 8, 128), 0)
        by = lax.broadcasted_iota(jnp.int32, (4, 8, 128), 1)
        bl = lax.broadcasted_iota(jnp.int32, (4, 8, 128), 2)
        l64 = bl & 63

        def pick(where):
            chosen = jnp.where(where, 1.0, 0.0).astype(BF16)
            return jnp.dot(values, chosen, preferred_element_type=F32).reshape(4, 8, 128)

        t0 = pick(j == 6 * ((l >> 1) & 7) + (l & 1))
        table[0] = jnp.sum(jnp.where(bx == (l64 >> 4), t0, 0.0), axis=0)
        t1_ = pick(j == 6 * ((l >> 1) & 7) + 2 + (l & 1))
        table[1, 0:4, :] = jnp.sum(jnp.where(by == (bl >> 4), t1_, 0.0), axis=1)
        for zz in range(8):
            t2_ = pick(j == 6 * zz + 4 + (l & 1))
            kept = jnp.where((bx == (l64 >> 4)) & (by == ((bl >> 1) & 7)), t2_, 0.0)
            table[2, zz : zz + 1, :] = jnp.sum(jnp.sum(kept, axis=0), axis=0, keepdims=True)
        for copy in ship:
            copy.wait()

    at = (lambda off: turned(y, off, 8), lambda off: turned(x, off, 4), lambda off: turned(z, off, 8))
    nt = (((1,), (1,)), ((), ()))

    def weights(blocks, m):
        columns = []
        for cb in range(8):
            pieces = []
            for k, off in blocks:
                if k == 0:
                    pieces.append(g0[at[0](off), :, cb, m].reshape(64, 128))
                elif k == 1:
                    pieces.append(g1[at[1](off), :, cb, m].reshape(128, 128))
                else:
                    pieces.append(g2[at[2](off), :, cb, m].reshape(64, 128))
            columns.append(jnp.concatenate(pieces, axis=0))
        return jnp.concatenate(columns, axis=1)

    def bias_row(blocks):
        out, pend = [], None
        for k, off in blocks:
            value = table[k, pl.ds(at[k](off), 1), :]
            if k == 1:
                out.append(value)
            elif pend is None:
                pend = value
            else:
                out.append(jnp.where(lane < 64, pend, value))
                pend = None
        return jnp.concatenate(out, axis=1)

    def front(blocks, a_in, a_out):
        pre = lax.dot_general(a_in, weights(blocks, 0), nt, preferred_element_type=F32) + bias_row(blocks)
        back = lax.dot_general(a_out, weights(blocks, 1), nt, preferred_element_type=F32)
        cdf = 0.5 * (1.0 + lax.erf(pre * 0.7071067811865476))
        slope = cdf + pre * jnp.exp(-0.5 * pre * pre) * 0.3989422804014327
        return (pre * cdf).astype(BF16), (back * slope).astype(BF16)

    def chunk_front(n):
        hidden, back_pre = front(CHUNKS[n], act[0].reshape(256, 1024), act[1].reshape(256, 1024))
        hid[0], hid[1] = hidden, back_pre

    def chunk_back(n):
        for m in range(2):
            value = jnp.dot(hid[m], weights(CHUNKS[n], 1 - m), preferred_element_type=F32).reshape(2, 128, 1024)
            for cb in range(8):
                piece = value[:, :, 128 * cb : 128 * cb + 128]
                acc[m, :, cb] = piece if n == 0 else acc[m, :, cb] + piece

    tasks = [(0.3, 0.5, None, bias_push), (0.6, 5.0, None, params), (1.2, 9.0, None, borders)]
    tasks += [(0.6, 0.0, None, functools.partial(conv_piece, i)) for i in range(4)]
    tasks += [(0.8, 0.0, None, norm), (0.6, 0.0, None, biases)]
    for n in range(LAST):
        tasks.append((1.0, 0.0, CHUNKS[n], functools.partial(chunk_front, n)))
        tasks.append((0.8, 0.0, CHUNKS[n], functools.partial(chunk_back, n)))
    home = (g0.at[y, x], g1.at[x, y], g2.at[z, x])
    for k, (got, first_row, step) in enumerate(((rz, 0, 4), (rz, 2, 4), (ry, 0, 2))):
        if k != 1:
            settle((rz, ry)[k // 2].at[0:7], fs.at[k])
            settle((rz, ry)[k // 2].at[0:7], fs.at[k + 1])
        put(home[k], tiles(got, first_row, step))
        for way in (0, 1):
            for j in range(2):
                go(inner[k].copy(way, 1, j))
        for way in (0, 1):
            go(outer[k].copy(way, 1, 0))
    halo1.start()
    for peer in dps:
        remote(par, pars.at[dp], ps.at[0], ps.at[1], peer).start()
    events = plan(outer, inner, (0.0, 0.3, 0.6))

    def needs(event, blocks):
        _, kind, (k, level, way, s, j) = event
        if blocks is None or kind:
            return False
        for kk, off in blocks:
            if kk != k:
                continue
            if off == 0 and level == 0:
                return True
            if off != 0 and level == 1 and (abs(off) == s) and (s == outer[k].n // 2 or (off < 0) == (way == 0)):
                return True
        return False

    clock = 0.0
    while events or tasks:
        ready = bool(tasks) and not any(needs(e, tasks[0][2]) for e in events)
        if events and (events[0][0] <= clock or not ready or clock < tasks[0][1]):
            event = events.pop(0)
            clock = max(clock, event[0])
            perform(*event[1:])
        else:
            length, _, _, piece = tasks.pop(0)
            piece()
            clock += length

    blocks = CHUNKS[LAST]
    swap = [remote(mypart.at[a], part.at[a], es.at[a], er.at[a], sibling) for a in range(2)]
    for turn, who in enumerate((1 - core, core)):
        for m, h in enumerate(front(blocks, act[0, who], act[1, who])):
            hid[m, 0:128, :] = h
        for m in range(2):
            value = jnp.dot(hid[m, 0:128, :], weights(blocks, 1 - m), preferred_element_type=F32)
            for cb in range(8):
                piece = acc[m, who, cb] + value[:, 128 * cb : 128 * cb + 128]
                if turn == 0:
                    mypart[m, cb] = piece.astype(BF16)
                else:
                    acc[m, core, cb] = piece
            if turn == 0:
                swap[m].start()
    for copy in swap:
        copy.wait_recv()

    sums[:, 48:64, :] = jnp.zeros((8, 16, 128), F32)

    def down(value):
        return jnp.sum(value, axis=0, keepdims=True)

    def ending(cb, carry):
        one, two = carry
        standard = conv[cb]
        upstream = cb_[cb].astype(F32)
        projected = acc[0, core, cb] + part[0, cb].astype(F32) + taps[cb, 53:54, :]
        normed = acc[1, core, cb] + part[1, cb].astype(F32)
        source = fb[cb].astype(F32).reshape(128, 128)
        ob[0, cb] = (source + taps[cb, 52:53, :] * projected).astype(BF16)
        sums[cb, 50:51, :] = down(normed * standard)
        sums[cb, 51:52, :] = down(normed)
        sums[cb, 52:53, :] = down(upstream * projected)
        scaled = normed * taps[cb, 50:51, :]
        bc[cb] = scaled
        return one + scaled, two + scaled * standard

    none = jnp.zeros((128, 128), F32)
    one, two = lax.fori_loop(0, 8, ending, (none, none))
    mean_one = jnp.sum(one, axis=-1, keepdims=True) * (1.0 / 1024)
    mean_two = jnp.sum(two, axis=-1, keepdims=True) * (1.0 / 1024)
    halo2 = Halo(wire, ecol, ecor, wrows, wcols, wcors, hs, h2r)
    inverse = inv[...]

    def rear(cb):
        back = inverse * (bc[cb] - mean_one - conv[cb] * mean_two)
        bc[cb] = back
        sums[cb, 49:50, :] = down(back)
        wire[cb] = back.reshape(8, 16, 128).astype(BF16)

    def block_grad(cb):
        back = bc[cb].reshape(8, 16, 128)
        for b in range(KS):
            window = pad[cb, :, 5 + b : 21 + b, :]
            for a in range(KS):
                product = jnp.sum(back * window[a : a + 8], axis=0)
                sums[cb, a * KS + b : a * KS + b + 1, :] = down(product)

    def firsts(k):
        other = lax.rem(mine + k, 8)
        peer = device(lax.rem(other, 2) * 2 + xl, yh * 4 + lax.div(other, 2), z, core)
        return other, remote(sums.at[other], r1.at[mine], ts.at[0], ts.at[1], peer)

    def grad_step(i):
        other, copy = firsts(i + 1)
        rear(other)
        block_grad(other)
        copy.start()

    each(7, grad_step)
    rear(mine)
    block_grad(mine)
    r1[mine] = sums[mine]
    each(8, lambda cb: halo2.cut(cb, bc[cb].reshape(8, 16, 128), stage))
    def conv_back(low_, count):
        def one(i):
            cb = i + low_
            halo2.fill(cb, bpad)
            start = cb_[cb].astype(F32).reshape(8, 16, 128)
            ob[1, cb] = block_conv(start, bpad, taps, cb, True).reshape(128, 128).astype(BF16)

        each(count, one)
        for cb in range(low_, low_ + count):
            pltpu.make_async_copy(ob.at[1, cb], grad_in.at[:, pl.ds(128 * cb, 128)], os_.at[1]).start()

    settle(r1.at[0:7], ts.at[1])
    mid[...] = jnp.sum(r1[...], axis=0).reshape(8, 8, 128)
    for k in range(7):
        remote(mid.at[turned(z, k + 1, 8)], r2.at[z], ts.at[2], ts.at[3], zps[k]).start()
    r2[z] = mid[z]
    halo2.start()
    for cb in range(8):
        pltpu.make_async_copy(ob.at[0, cb], block_out.at[:, pl.ds(128 * cb, 128)], os_.at[0]).start()
    settle(r2.at[0:7], ts.at[3])
    low[...] = jnp.sum(r2[...], axis=0)
    for k in range(7):
        remote(low, r3.at[member], ts.at[4], ts.at[5], thirds[k]).start()
    r3[member] = low[...]
    settle(r3.at[0:7], ts.at[5])
    fin[...] = jnp.sum(r3[...], axis=0)
    for k in range(7):
        remote(fin, tot.at[z], ts.at[6], ts.at[7], zps[k]).start()
    tot[z] = fin[...]
    halo2.finish()
    conv_back(0, 8)
    settle(r1.at[0:7], ts.at[0])
    for k, ref in enumerate((g0.at[0, 0:3], g1.at[0, 0:7], g2.at[0, 0:3], g0.at[0:7], g1.at[0:3], g2.at[0:7])):
        settle(ref, rs.at[k])
    for copy in swap:
        copy.wait_send()
    settle(r2.at[0:7], ts.at[2])
    settle(r3.at[0:7], ts.at[4])
    settle(ob.at[0], os_.at[0])
    settle(ob.at[1], os_.at[1])
    settle(tot.at[0:7], ts.at[6])
    settle(tot.at[0:7], ts.at[7])
    final = tot[...].reshape(64, 128) * (1.0 / 256.0)
    final = jnp.where(xl == 0, final, pltpu.roll(final, 64, 1))
    out_sums[...] = final[0:56, 0:64]


def whole(*args):
    cell = (2, 16, 128)
    any_ = pl.BlockSpec(memory_space=pl.ANY)
    scratch = [
        ((8, 8, 16, 128), BF16), ((8, 128, 128), BF16), ((2, 8, 1024), F32), ((8, 1024), BF16), ((8, 1024), BF16),
        ((56, 128), F32), ((28, 128), F32), ((1, 128), F32), ((2, 8, 24, 128), BF16), ((4, 8, 16, 128), BF16), ((112, 128), F32),
        ((2, 8, 3, 16, 128), BF16), ((2, 8, 24, 128), BF16), ((4, 8, 16, 128), BF16),
        ((2, 8, 3, 16, 128), BF16), ((2, 8, 24, 128), BF16), ((4, 8, 16, 128), BF16),
        ((8, 14, 32, 128), F32), ((8, 14, 32, 128), F32), ((16, 28, 128), F32), ((8, 56, 128), F32),
        ((1, 128), F32), ((8, 1, 128), F32), ((32, 1, 128), F32), ((3, 8, 128), F32),
        ((8, 8, 1024), BF16), ((8, 8, 1024), BF16),
        ((8, 4, 8) + cell, BF16), ((4, 8, 8) + cell, BF16), ((8, 4, 8) + cell, BF16),
        ((2, 2, 128, 1024), BF16), ((2, 256, 256), BF16), ((2, 2, 8, 128, 128), F32),
        ((2, 8, 128, 128), BF16), ((2, 8, 128, 128), BF16), ((8, 128, 128), F32), ((128, 128), F32),
        ((8, 128, 128), F32), ((8, 8, 16, 128), BF16), ((2, 8, 128, 128), BF16), ((8, 64, 128), F32),
        ((8, 64, 128), F32), ((8, 8, 128), F32), ((8, 8, 128), F32), ((8, 8, 128), F32), ((8, 128), F32), ((8, 128), F32),
        ((8, 8, 128), F32),
    ]
    sems = [(2,), (8,), (8,), (8,), (2,), (2,), (2,), (2,), (2,), (4,), (2, 3), (2, 7), (2, 3), (2, 14), (2, 12), (2, 14)]
    sems += [(6,), (2,), (2,), (8,), (2,)]
    return pl.pallas_call(
        whole_body,
        out_shape=(
            jax.ShapeDtypeStruct((128, 1024), BF16),
            jax.ShapeDtypeStruct((128, 1024), BF16),
            jax.ShapeDtypeStruct((56, 64), F32),
        ),
        in_specs=[any_, any_] + [VMEM] * 9,
        out_specs=[any_, any_, VMEM],
        scratch_shapes=[pltpu.VMEM(*s) for s in scratch] + [DMA(s) for s in sems],
        compiler_params=pltpu.CompilerParams(
            collective_id=0, has_side_effects=True, vmem_limit_bytes=56 * 1024 * 1024
        ),
        name="whole",
    )(*args)


def hand_out(block_in, grad_in, sums, block_out, grad_out, kernel_out, *rest):
    block_out[...] = block_in[...]
    grad_out[...] = grad_in[...]
    kernel_out[...] = sums[0:49, :]
    for k, out in enumerate(rest):
        out[...] = sums[49 + k : 50 + k, :]


def per_device(
    features,
    cotangent,
    in_weight,
    out_weight,
    hidden_bias,
    kernel,
    conv_bias,
    norm_gain,
    norm_bias,
    layer_scale,
    out_bias,
):
    _, _, rows, cols, width = features.shape
    field = features.reshape(rows, cols, width)
    cot = cotangent.reshape(rows * cols, width)
    pixels = rows * cols
    vectors = [v.reshape(1, -1) for v in (conv_bias, norm_gain, norm_bias, layer_scale, out_bias)]
    made = whole(field, cot, in_weight, out_weight, hidden_bias.reshape(1, -1), kernel, *vectors)
    block_out, grad_in, out_kernel, *rest = pl.pallas_call(
        hand_out,
        out_shape=[jax.ShapeDtypeStruct((pixels, width), BF16)] * 2
        + [jax.ShapeDtypeStruct((49, 64), F32)]
        + [jax.ShapeDtypeStruct((1, 64), F32)] * 4,
        in_specs=[VMEM] * 3,
        out_specs=[VMEM] * 7,
        name="hand_out",
    )(*made)
    return (block_out.reshape(features.shape), grad_in.reshape(features.shape), out_kernel, *[v.reshape(-1) for v in rest])


def solution(mesh):
    placed = (
        P("dp", "tile", None, None, None),
        P("dp", "tile", None, None, None),
        P(("dp", "tile"), None),
        P(("dp", "tile"), None),
        P(("dp", "tile")),
        P(None, "dp"),
        P("dp"),
        P("dp"),
        P("dp"),
        P("dp"),
        P("dp"),
    )
    return jax.shard_map(
        per_device,
        mesh=mesh,
        in_specs=placed,
        out_specs=(
            P("dp", "tile", None, None, None),
            P("dp", "tile", None, None, None),
            P(None, "dp"),
            P("dp"),
            P("dp"),
            P("dp"),
            P("dp"),
        ),
        check_vma=False,
    )
```

```python
import functools
import heapq

import jax
import jax.numpy as jnp
from jax import lax
from jax.experimental import pallas as pl
from jax.experimental.pallas import tpu as pltpu
from jax.sharding import PartitionSpec as P

KS = 7
GX = 4
NX, NY, NZ = 4, 8, 8
MESH = pl.DeviceIdType.MESH
VMEM = pl.BlockSpec(memory_space=pltpu.VMEM)
F32 = jnp.float32
BF16 = jnp.bfloat16
DMA = pltpu.SemaphoreType.DMA


def place():
    dp = lax.axis_index("dp")
    tile = lax.axis_index("tile")
    x = lax.rem(dp, 4)
    y = lax.div(tile, 16) * 4 + lax.div(dp, 4)
    z = lax.rem(lax.div(tile, 2), 8)
    core = lax.rem(tile, 2)
    return x, y, z, core


def device(x, y, z, core):
    return (lax.rem(y, 4) * 4 + x, lax.div(y, 4) * 16 + z * 2 + core)


def turned(index, by, size):
    return lax.rem(index + (by % size), size)


def greet(barrier, peer):
    pl.semaphore_signal(barrier, inc=1, device_id=peer, device_id_type=MESH)


def remote(src, dst, ssem, rsem, peer):
    return pltpu.make_async_remote_copy(
        src_ref=src, dst_ref=dst, send_sem=ssem, recv_sem=rsem, device_id=peer, device_id_type=MESH
    )


STEPS = [(-1, 0), (1, 0), (0, -1), (0, 1), (-1, -1), (-1, 1), (1, -1), (1, 1)]


def halo_sides():
    dp = lax.axis_index("dp")
    tile = lax.axis_index("tile")
    ty = lax.div(tile, GX)
    tx = lax.rem(tile, GX)
    sides = []
    for dr, dc in STEPS:
        there = None
        for ok in ([ty >= 1] if dr < 0 else [ty <= 6] if dr > 0 else []) + (
            [tx >= 1] if dc < 0 else [tx <= 2] if dc > 0 else []
        ):
            there = ok if there is None else there & ok
        sides.append((there, (dp, tile + dr * GX + dc)))
    return sides


OFF4 = [0, -1, 1, 2]
OFF8 = [0, -1, 1, -2, 2, -3, 3, 4]


def ring_slots(n, count):
    half = n // 2
    right = [(s, j) for s in range(1, half) for j in range(count)] + [(half, j) for j in range(count // 2)]
    left = [(s, j) for s in range(1, half) for j in range(count)] + [(half, j) for j in range(count // 2, count)]
    return right, left


class Ring:
    def __init__(self, axis, n, count, offs, sub, peers, ssem, rsem, wire):
        self.axis, self.n, self.count, self.offs, self.sub, self.peers = axis, n, count, offs, sub, peers
        self.ssem, self.rsem, self.wire = ssem, rsem, wire
        self.slots = ring_slots(n, count)

    def copy(self, way, s, j):
        i = self.slots[way].index((s, j))
        ref = self.sub(-(s - 1) if way == 0 else (s - 1), j)
        return remote(ref, ref, self.ssem, self.rsem.at[way, i], self.peers[way])

    def landed(self, way, s, j):
        i = self.slots[way].index((s, j))
        ref = self.sub(-s if way == 0 else s, j)
        return pltpu.make_async_copy(ref, ref, self.rsem.at[way, i])

    def completes(self, way, s, seen):
        half = self.n // 2
        parts = [(w, s, j) for w in (0, 1) for j in range(self.count) if (s, j) in self.slots[w] and (s == half or w == way)]
        if not all(part in seen for part in parts):
            return None
        return self.offs.index(half if s == half else -s if way == 0 else s)


LEAD = 1.5


def plan(outer, inner, begin):
    rings = (inner, outer)
    free = {(axis, way): late for axis, late in zip("xyz", (0.0, 1.0, 2.0)) for way in (0, 1)}
    queues = {link: [] for link in free}
    heap, steps, seen = [], [], {}
    count = 0

    def push(at, kind, what):
        nonlocal count
        count += 1
        heapq.heappush(heap, (at, count, kind, what))

    def dispatch(at, link):
        if queues[link] and free[link] <= at:
            _, _, ready, given, (k, level, way, s, j) = heapq.heappop(queues[link])
            free[link] = at + rings[level][k].wire
            push(free[link], "free", link)
            push(free[link] + 1.7, "landed", (k, level, way, s, j))
            if not given:
                steps.append((max(ready, at - LEAD), 1, (k, level, way, s, j)))

    for link, late in free.items():
        push(late, "free", link)
    for k in range(3):
        for way in (0, 1):
            for j in range(2):
                push(begin[k], "given", (k, 0, way, 1, j))
        for way in (0, 1):
            push(begin[k], "given", (k, 1, way, 1, 0))
    while heap:
        at, number, kind, what = heapq.heappop(heap)
        if kind == "free":
            dispatch(at, what)
            continue
        k, level, way, s, j = what
        ring = rings[level][k]
        if kind in ("ready", "given"):
            link = (ring.axis, way)
            heapq.heappush(queues[link], (0 if kind == "given" else level, number, at, kind == "given", what))
            dispatch(at, link)
            continue
        steps.append((at, 0, what))
        if (s + 1, j) in ring.slots[way]:
            push(at, "ready", (k, level, way, s + 1, j))
        if level == 0:
            seen.setdefault(k, set()).add((way, s, j))
            index = ring.completes(way, s, seen[k])
            for w in (0, 1):
                if index is not None and (1, index) in outer[k].slots[w]:
                    push(at, "ready", (k, 1, w, 1, index))
    return sorted(steps)


def halo_count():
    count = 0
    for there, _ in halo_sides():
        count = count + there.astype(jnp.int32)
    return count


BACK = [1, 0, 3, 2, 7, 6, 5, 4]


class Halo:
    def __init__(self, grid, ecol, ecor, rows, cols, cors, ssem, rsem):
        self.grid, self.ecol, self.ecor = grid, ecol, ecor
        self.rows, self.cols, self.cors = rows, cols, cors
        src = [grid.at[:, 0:3], grid.at[:, 5:8], ecol.at[0], ecol.at[1]] + [ecor.at[k] for k in range(4)]
        self.dst = [rows.at[1], rows.at[0], cols.at[1], cols.at[0], cors.at[3], cors.at[2], cors.at[1], cors.at[0]]
        self.rsem = rsem
        self.moves = []
        for k, (there, peer) in enumerate(halo_sides()):
            self.moves.append((there, remote(src[k], self.dst[k], ssem.at[k], rsem.at[BACK[k]], peer)))

    def start(self):
        for there, copy in self.moves:
            @pl.when(there)
            def _():
                copy.start()

    def finish(self):
        for k, (there, copy) in enumerate(self.moves):
            landed = self.dst[BACK[k]]
            @pl.when(there)
            def _():
                pltpu.make_async_copy(landed, landed, self.rsem.at[k]).wait()
                copy.wait_send()

            @pl.when(jnp.logical_not(there))
            def _():
                landed[...] = jnp.zeros(landed.shape, landed.dtype)

    def cut(self, cb, value, stage):
        for i in range(8):
            stage[3 * i : 3 * i + 3, :] = value[i, 0:3, :]
            stage[24 + 3 * i : 27 + 3 * i, :] = value[i, 13:16, :]
        for k, (r, c) in enumerate(((0, 0), (0, 13), (5, 0), (5, 13))):
            for i in range(3):
                at = 48 + 16 * k + 3 * i
                stage[at : at + 3, :] = value[r + i, c : c + 3, :]
        self.ecol[0, cb] = stage[0:24, :].astype(BF16)
        self.ecol[1, cb] = stage[24:48, :].astype(BF16)
        for k in range(4):
            self.ecor[k, cb] = stage[48 + 16 * k : 64 + 16 * k, :].astype(BF16)

    def fill(self, cb, pad):
        pad[cb, 3:11, 8:24, :] = self.grid[cb].astype(F32)
        pad[cb, 0:3, 8:24, :] = self.rows[0, cb].astype(F32)
        pad[cb, 11:14, 8:24, :] = self.rows[1, cb].astype(F32)
        for side, col in ((0, 5), (1, 24)):
            value = self.cols[side, cb].astype(F32)
            for i in range(8):
                pad[cb, 3 + i, col : col + 3, :] = value[3 * i : 3 * i + 3, :]
        for k, (row, col) in enumerate(((0, 5), (0, 24), (11, 5), (11, 24))):
            value = self.cors[k, cb].astype(F32)
            for i in range(3):
                pad[cb, row + i, col : col + 3, :] = value[3 * i : 3 * i + 3, :]


def each(count, body):
    def step(i, carry):
        body(i)
        return carry

    lax.fori_loop(0, count, step, 0)


def block_conv(start, pad, taps, cb, flip):
    total = start
    for b in range(KS):
        window = pad[cb, :, 5 + b : 21 + b, :]
        for a in range(KS):
            tap = (6 - a) * KS + (6 - b) if flip else a * KS + b
            total = total + taps[cb, tap : tap + 1, :][None] * window[a : a + 8]
    return total


LAST = 5
CHUNKS = [
    [(0, 0), (2, 0), (1, 0)],
    [(0, -1), (0, 1), (2, -1), (2, 1)],
    [(1, -1), (1, 1)],
    [(0, -2), (0, 2), (2, -2), (2, 2)],
    [(0, -3), (0, 3), (2, -3), (2, 3)],
    [(0, 4), (2, 4), (1, 2)],
]


def whole_body(
    field, cot, w_in, w_out, hbias, taps_in, v0, v1, v2, v3, v4,
    block_out, grad_in, out_sums,
    fb, cb_, raw, rawz, rawy, slab, par, bia, ecol, ecor, stage, hrows, hcols, hcors, wrows, wcols, wcors, pad, bpad, pars, taps, row, zbias, bias, table,
    rz, ry, g0, g1, g2, act, hid, acc, part, mypart, conv, inv, bc, wire, ob, sums,
    r1, r2, r3, mid, low, fin, tot,
    ls, hs, hr, h2r, ps, zs, bs, as_, ar, fs, q0r, q1r, q2r, r0r, r1r, r2r, rs, es, er, ts, os_,
):
    x, y, z, core = place()
    dp = lax.axis_index("dp")
    tile = lax.axis_index("tile")
    yl, yh = lax.rem(y, 4), lax.div(y, 4)
    xl, xh = lax.rem(x, 2), lax.div(x, 2)
    lane = lax.broadcasted_iota(jnp.int32, (1, 128), 1)
    barrier = pltpu.get_barrier_semaphore()
    sibling = device(x, y, z, 1 - core)
    xps = [device(turned(x, k, NX), y, z, core) for k in range(1, NX)]
    yps = [device(x, turned(y, k, NY), z, core) for k in range(1, NY)]
    zps = [device(x, y, turned(z, k, NZ), core) for k in range(1, NZ)]
    dps = [(turned(dp, k, 16), tile) for k in range(1, 16)]
    xys = [device(turned(x, k % 4, NX), turned(y, k // 4, NY), z, core) for k in range(1, 32)]
    mine = yl * 2 + xh
    member = yh * 4 + xl * 2 + core
    thirds = []
    for k in range(1, 8):
        o = turned(member, k, 8)
        thirds.append(device(xh * 2 + lax.rem(lax.div(o, 2), 2), lax.div(o, 4) * 4 + yl, z, lax.rem(o, 2)))
    for peer in xys + zps + thirds[0::2]:
        greet(barrier, peer)
    for there, peer in halo_sides():
        @pl.when(there)
        def _():
            greet(barrier, peer)

    for cb in range(8):
        lanes = pl.ds(128 * cb, 128)
        pltpu.make_async_copy(field.at[:, :, lanes], fb.at[cb], ls.at[0]).start()
        pltpu.make_async_copy(cot.at[:, lanes], cb_.at[cb], ls.at[1]).start()

    def settle(ref, sem):
        pltpu.make_async_copy(ref, ref, sem).wait()

    rows_in, rows_out = w_in[...].astype(F32), w_out[...].astype(F32)
    raw[0, 0:2, :], raw[0, 2:4, :] = rows_in[0:2], rows_out[0:2]
    raw[0, 4:8, :] = jnp.zeros((4, 1024), F32)
    raw[1, 0:4, :], raw[1, 4:8, :] = rows_in[2:6], rows_out[2:6]
    rawz[...] = raw[0].astype(BF16)
    rawy[...] = raw[1].astype(BF16)
    bia[...] = jnp.zeros((1, 128), F32)
    bia[:, 0:6] = hbias[...].astype(F32)
    slab[...] = jnp.zeros_like(slab)
    slab[0:49, 0:64] = taps_in[...]
    for k, v in enumerate((v0, v1, v2, v3, v4)):
        slab[49 + k : 50 + k, 0:64] = v[...]
    par[...] = jnp.where(lane < 64, slab[0:28, :], pltpu.roll(slab[28:56, :], 64, 1))
    stage[...] = jnp.zeros_like(stage)
    halo1 = Halo(fb, ecol, ecor, hrows, hcols, hcors, hs, hr)
    pl.semaphore_wait(barrier, 31 + 7 + 4 + halo_count())

    for peer in zps:
        remote(rawz, rz.at[z], fs.at[0], fs.at[1], peer).start()
    for peer in yps:
        remote(rawy, ry.at[y], fs.at[2], fs.at[3], peer).start()
    for peer in zps:
        remote(bia, zbias.at[z], zs.at[0], zs.at[1], peer).start()
    settle(fb, ls.at[0])
    settle(cb_, ls.at[1])
    each(8, lambda cb: halo1.cut(cb, fb[cb].astype(F32), stage))
    rz[z] = rawz[...]
    ry[y] = rawy[...]
    zbias[z] = bia[...]
    pars[dp] = par[...]

    to = lax.broadcasted_iota(jnp.int32, (32, 64), 0)
    fro = lax.broadcasted_iota(jnp.int32, (32, 64), 1)

    def tiles(got, first_row, step):
        chosen = fro == ((to >> 1) & 7) * 8 + (to >> 4) * step + first_row + (to & 1)
        rows = jnp.concatenate([got[d].astype(F32) for d in range(8)], axis=0).astype(BF16)
        made = jnp.dot(jnp.where(chosen, 1.0, 0.0).astype(BF16), rows, preferred_element_type=F32)
        return made.astype(BF16)

    def put(home, made):
        for cb in range(8):
            for m in range(2):
                home[cb, m] = made[16 * m : 16 * m + 16, 128 * cb : 128 * cb + 128]

    xr, xb = xps[0], xps[-1]
    yr, yb = yps[0], yps[-1]
    zr_, zb = zps[0], zps[-1]
    inner = [
        Ring("x", 4, 2, OFF4, lambda b, j: g0.at[y, turned(x, b, 4), pl.ds(4 * j, 4)], (xr, xb), rs.at[0], q0r, 0.7),
        Ring("z", 8, 2, OFF8, lambda b, j: g1.at[x, turned(z, b, 8), pl.ds(4 * j, 4)], (zr_, zb), rs.at[1], q1r, 0.7),
        Ring("x", 4, 2, OFF4, lambda b, j: g2.at[z, turned(x, b, 4), pl.ds(4 * j, 4)], (xr, xb), rs.at[2], q2r, 0.7),
    ]
    outer = [
        Ring("y", 8, 4, OFF4, lambda b, j: g0.at[turned(y, b, 8), turned(x, OFF4[j], 4)], (yr, yb), rs.at[3], r0r, 1.4),
        Ring("x", 4, 8, OFF8, lambda b, j: g1.at[turned(x, b, 4), turned(z, OFF8[j], 8)], (xr, xb), rs.at[4], r1r, 1.4),
        Ring("z", 8, 4, OFF4, lambda b, j: g2.at[turned(z, b, 8), turned(x, OFF4[j], 4)], (zr_, zb), rs.at[5], r2r, 1.4),
    ]
    def go(copy):
        copy.start()

    def perform(kind, what):
        k, level, way, s, j = what
        ring = (inner, outer)[level][k]
        if kind == 0:
            ring.landed(way, s, j).wait()
        else:
            go(ring.copy(way, s, j))

    ship = [remote(act.at[a, core], act.at[a, core], as_.at[a], ar.at[a], sibling) for a in range(2)]

    def bias_push():
        settle(zbias.at[0:7], zs.at[0])
        settle(zbias.at[0:7], zs.at[1])
        total = zbias[0]
        for k in range(1, NZ):
            total = total + pltpu.roll(zbias[k], 6 * k, 1)
        row[...] = total
        me = x * 8 + y
        bias[me] = total
        for peer in xys:
            remote(row, bias.at[me], bs.at[0], bs.at[1], peer).start()

    def params():
        settle(pars.at[0:15], ps.at[0])
        settle(pars.at[0:15], ps.at[1])

        def unpack(cb):
            one, two = pars[2 * cb], pars[2 * cb + 1]
            taps[cb, 0:28, :] = jnp.where(lane < 64, one, pltpu.roll(two, 64, 1))
            taps[cb, 28:56, :] = jnp.where(lane < 64, pltpu.roll(one, 64, 1), two)

        each(8, unpack)
        for cb in range(8):
            scaled = cb_[cb].astype(F32) * taps[cb, 52:53, :]
            act[1, core, :, 128 * cb : 128 * cb + 128] = scaled.astype(BF16)

    def borders():
        ship[1].start()
        halo1.finish()
        each(8, lambda cb: halo1.fill(cb, pad))

    def conv_piece(part_number):
        def one(i):
            cb = i + 2 * part_number
            start = jnp.broadcast_to(taps[cb, 49:50, :][None], (8, 16, 128))
            conv[cb] = block_conv(start, pad, taps, cb, False).reshape(128, 128)

        each(2, one)

    def norm():
        mean = jnp.sum(sum(conv[cb] for cb in range(8)), axis=-1, keepdims=True) * (1.0 / 1024)
        square = jnp.zeros((128, 128), F32)
        for cb in range(8):
            centered = conv[cb] - mean
            square = square + centered * centered
        inverse = lax.rsqrt(jnp.sum(square, axis=-1, keepdims=True) * (1.0 / 1024) + 1e-06)
        inv[...] = jnp.broadcast_to(inverse, (128, 128))
        for cb in range(8):
            standard = (conv[cb] - mean) * inverse
            conv[cb] = standard
            normed = standard * taps[cb, 50:51, :] + taps[cb, 51:52, :]
            act[0, core, :, 128 * cb : 128 * cb + 128] = normed.astype(BF16)

    def biases():
        ship[0].start()
        settle(bias.at[0:31], bs.at[0])
        settle(bias.at[0:31], bs.at[1])
        values = bias[...].reshape(32, 128).astype(BF16)
        j = lax.broadcasted_iota(jnp.int32, (128, 128), 0)
        l = lax.broadcasted_iota(jnp.int32, (128, 128), 1)
        bx = lax.broadcasted_iota(jnp.int32, (4, 8, 128), 0)
        by = lax.broadcasted_iota(jnp.int32, (4, 8, 128), 1)
        bl = lax.broadcasted_iota(jnp.int32, (4, 8, 128), 2)
        l64 = bl & 63

        def pick(where):
            chosen = jnp.where(where, 1.0, 0.0).astype(BF16)
            return jnp.dot(values, chosen, preferred_element_type=F32).reshape(4, 8, 128)

        t0 = pick(j == 6 * ((l >> 1) & 7) + (l & 1))
        table[0] = jnp.sum(jnp.where(bx == (l64 >> 4), t0, 0.0), axis=0)
        t1_ = pick(j == 6 * (l >> 4) + 2 + (l & 1))
        table[1, 0:4, :] = jnp.sum(jnp.where(by == ((bl >> 1) & 7), t1_, 0.0), axis=1)
        for zz in range(8):
            t2_ = pick(j == 6 * zz + 4 + (l & 1))
            kept = jnp.where((bx == (l64 >> 4)) & (by == ((bl >> 1) & 7)), t2_, 0.0)
            table[2, zz : zz + 1, :] = jnp.sum(jnp.sum(kept, axis=0), axis=0, keepdims=True)
        for copy in ship:
            copy.wait()

    at = (lambda off: turned(y, off, 8), lambda off: turned(x, off, 4), lambda off: turned(z, off, 8))
    nt = (((1,), (1,)), ((), ()))

    def weights(blocks, m):
        columns = []
        for cb in range(8):
            pieces = []
            for k, off in blocks:
                if k == 0:
                    pieces.append(g0[at[0](off), :, cb, m].reshape(64, 128))
                elif k == 1:
                    pieces.append(g1[at[1](off), :, cb, m].reshape(128, 128))
                else:
                    pieces.append(g2[at[2](off), :, cb, m].reshape(64, 128))
            columns.append(jnp.concatenate(pieces, axis=0))
        return jnp.concatenate(columns, axis=1)

    def bias_row(blocks):
        out, pend = [], None
        for k, off in blocks:
            value = table[k, pl.ds(at[k](off), 1), :]
            if k == 1:
                out.append(value)
            elif pend is None:
                pend = value
            else:
                out.append(jnp.where(lane < 64, pend, value))
                pend = None
        return jnp.concatenate(out, axis=1)

    def front(blocks, a_in, a_out):
        pre = lax.dot_general(a_in, weights(blocks, 0), nt, preferred_element_type=F32) + bias_row(blocks)
        back = lax.dot_general(a_out, weights(blocks, 1), nt, preferred_element_type=F32)
        cdf = 0.5 * (1.0 + lax.erf(pre * 0.7071067811865476))
        slope = cdf + pre * jnp.exp(-0.5 * pre * pre) * 0.3989422804014327
        return (pre * cdf).astype(BF16), (back * slope).astype(BF16)

    def chunk_front(n):
        hidden, back_pre = front(CHUNKS[n], act[0].reshape(256, 1024), act[1].reshape(256, 1024))
        hid[0], hid[1] = hidden, back_pre

    def chunk_back(n):
        for m in range(2):
            value = jnp.dot(hid[m], weights(CHUNKS[n], 1 - m), preferred_element_type=F32).reshape(2, 128, 1024)
            for cb in range(8):
                piece = value[:, :, 128 * cb : 128 * cb + 128]
                acc[m, :, cb] = piece if n == 0 else acc[m, :, cb] + piece

    tasks = [(0.3, 0.5, None, bias_push), (0.6, 5.0, None, params), (1.2, 9.0, None, borders)]
    tasks += [(0.6, 0.0, None, functools.partial(conv_piece, i)) for i in range(4)]
    tasks += [(0.8, 0.0, None, norm), (0.6, 0.0, None, biases)]
    for n in range(LAST):
        tasks.append((1.0, 0.0, CHUNKS[n], functools.partial(chunk_front, n)))
        tasks.append((0.8, 0.0, CHUNKS[n], functools.partial(chunk_back, n)))
    home = (g0.at[y, x], g1.at[x, z], g2.at[z, x])
    for k, (got, first_row, step) in enumerate(((rz, 0, 2), (ry, 0, 4), (ry, 2, 4))):
        if k != 2:
            settle(got.at[0:7], fs.at[2 * k])
            settle(got.at[0:7], fs.at[2 * k + 1])
        put(home[k], tiles(got, first_row, step))
        for way in (0, 1):
            for j in range(2):
                go(inner[k].copy(way, 1, j))
        for way in (0, 1):
            go(outer[k].copy(way, 1, 0))
    halo1.start()
    for peer in dps:
        remote(par, pars.at[dp], ps.at[0], ps.at[1], peer).start()
    events = plan(outer, inner, (0.0, 0.3, 0.3))

    def needs(event, blocks):
        _, kind, (k, level, way, s, j) = event
        if blocks is None or kind:
            return False
        for kk, off in blocks:
            if kk != k:
                continue
            if off == 0 and level == 0:
                return True
            if off != 0 and level == 1 and (abs(off) == s) and (s == outer[k].n // 2 or (off < 0) == (way == 0)):
                return True
        return False

    clock = 0.0
    while events or tasks:
        ready = bool(tasks) and not any(needs(e, tasks[0][2]) for e in events)
        if events and (events[0][0] <= clock or not ready or clock < tasks[0][1]):
            event = events.pop(0)
            clock = max(clock, event[0])
            perform(*event[1:])
        else:
            length, _, _, piece = tasks.pop(0)
            piece()
            clock += length

    blocks = CHUNKS[LAST]
    swap = [remote(mypart.at[a], part.at[a], es.at[a], er.at[a], sibling) for a in range(2)]
    for turn, who in enumerate((1 - core, core)):
        for m, h in enumerate(front(blocks, act[0, who], act[1, who])):
            hid[m, 0:128, :] = h
        for m in range(2):
            value = jnp.dot(hid[m, 0:128, :], weights(blocks, 1 - m), preferred_element_type=F32)
            for cb in range(8):
                piece = acc[m, who, cb] + value[:, 128 * cb : 128 * cb + 128]
                if turn == 0:
                    mypart[m, cb] = piece.astype(BF16)
                else:
                    acc[m, core, cb] = piece
            if turn == 0:
                swap[m].start()
    for copy in swap:
        copy.wait_recv()

    sums[:, 48:64, :] = jnp.zeros((8, 16, 128), F32)

    def down(value):
        return jnp.sum(value, axis=0, keepdims=True)

    def ending(cb, carry):
        one, two = carry
        standard = conv[cb]
        upstream = cb_[cb].astype(F32)
        projected = acc[0, core, cb] + part[0, cb].astype(F32) + taps[cb, 53:54, :]
        normed = acc[1, core, cb] + part[1, cb].astype(F32)
        source = fb[cb].astype(F32).reshape(128, 128)
        ob[0, cb] = (source + taps[cb, 52:53, :] * projected).astype(BF16)
        sums[cb, 50:51, :] = down(normed * standard)
        sums[cb, 51:52, :] = down(normed)
        sums[cb, 52:53, :] = down(upstream * projected)
        scaled = normed * taps[cb, 50:51, :]
        bc[cb] = scaled
        return one + scaled, two + scaled * standard

    none = jnp.zeros((128, 128), F32)
    one, two = lax.fori_loop(0, 8, ending, (none, none))
    mean_one = jnp.sum(one, axis=-1, keepdims=True) * (1.0 / 1024)
    mean_two = jnp.sum(two, axis=-1, keepdims=True) * (1.0 / 1024)
    halo2 = Halo(wire, ecol, ecor, wrows, wcols, wcors, hs, h2r)
    inverse = inv[...]

    def rear(cb):
        back = inverse * (bc[cb] - mean_one - conv[cb] * mean_two)
        bc[cb] = back
        sums[cb, 49:50, :] = down(back)
        wire[cb] = back.reshape(8, 16, 128).astype(BF16)

    def block_grad(cb):
        back = bc[cb].reshape(8, 16, 128)
        for b in range(KS):
            window = pad[cb, :, 5 + b : 21 + b, :]
            for a in range(KS):
                product = jnp.sum(back * window[a : a + 8], axis=0)
                sums[cb, a * KS + b : a * KS + b + 1, :] = down(product)

    def firsts(k):
        other = lax.rem(mine + k, 8)
        peer = device(lax.rem(other, 2) * 2 + xl, yh * 4 + lax.div(other, 2), z, core)
        return other, remote(sums.at[other], r1.at[mine], ts.at[0], ts.at[1], peer)

    def grad_step(i):
        other, copy = firsts(i + 1)
        rear(other)
        block_grad(other)
        copy.start()

    each(7, grad_step)
    rear(mine)
    block_grad(mine)
    r1[mine] = sums[mine]
    each(8, lambda cb: halo2.cut(cb, bc[cb].reshape(8, 16, 128), stage))
    def conv_back(low_, count):
        def one(i):
            cb = i + low_
            halo2.fill(cb, bpad)
            start = cb_[cb].astype(F32).reshape(8, 16, 128)
            ob[1, cb] = block_conv(start, bpad, taps, cb, True).reshape(128, 128).astype(BF16)

        each(count, one)
        for cb in range(low_, low_ + count):
            pltpu.make_async_copy(ob.at[1, cb], grad_in.at[:, pl.ds(128 * cb, 128)], os_.at[1]).start()

    settle(r1.at[0:7], ts.at[1])
    mid[...] = jnp.sum(r1[...], axis=0).reshape(8, 8, 128)
    for k in range(7):
        remote(mid.at[turned(z, k + 1, 8)], r2.at[z], ts.at[2], ts.at[3], zps[k]).start()
    r2[z] = mid[z]
    halo2.start()
    for cb in range(8):
        pltpu.make_async_copy(ob.at[0, cb], block_out.at[:, pl.ds(128 * cb, 128)], os_.at[0]).start()
    settle(r2.at[0:7], ts.at[3])
    low[...] = jnp.sum(r2[...], axis=0)
    for k in range(7):
        remote(low, r3.at[member], ts.at[4], ts.at[5], thirds[k]).start()
    r3[member] = low[...]
    settle(r3.at[0:7], ts.at[5])
    fin[...] = jnp.sum(r3[...], axis=0)
    for k in range(7):
        remote(fin, tot.at[z], ts.at[6], ts.at[7], zps[k]).start()
    tot[z] = fin[...]
    halo2.finish()
    conv_back(0, 8)
    settle(r1.at[0:7], ts.at[0])
    for k, ref in enumerate((g0.at[0, 0:3], g1.at[0, 0:7], g2.at[0, 0:3], g0.at[0:7], g1.at[0:3], g2.at[0:7])):
        settle(ref, rs.at[k])
    for copy in swap:
        copy.wait_send()
    settle(r2.at[0:7], ts.at[2])
    settle(r3.at[0:7], ts.at[4])
    settle(ob.at[0], os_.at[0])
    settle(ob.at[1], os_.at[1])
    settle(tot.at[0:7], ts.at[6])
    settle(tot.at[0:7], ts.at[7])
    final = tot[...].reshape(64, 128) * (1.0 / 256.0)
    final = jnp.where(xl == 0, final, pltpu.roll(final, 64, 1))
    out_sums[...] = final[0:56, 0:64]


def whole(*args):
    cell = (2, 16, 128)
    any_ = pl.BlockSpec(memory_space=pl.ANY)
    scratch = [
        ((8, 8, 16, 128), BF16), ((8, 128, 128), BF16), ((2, 8, 1024), F32), ((8, 1024), BF16), ((8, 1024), BF16),
        ((56, 128), F32), ((28, 128), F32), ((1, 128), F32), ((2, 8, 24, 128), BF16), ((4, 8, 16, 128), BF16), ((112, 128), F32),
        ((2, 8, 3, 16, 128), BF16), ((2, 8, 24, 128), BF16), ((4, 8, 16, 128), BF16),
        ((2, 8, 3, 16, 128), BF16), ((2, 8, 24, 128), BF16), ((4, 8, 16, 128), BF16),
        ((8, 14, 32, 128), F32), ((8, 14, 32, 128), F32), ((16, 28, 128), F32), ((8, 56, 128), F32),
        ((1, 128), F32), ((8, 1, 128), F32), ((32, 1, 128), F32), ((3, 8, 128), F32),
        ((8, 8, 1024), BF16), ((8, 8, 1024), BF16),
        ((8, 4, 8) + cell, BF16), ((4, 8, 8) + cell, BF16), ((8, 4, 8) + cell, BF16),
        ((2, 2, 128, 1024), BF16), ((2, 256, 256), BF16), ((2, 2, 8, 128, 128), F32),
        ((2, 8, 128, 128), BF16), ((2, 8, 128, 128), BF16), ((8, 128, 128), F32), ((128, 128), F32),
        ((8, 128, 128), F32), ((8, 8, 16, 128), BF16), ((2, 8, 128, 128), BF16), ((8, 64, 128), F32),
        ((8, 64, 128), F32), ((8, 8, 128), F32), ((8, 8, 128), F32), ((8, 8, 128), F32), ((8, 128), F32), ((8, 128), F32),
        ((8, 8, 128), F32),
    ]
    sems = [(2,), (8,), (8,), (8,), (2,), (2,), (2,), (2,), (2,), (4,), (2, 3), (2, 7), (2, 3), (2, 14), (2, 12), (2, 14)]
    sems += [(6,), (2,), (2,), (8,), (2,)]
    return pl.pallas_call(
        whole_body,
        out_shape=(
            jax.ShapeDtypeStruct((128, 1024), BF16),
            jax.ShapeDtypeStruct((128, 1024), BF16),
            jax.ShapeDtypeStruct((56, 64), F32),
        ),
        in_specs=[any_, any_] + [VMEM] * 9,
        out_specs=[any_, any_, VMEM],
        scratch_shapes=[pltpu.VMEM(*s) for s in scratch] + [DMA(s) for s in sems],
        compiler_params=pltpu.CompilerParams(
            collective_id=0, has_side_effects=True, vmem_limit_bytes=56 * 1024 * 1024
        ),
        name="whole",
    )(*args)


def hand_out(block_in, grad_in, sums, block_out, grad_out, kernel_out, *rest):
    block_out[...] = block_in[...]
    grad_out[...] = grad_in[...]
    kernel_out[...] = sums[0:49, :]
    for k, out in enumerate(rest):
        out[...] = sums[49 + k : 50 + k, :]


def per_device(
    features,
    cotangent,
    in_weight,
    out_weight,
    hidden_bias,
    kernel,
    conv_bias,
    norm_gain,
    norm_bias,
    layer_scale,
    out_bias,
):
    _, _, rows, cols, width = features.shape
    field = features.reshape(rows, cols, width)
    cot = cotangent.reshape(rows * cols, width)
    pixels = rows * cols
    vectors = [v.reshape(1, -1) for v in (conv_bias, norm_gain, norm_bias, layer_scale, out_bias)]
    made = whole(field, cot, in_weight, out_weight, hidden_bias.reshape(1, -1), kernel, *vectors)
    block_out, grad_in, out_kernel, *rest = pl.pallas_call(
        hand_out,
        out_shape=[jax.ShapeDtypeStruct((pixels, width), BF16)] * 2
        + [jax.ShapeDtypeStruct((49, 64), F32)]
        + [jax.ShapeDtypeStruct((1, 64), F32)] * 4,
        in_specs=[VMEM] * 3,
        out_specs=[VMEM] * 7,
        name="hand_out",
    )(*made)
    return (block_out.reshape(features.shape), grad_in.reshape(features.shape), out_kernel, *[v.reshape(-1) for v in rest])


def solution(mesh):
    placed = (
        P("dp", "tile", None, None, None),
        P("dp", "tile", None, None, None),
        P(("dp", "tile"), None),
        P(("dp", "tile"), None),
        P(("dp", "tile")),
        P(None, "dp"),
        P("dp"),
        P("dp"),
        P("dp"),
        P("dp"),
        P("dp"),
    )
    return jax.shard_map(
        per_device,
        mesh=mesh,
        in_specs=placed,
        out_specs=(
            P("dp", "tile", None, None, None),
            P("dp", "tile", None, None, None),
            P(None, "dp"),
            P("dp"),
            P("dp"),
            P("dp"),
            P("dp"),
        ),
        check_vma=False,
    )
```

```python
import functools
import heapq

import jax
import jax.numpy as jnp
from jax import lax
from jax.experimental import pallas as pl
from jax.experimental.pallas import tpu as pltpu
from jax.sharding import PartitionSpec as P

KS = 7
GX = 4
NX, NY, NZ = 4, 8, 8
MESH = pl.DeviceIdType.MESH
VMEM = pl.BlockSpec(memory_space=pltpu.VMEM)
F32 = jnp.float32
BF16 = jnp.bfloat16
DMA = pltpu.SemaphoreType.DMA


def place():
    dp = lax.axis_index("dp")
    tile = lax.axis_index("tile")
    x = lax.rem(dp, 4)
    y = lax.div(tile, 16) * 4 + lax.div(dp, 4)
    z = lax.rem(lax.div(tile, 2), 8)
    core = lax.rem(tile, 2)
    return x, y, z, core


def device(x, y, z, core):
    return (lax.rem(y, 4) * 4 + x, lax.div(y, 4) * 16 + z * 2 + core)


def turned(index, by, size):
    return lax.rem(index + (by % size), size)


def greet(barrier, peer):
    pl.semaphore_signal(barrier, inc=1, device_id=peer, device_id_type=MESH)


def remote(src, dst, ssem, rsem, peer):
    return pltpu.make_async_remote_copy(
        src_ref=src, dst_ref=dst, send_sem=ssem, recv_sem=rsem, device_id=peer, device_id_type=MESH
    )


STEPS = [(-1, 0), (1, 0), (0, -1), (0, 1), (-1, -1), (-1, 1), (1, -1), (1, 1)]


def halo_sides():
    dp = lax.axis_index("dp")
    tile = lax.axis_index("tile")
    ty = lax.div(tile, GX)
    tx = lax.rem(tile, GX)
    sides = []
    for dr, dc in STEPS:
        there = None
        for ok in ([ty >= 1] if dr < 0 else [ty <= 6] if dr > 0 else []) + (
            [tx >= 1] if dc < 0 else [tx <= 2] if dc > 0 else []
        ):
            there = ok if there is None else there & ok
        sides.append((there, (dp, tile + dr * GX + dc)))
    return sides


OFF4 = [0, -1, 1, 2]
OFF8 = [0, -1, 1, -2, 2, -3, 3, 4]


def ring_slots(n, count):
    half = n // 2
    right = [(s, j) for s in range(1, half) for j in range(count)] + [(half, j) for j in range(count // 2)]
    left = [(s, j) for s in range(1, half) for j in range(count)] + [(half, j) for j in range(count // 2, count)]
    return right, left


class Ring:
    def __init__(self, axis, n, count, offs, sub, peers, ssem, rsem, wire):
        self.axis, self.n, self.count, self.offs, self.sub, self.peers = axis, n, count, offs, sub, peers
        self.ssem, self.rsem, self.wire = ssem, rsem, wire
        self.slots = ring_slots(n, count)

    def copy(self, way, s, j):
        i = self.slots[way].index((s, j))
        ref = self.sub(-(s - 1) if way == 0 else (s - 1), j)
        return remote(ref, ref, self.ssem, self.rsem.at[way, i], self.peers[way])

    def landed(self, way, s, j):
        i = self.slots[way].index((s, j))
        ref = self.sub(-s if way == 0 else s, j)
        return pltpu.make_async_copy(ref, ref, self.rsem.at[way, i])

    def completes(self, way, s, seen):
        half = self.n // 2
        parts = [(w, s, j) for w in (0, 1) for j in range(self.count) if (s, j) in self.slots[w] and (s == half or w == way)]
        if not all(part in seen for part in parts):
            return None
        return self.offs.index(half if s == half else -s if way == 0 else s)


LEAD = 1.5


def plan(outer, inner, begin):
    rings = (inner, outer)
    free = {(axis, way): late for axis, late in zip("xyz", (0.0, 1.0, 2.0)) for way in (0, 1)}
    queues = {link: [] for link in free}
    heap, steps, seen = [], [], {}
    count = 0

    def push(at, kind, what):
        nonlocal count
        count += 1
        heapq.heappush(heap, (at, count, kind, what))

    def dispatch(at, link):
        if queues[link] and free[link] <= at:
            _, _, ready, given, (k, level, way, s, j) = heapq.heappop(queues[link])
            free[link] = at + rings[level][k].wire
            push(free[link], "free", link)
            push(free[link] + 1.7, "landed", (k, level, way, s, j))
            if not given:
                steps.append((max(ready, at - LEAD), 1, (k, level, way, s, j)))

    for link, late in free.items():
        push(late, "free", link)
    for k in range(3):
        for way in (0, 1):
            for j in range(2):
                push(begin[k], "given", (k, 0, way, 1, j))
        for way in (0, 1):
            push(begin[k], "given", (k, 1, way, 1, 0))
    while heap:
        at, number, kind, what = heapq.heappop(heap)
        if kind == "free":
            dispatch(at, what)
            continue
        k, level, way, s, j = what
        ring = rings[level][k]
        if kind in ("ready", "given"):
            link = (ring.axis, way)
            heapq.heappush(queues[link], (0 if kind == "given" else level, number, at, kind == "given", what))
            dispatch(at, link)
            continue
        steps.append((at, 0, what))
        if (s + 1, j) in ring.slots[way]:
            push(at, "ready", (k, level, way, s + 1, j))
        if level == 0:
            seen.setdefault(k, set()).add((way, s, j))
            index = ring.completes(way, s, seen[k])
            for w in (0, 1):
                if index is not None and (1, index) in outer[k].slots[w]:
                    push(at, "ready", (k, 1, w, 1, index))
    return sorted(steps)


def halo_count():
    count = 0
    for there, _ in halo_sides():
        count = count + there.astype(jnp.int32)
    return count


BACK = [1, 0, 3, 2, 7, 6, 5, 4]


class Halo:
    def __init__(self, grid, ecol, ecor, rows, cols, cors, ssem, rsem):
        self.grid, self.ecol, self.ecor = grid, ecol, ecor
        self.rows, self.cols, self.cors = rows, cols, cors
        src = [grid.at[:, 0:3], grid.at[:, 5:8], ecol.at[0], ecol.at[1]] + [ecor.at[k] for k in range(4)]
        self.dst = [rows.at[1], rows.at[0], cols.at[1], cols.at[0], cors.at[3], cors.at[2], cors.at[1], cors.at[0]]
        self.rsem = rsem
        self.moves = []
        for k, (there, peer) in enumerate(halo_sides()):
            self.moves.append((there, remote(src[k], self.dst[k], ssem.at[k], rsem.at[BACK[k]], peer)))

    def start(self):
        for there, copy in self.moves:
            @pl.when(there)
            def _():
                copy.start()

    def finish(self):
        for k, (there, copy) in enumerate(self.moves):
            landed = self.dst[BACK[k]]
            @pl.when(there)
            def _():
                pltpu.make_async_copy(landed, landed, self.rsem.at[k]).wait()
                copy.wait_send()

            @pl.when(jnp.logical_not(there))
            def _():
                landed[...] = jnp.zeros(landed.shape, landed.dtype)

    def cut(self, cb, value, stage):
        for i in range(8):
            stage[3 * i : 3 * i + 3, :] = value[i, 0:3, :]
            stage[24 + 3 * i : 27 + 3 * i, :] = value[i, 13:16, :]
        for k, (r, c) in enumerate(((0, 0), (0, 13), (5, 0), (5, 13))):
            for i in range(3):
                at = 48 + 16 * k + 3 * i
                stage[at : at + 3, :] = value[r + i, c : c + 3, :]
        self.ecol[0, cb] = stage[0:24, :].astype(BF16)
        self.ecol[1, cb] = stage[24:48, :].astype(BF16)
        for k in range(4):
            self.ecor[k, cb] = stage[48 + 16 * k : 64 + 16 * k, :].astype(BF16)

    def fill(self, cb, pad):
        pad[cb, 3:11, 8:24, :] = self.grid[cb].astype(F32)
        pad[cb, 0:3, 8:24, :] = self.rows[0, cb].astype(F32)
        pad[cb, 11:14, 8:24, :] = self.rows[1, cb].astype(F32)
        for side, col in ((0, 5), (1, 24)):
            value = self.cols[side, cb].astype(F32)
            for i in range(8):
                pad[cb, 3 + i, col : col + 3, :] = value[3 * i : 3 * i + 3, :]
        for k, (row, col) in enumerate(((0, 5), (0, 24), (11, 5), (11, 24))):
            value = self.cors[k, cb].astype(F32)
            for i in range(3):
                pad[cb, row + i, col : col + 3, :] = value[3 * i : 3 * i + 3, :]


def each(count, body):
    def step(i, carry):
        body(i)
        return carry

    lax.fori_loop(0, count, step, 0)


def block_conv(start, pad, taps, cb, flip):
    total = start
    for b in range(KS):
        window = pad[cb, :, 5 + b : 21 + b, :]
        for a in range(KS):
            tap = (6 - a) * KS + (6 - b) if flip else a * KS + b
            total = total + taps[cb, tap : tap + 1, :][None] * window[a : a + 8]
    return total


LAST = 5
CHUNKS = [
    [(0, 0), (2, 0), (1, 0)],
    [(0, -1), (0, 1), (2, -1), (2, 1)],
    [(1, -1), (1, 1)],
    [(0, -2), (0, 2), (2, -2), (2, 2)],
    [(0, -3), (0, 3), (2, -3), (2, 3)],
    [(0, 4), (2, 4), (1, 2)],
]


def whole_body(
    field, cot, w_in, w_out, hbias, taps_in, v0, v1, v2, v3, v4,
    block_out, grad_in, out_sums,
    fb, cb_, raw, rawz, rawy, slab, par, bia, ecol, ecor, stage, hrows, hcols, hcors, wrows, wcols, wcors, pad, bpad, pars, taps, row, zbias, bias, table,
    rz, ry, g0, g1, g2, act, hid, acc, part, mypart, conv, inv, bc, wire, ob, sums,
    sent, r1, r2, r3, mid, low, fin, tot,
    ls, hs, hr, h2r, ps, zs, bs, as_, ar, fs, q0r, q1r, q2r, r0r, r1r, r2r, rs, es, er, ts, os_,
):
    x, y, z, core = place()
    dp = lax.axis_index("dp")
    tile = lax.axis_index("tile")
    yl, yh = lax.rem(y, 4), lax.div(y, 4)
    xl, xh = lax.rem(x, 2), lax.div(x, 2)
    lane = lax.broadcasted_iota(jnp.int32, (1, 128), 1)
    barrier = pltpu.get_barrier_semaphore()
    sibling = device(x, y, z, 1 - core)
    xps = [device(turned(x, k, NX), y, z, core) for k in range(1, NX)]
    yps = [device(x, turned(y, k, NY), z, core) for k in range(1, NY)]
    zps = [device(x, y, turned(z, k, NZ), core) for k in range(1, NZ)]
    dps = [(turned(dp, k, 16), tile) for k in range(1, 16)]
    xys = [device(turned(x, k % 4, NX), turned(y, k // 4, NY), z, core) for k in range(1, 32)]
    mine = yl * 2 + xh
    member = yh * 4 + xl * 2 + core
    thirds = []
    for k in range(1, 8):
        o = turned(member, k, 8)
        thirds.append(device(xh * 2 + lax.rem(lax.div(o, 2), 2), lax.div(o, 4) * 4 + yl, z, lax.rem(o, 2)))
    for peer in xys + zps + thirds[0::2]:
        greet(barrier, peer)
    for there, peer in halo_sides():
        @pl.when(there)
        def _():
            greet(barrier, peer)

    for cb in range(8):
        lanes = pl.ds(128 * cb, 128)
        pltpu.make_async_copy(field.at[:, :, lanes], fb.at[cb], ls.at[0]).start()
        pltpu.make_async_copy(cot.at[:, lanes], cb_.at[cb], ls.at[1]).start()

    def settle(ref, sem):
        pltpu.make_async_copy(ref, ref, sem).wait()

    rows_in, rows_out = w_in[...].astype(F32), w_out[...].astype(F32)
    raw[0, 0:2, :], raw[0, 2:4, :] = rows_in[0:2], rows_out[0:2]
    raw[0, 4:8, :] = jnp.zeros((4, 1024), F32)
    raw[1, 0:4, :], raw[1, 4:8, :] = rows_in[2:6], rows_out[2:6]
    rawz[...] = raw[0].astype(BF16)
    rawy[...] = raw[1].astype(BF16)
    bia[...] = jnp.zeros((1, 128), F32)
    bia[:, 0:6] = hbias[...].astype(F32)
    slab[...] = jnp.zeros_like(slab)
    slab[0:49, 0:64] = taps_in[...]
    for k, v in enumerate((v0, v1, v2, v3, v4)):
        slab[49 + k : 50 + k, 0:64] = v[...]
    par[...] = jnp.where(lane < 64, slab[0:28, :], pltpu.roll(slab[28:56, :], 64, 1))
    stage[...] = jnp.zeros_like(stage)
    halo1 = Halo(fb, ecol, ecor, hrows, hcols, hcors, hs, hr)
    pl.semaphore_wait(barrier, 31 + 7 + 4 + halo_count())

    for peer in zps:
        remote(rawz, rz.at[z], fs.at[0], fs.at[1], peer).start()
    for peer in yps:
        remote(rawy, ry.at[y], fs.at[2], fs.at[3], peer).start()
    for peer in zps:
        remote(bia, zbias.at[z], zs.at[0], zs.at[1], peer).start()
    settle(fb, ls.at[0])
    settle(cb_, ls.at[1])
    each(8, lambda cb: halo1.cut(cb, fb[cb].astype(F32), stage))
    rz[z] = rawz[...]
    ry[y] = rawy[...]
    zbias[z] = bia[...]
    pars[dp] = par[...]

    to = lax.broadcasted_iota(jnp.int32, (32, 64), 0)
    fro = lax.broadcasted_iota(jnp.int32, (32, 64), 1)

    def tiles(got, first_row, step):
        chosen = fro == ((to >> 1) & 7) * 8 + (to >> 4) * step + first_row + (to & 1)
        rows = jnp.concatenate([got[d].astype(F32) for d in range(8)], axis=0).astype(BF16)
        made = jnp.dot(jnp.where(chosen, 1.0, 0.0).astype(BF16), rows, preferred_element_type=F32)
        return made.astype(BF16)

    def put(home, made):
        for cb in range(8):
            for m in range(2):
                home[cb, m] = made[16 * m : 16 * m + 16, 128 * cb : 128 * cb + 128]

    xr, xb = xps[0], xps[-1]
    yr, yb = yps[0], yps[-1]
    zr_, zb = zps[0], zps[-1]
    inner = [
        Ring("x", 4, 2, OFF4, lambda b, j: g0.at[y, turned(x, b, 4), pl.ds(4 * j, 4)], (xr, xb), rs.at[0], q0r, 0.7),
        Ring("z", 8, 2, OFF8, lambda b, j: g1.at[x, turned(z, b, 8), pl.ds(4 * j, 4)], (zr_, zb), rs.at[1], q1r, 0.7),
        Ring("x", 4, 2, OFF4, lambda b, j: g2.at[z, turned(x, b, 4), pl.ds(4 * j, 4)], (xr, xb), rs.at[2], q2r, 0.7),
    ]
    outer = [
        Ring("y", 8, 4, OFF4, lambda b, j: g0.at[turned(y, b, 8), turned(x, OFF4[j], 4)], (yr, yb), rs.at[3], r0r, 1.4),
        Ring("x", 4, 8, OFF8, lambda b, j: g1.at[turned(x, b, 4), turned(z, OFF8[j], 8)], (xr, xb), rs.at[4], r1r, 1.4),
        Ring("z", 8, 4, OFF4, lambda b, j: g2.at[turned(z, b, 8), turned(x, OFF4[j], 4)], (zr_, zb), rs.at[5], r2r, 1.4),
    ]
    def go(copy):
        copy.start()

    def perform(kind, what):
        k, level, way, s, j = what
        ring = (inner, outer)[level][k]
        if kind == 0:
            ring.landed(way, s, j).wait()
        else:
            go(ring.copy(way, s, j))

    ship = [remote(act.at[a, core], act.at[a, core], as_.at[a], ar.at[a], sibling) for a in range(2)]

    def bias_push():
        settle(zbias.at[0:7], zs.at[0])
        settle(zbias.at[0:7], zs.at[1])
        total = zbias[0]
        for k in range(1, NZ):
            total = total + pltpu.roll(zbias[k], 6 * k, 1)
        row[...] = total
        me = x * 8 + y
        bias[me] = total
        for peer in xys:
            remote(row, bias.at[me], bs.at[0], bs.at[1], peer).start()

    def params():
        settle(pars.at[0:15], ps.at[0])
        settle(pars.at[0:15], ps.at[1])

        def unpack(cb):
            one, two = pars[2 * cb], pars[2 * cb + 1]
            taps[cb, 0:28, :] = jnp.where(lane < 64, one, pltpu.roll(two, 64, 1))
            taps[cb, 28:56, :] = jnp.where(lane < 64, pltpu.roll(one, 64, 1), two)

        each(8, unpack)
        for cb in range(8):
            scaled = cb_[cb].astype(F32) * taps[cb, 52:53, :]
            act[1, core, :, 128 * cb : 128 * cb + 128] = scaled.astype(BF16)

    def borders():
        ship[1].start()
        halo1.finish()
        each(8, lambda cb: halo1.fill(cb, pad))

    def conv_piece(part_number):
        def one(i):
            cb = i + 2 * part_number
            start = jnp.broadcast_to(taps[cb, 49:50, :][None], (8, 16, 128))
            conv[cb] = block_conv(start, pad, taps, cb, False).reshape(128, 128)

        each(2, one)

    def norm():
        mean = jnp.sum(sum(conv[cb] for cb in range(8)), axis=-1, keepdims=True) * (1.0 / 1024)
        square = jnp.zeros((128, 128), F32)
        for cb in range(8):
            centered = conv[cb] - mean
            square = square + centered * centered
        inverse = lax.rsqrt(jnp.sum(square, axis=-1, keepdims=True) * (1.0 / 1024) + 1e-06)
        inv[...] = jnp.broadcast_to(inverse, (128, 128))
        for cb in range(8):
            standard = (conv[cb] - mean) * inverse
            conv[cb] = standard
            normed = standard * taps[cb, 50:51, :] + taps[cb, 51:52, :]
            act[0, core, :, 128 * cb : 128 * cb + 128] = normed.astype(BF16)

    def biases():
        ship[0].start()
        settle(bias.at[0:31], bs.at[0])
        settle(bias.at[0:31], bs.at[1])
        values = bias[...].reshape(32, 128).astype(BF16)
        j = lax.broadcasted_iota(jnp.int32, (128, 128), 0)
        l = lax.broadcasted_iota(jnp.int32, (128, 128), 1)
        bx = lax.broadcasted_iota(jnp.int32, (4, 8, 128), 0)
        by = lax.broadcasted_iota(jnp.int32, (4, 8, 128), 1)
        bl = lax.broadcasted_iota(jnp.int32, (4, 8, 128), 2)
        l64 = bl & 63

        def pick(where):
            chosen = jnp.where(where, 1.0, 0.0).astype(BF16)
            return jnp.dot(values, chosen, preferred_element_type=F32).reshape(4, 8, 128)

        t0 = pick(j == 6 * ((l >> 1) & 7) + (l & 1))
        table[0] = jnp.sum(jnp.where(bx == (l64 >> 4), t0, 0.0), axis=0)
        t1_ = pick(j == 6 * (l >> 4) + 2 + (l & 1))
        table[1, 0:4, :] = jnp.sum(jnp.where(by == ((bl >> 1) & 7), t1_, 0.0), axis=1)
        for zz in range(8):
            t2_ = pick(j == 6 * zz + 4 + (l & 1))
            kept = jnp.where((bx == (l64 >> 4)) & (by == ((bl >> 1) & 7)), t2_, 0.0)
            table[2, zz : zz + 1, :] = jnp.sum(jnp.sum(kept, axis=0), axis=0, keepdims=True)
        for copy in ship:
            copy.wait()

    at = (lambda off: turned(y, off, 8), lambda off: turned(x, off, 4), lambda off: turned(z, off, 8))
    nt = (((1,), (1,)), ((), ()))

    def weights(blocks, m):
        columns = []
        for cb in range(8):
            pieces = []
            for k, off in blocks:
                if k == 0:
                    pieces.append(g0[at[0](off), :, cb, m].reshape(64, 128))
                elif k == 1:
                    pieces.append(g1[at[1](off), :, cb, m].reshape(128, 128))
                else:
                    pieces.append(g2[at[2](off), :, cb, m].reshape(64, 128))
            columns.append(jnp.concatenate(pieces, axis=0))
        return jnp.concatenate(columns, axis=1)

    def bias_row(blocks):
        out, pend = [], None
        for k, off in blocks:
            value = table[k, pl.ds(at[k](off), 1), :]
            if k == 1:
                out.append(value)
            elif pend is None:
                pend = value
            else:
                out.append(jnp.where(lane < 64, pend, value))
                pend = None
        return jnp.concatenate(out, axis=1)

    def front(blocks, a_in, a_out):
        pre = lax.dot_general(a_in, weights(blocks, 0), nt, preferred_element_type=F32) + bias_row(blocks)
        back = lax.dot_general(a_out, weights(blocks, 1), nt, preferred_element_type=F32)
        cdf = 0.5 * (1.0 + lax.erf(pre * 0.7071067811865476))
        slope = cdf + pre * jnp.exp(-0.5 * pre * pre) * 0.3989422804014327
        return (pre * cdf).astype(BF16), (back * slope).astype(BF16)

    def chunk_front(n):
        hidden, back_pre = front(CHUNKS[n], act[0].reshape(256, 1024), act[1].reshape(256, 1024))
        hid[0], hid[1] = hidden, back_pre

    def chunk_back(n):
        for m in range(2):
            value = jnp.dot(hid[m], weights(CHUNKS[n], 1 - m), preferred_element_type=F32).reshape(2, 128, 1024)
            for cb in range(8):
                piece = value[:, :, 128 * cb : 128 * cb + 128]
                acc[m, :, cb] = piece if n == 0 else acc[m, :, cb] + piece

    tasks = [(0.3, 0.5, None, bias_push), (0.6, 5.0, None, params), (1.2, 9.0, None, borders)]
    tasks += [(0.6, 0.0, None, functools.partial(conv_piece, i)) for i in range(4)]
    tasks += [(0.8, 0.0, None, norm), (0.6, 0.0, None, biases)]
    for n in range(LAST):
        tasks.append((1.0, 0.0, CHUNKS[n], functools.partial(chunk_front, n)))
        tasks.append((0.8, 0.0, CHUNKS[n], functools.partial(chunk_back, n)))
    home = (g0.at[y, x], g1.at[x, z], g2.at[z, x])
    for k, (got, first_row, step) in enumerate(((rz, 0, 2), (ry, 0, 4), (ry, 2, 4))):
        if k != 2:
            settle(got.at[0:7], fs.at[2 * k])
            settle(got.at[0:7], fs.at[2 * k + 1])
        put(home[k], tiles(got, first_row, step))
        for way in (0, 1):
            for j in range(2):
                go(inner[k].copy(way, 1, j))
        for way in (0, 1):
            go(outer[k].copy(way, 1, 0))
    halo1.start()
    for peer in dps:
        remote(par, pars.at[dp], ps.at[0], ps.at[1], peer).start()
    events = plan(outer, inner, (0.0, 0.3, 0.3))

    def needs(event, blocks):
        _, kind, (k, level, way, s, j) = event
        if blocks is None or kind:
            return False
        for kk, off in blocks:
            if kk != k:
                continue
            if off == 0 and level == 0:
                return True
            if off != 0 and level == 1 and (abs(off) == s) and (s == outer[k].n // 2 or (off < 0) == (way == 0)):
                return True
        return False

    clock = 0.0
    while events or tasks:
        ready = bool(tasks) and not any(needs(e, tasks[0][2]) for e in events)
        if events and (events[0][0] <= clock or not ready or clock < tasks[0][1]):
            event = events.pop(0)
            clock = max(clock, event[0])
            perform(*event[1:])
        else:
            length, _, _, piece = tasks.pop(0)
            piece()
            clock += length

    blocks = CHUNKS[LAST]
    swap = [remote(mypart.at[a], part.at[a], es.at[a], er.at[a], sibling) for a in range(2)]
    for turn, who in enumerate((1 - core, core)):
        for m, h in enumerate(front(blocks, act[0, who], act[1, who])):
            hid[m, 0:128, :] = h
        for m in range(2):
            value = jnp.dot(hid[m, 0:128, :], weights(blocks, 1 - m), preferred_element_type=F32)
            for cb in range(8):
                piece = acc[m, who, cb] + value[:, 128 * cb : 128 * cb + 128]
                if turn == 0:
                    mypart[m, cb] = piece.astype(BF16)
                else:
                    acc[m, core, cb] = piece
            if turn == 0:
                swap[m].start()
    for copy in swap:
        copy.wait_recv()

    sums[:, 48:64, :] = jnp.zeros((8, 16, 128), F32)

    def down(value):
        return jnp.sum(value, axis=0, keepdims=True)

    def ending(cb, carry):
        one, two = carry
        standard = conv[cb]
        upstream = cb_[cb].astype(F32)
        projected = acc[0, core, cb] + part[0, cb].astype(F32) + taps[cb, 53:54, :]
        normed = acc[1, core, cb] + part[1, cb].astype(F32)
        source = fb[cb].astype(F32).reshape(128, 128)
        ob[0, cb] = (source + taps[cb, 52:53, :] * projected).astype(BF16)
        sums[cb, 50:51, :] = down(normed * standard)
        sums[cb, 51:52, :] = down(normed)
        sums[cb, 52:53, :] = down(upstream * projected)
        scaled = normed * taps[cb, 50:51, :]
        bc[cb] = scaled
        return one + scaled, two + scaled * standard

    none = jnp.zeros((128, 128), F32)
    one, two = lax.fori_loop(0, 8, ending, (none, none))
    mean_one = jnp.sum(one, axis=-1, keepdims=True) * (1.0 / 1024)
    mean_two = jnp.sum(two, axis=-1, keepdims=True) * (1.0 / 1024)
    halo2 = Halo(wire, ecol, ecor, wrows, wcols, wcors, hs, h2r)
    inverse = inv[...]

    def rear(cb):
        back = inverse * (bc[cb] - mean_one - conv[cb] * mean_two)
        bc[cb] = back
        sums[cb, 49:50, :] = down(back)
        wire[cb] = back.reshape(8, 16, 128).astype(BF16)

    def block_grad(cb):
        back = bc[cb].reshape(8, 16, 128)
        for b in range(KS):
            window = pad[cb, :, 5 + b : 21 + b, :]
            for a in range(KS):
                product = jnp.sum(back * window[a : a + 8], axis=0)
                sums[cb, a * KS + b : a * KS + b + 1, :] = down(product)

    def firsts(k):
        other = lax.rem(mine + k, 8)
        peer = device(lax.rem(other, 2) * 2 + xl, yh * 4 + lax.div(other, 2), z, core)
        return other, remote(sent.at[other], r1.at[mine], ts.at[0], ts.at[1], peer)

    def grad_step(i):
        other, copy = firsts(i + 1)
        rear(other)
        block_grad(other)
        sent[other] = sums[other].astype(BF16)
        copy.start()

    each(7, grad_step)
    rear(mine)
    block_grad(mine)
    r1[mine] = sums[mine].astype(BF16)
    each(8, lambda cb: halo2.cut(cb, bc[cb].reshape(8, 16, 128), stage))
    def conv_back(low_, count):
        def one(i):
            cb = i + low_
            halo2.fill(cb, bpad)
            start = cb_[cb].astype(F32).reshape(8, 16, 128)
            ob[1, cb] = block_conv(start, bpad, taps, cb, True).reshape(128, 128).astype(BF16)

        each(count, one)
        for cb in range(low_, low_ + count):
            pltpu.make_async_copy(ob.at[1, cb], grad_in.at[:, pl.ds(128 * cb, 128)], os_.at[1]).start()

    settle(r1.at[0:7], ts.at[1])
    mid[...] = jnp.sum(r1[...].astype(F32), axis=0).reshape(8, 8, 128)
    for k in range(7):
        remote(mid.at[turned(z, k + 1, 8)], r2.at[z], ts.at[2], ts.at[3], zps[k]).start()
    r2[z] = mid[z]
    halo2.start()
    for cb in range(8):
        pltpu.make_async_copy(ob.at[0, cb], block_out.at[:, pl.ds(128 * cb, 128)], os_.at[0]).start()
    settle(r2.at[0:7], ts.at[3])
    low[...] = jnp.sum(r2[...], axis=0)
    for k in range(7):
        remote(low, r3.at[member], ts.at[4], ts.at[5], thirds[k]).start()
    r3[member] = low[...]
    settle(r3.at[0:7], ts.at[5])
    fin[...] = jnp.sum(r3[...], axis=0)
    for k in range(7):
        remote(fin, tot.at[z], ts.at[6], ts.at[7], zps[k]).start()
    tot[z] = fin[...]
    halo2.finish()
    conv_back(0, 8)
    settle(r1.at[0:7], ts.at[0])
    for k, ref in enumerate((g0.at[0, 0:3], g1.at[0, 0:7], g2.at[0, 0:3], g0.at[0:7], g1.at[0:3], g2.at[0:7])):
        settle(ref, rs.at[k])
    for copy in swap:
        copy.wait_send()
    settle(r2.at[0:7], ts.at[2])
    settle(r3.at[0:7], ts.at[4])
    settle(ob.at[0], os_.at[0])
    settle(ob.at[1], os_.at[1])
    settle(tot.at[0:7], ts.at[6])
    settle(tot.at[0:7], ts.at[7])
    final = tot[...].reshape(64, 128) * (1.0 / 256.0)
    final = jnp.where(xl == 0, final, pltpu.roll(final, 64, 1))
    out_sums[...] = final[0:56, 0:64]


def whole(*args):
    cell = (2, 16, 128)
    any_ = pl.BlockSpec(memory_space=pl.ANY)
    scratch = [
        ((8, 8, 16, 128), BF16), ((8, 128, 128), BF16), ((2, 8, 1024), F32), ((8, 1024), BF16), ((8, 1024), BF16),
        ((56, 128), F32), ((28, 128), F32), ((1, 128), F32), ((2, 8, 24, 128), BF16), ((4, 8, 16, 128), BF16), ((112, 128), F32),
        ((2, 8, 3, 16, 128), BF16), ((2, 8, 24, 128), BF16), ((4, 8, 16, 128), BF16),
        ((2, 8, 3, 16, 128), BF16), ((2, 8, 24, 128), BF16), ((4, 8, 16, 128), BF16),
        ((8, 14, 32, 128), F32), ((8, 14, 32, 128), F32), ((16, 28, 128), F32), ((8, 56, 128), F32),
        ((1, 128), F32), ((8, 1, 128), F32), ((32, 1, 128), F32), ((3, 8, 128), F32),
        ((8, 8, 1024), BF16), ((8, 8, 1024), BF16),
        ((8, 4, 8) + cell, BF16), ((4, 8, 8) + cell, BF16), ((8, 4, 8) + cell, BF16),
        ((2, 2, 128, 1024), BF16), ((2, 256, 256), BF16), ((2, 2, 8, 128, 128), F32),
        ((2, 8, 128, 128), BF16), ((2, 8, 128, 128), BF16), ((8, 128, 128), F32), ((128, 128), F32),
        ((8, 128, 128), F32), ((8, 8, 16, 128), BF16), ((2, 8, 128, 128), BF16), ((8, 64, 128), F32),
        ((8, 64, 128), BF16), ((8, 64, 128), BF16), ((8, 8, 128), F32), ((8, 8, 128), F32), ((8, 8, 128), F32), ((8, 128), F32), ((8, 128), F32),
        ((8, 8, 128), F32),
    ]
    sems = [(2,), (8,), (8,), (8,), (2,), (2,), (2,), (2,), (2,), (4,), (2, 3), (2, 7), (2, 3), (2, 14), (2, 12), (2, 14)]
    sems += [(6,), (2,), (2,), (8,), (2,)]
    return pl.pallas_call(
        whole_body,
        out_shape=(
            jax.ShapeDtypeStruct((128, 1024), BF16),
            jax.ShapeDtypeStruct((128, 1024), BF16),
            jax.ShapeDtypeStruct((56, 64), F32),
        ),
        in_specs=[any_, any_] + [VMEM] * 9,
        out_specs=[any_, any_, VMEM],
        scratch_shapes=[pltpu.VMEM(*s) for s in scratch] + [DMA(s) for s in sems],
        compiler_params=pltpu.CompilerParams(
            collective_id=0, has_side_effects=True, vmem_limit_bytes=56 * 1024 * 1024
        ),
        name="whole",
    )(*args)


def hand_out(block_in, grad_in, sums, block_out, grad_out, kernel_out, *rest):
    block_out[...] = block_in[...]
    grad_out[...] = grad_in[...]
    kernel_out[...] = sums[0:49, :]
    for k, out in enumerate(rest):
        out[...] = sums[49 + k : 50 + k, :]


def per_device(
    features,
    cotangent,
    in_weight,
    out_weight,
    hidden_bias,
    kernel,
    conv_bias,
    norm_gain,
    norm_bias,
    layer_scale,
    out_bias,
):
    _, _, rows, cols, width = features.shape
    field = features.reshape(rows, cols, width)
    cot = cotangent.reshape(rows * cols, width)
    pixels = rows * cols
    vectors = [v.reshape(1, -1) for v in (conv_bias, norm_gain, norm_bias, layer_scale, out_bias)]
    made = whole(field, cot, in_weight, out_weight, hidden_bias.reshape(1, -1), kernel, *vectors)
    block_out, grad_in, out_kernel, *rest = pl.pallas_call(
        hand_out,
        out_shape=[jax.ShapeDtypeStruct((pixels, width), BF16)] * 2
        + [jax.ShapeDtypeStruct((49, 64), F32)]
        + [jax.ShapeDtypeStruct((1, 64), F32)] * 4,
        in_specs=[VMEM] * 3,
        out_specs=[VMEM] * 7,
        name="hand_out",
    )(*made)
    return (block_out.reshape(features.shape), grad_in.reshape(features.shape), out_kernel, *[v.reshape(-1) for v in rest])


def solution(mesh):
    placed = (
        P("dp", "tile", None, None, None),
        P("dp", "tile", None, None, None),
        P(("dp", "tile"), None),
        P(("dp", "tile"), None),
        P(("dp", "tile")),
        P(None, "dp"),
        P("dp"),
        P("dp"),
        P("dp"),
        P("dp"),
        P("dp"),
    )
    return jax.shard_map(
        per_device,
        mesh=mesh,
        in_specs=placed,
        out_specs=(
            P("dp", "tile", None, None, None),
            P("dp", "tile", None, None, None),
            P(None, "dp"),
            P("dp"),
            P("dp"),
            P("dp"),
            P("dp"),
        ),
        check_vma=False,
    )
```
